32 devices in a mesh: query: 8 (over z, y), item: 4 (over x, core).
Axes of the slice: x: 2, y: 2, z: 4, core: 2. Of those that a mesh axis runs over, the one named last changes fastest.
Arguments:
- query_emb: bfloat16 [2048, 256], P(('query', 'item')), may hold values from -400 to 400
- targets: int32 [2048], P('query'), may hold values from 0 to 8191, as said below
- eligible_tiles: int32 [32, 32], P('query', 'item'), may hold values from 0 to 1, as said below
- item_feats: bfloat16 [4, 2048, 512], P('item', 'query'), may hold values from -6 to 6
- w_first: bfloat16 [512, 1024], replicated, may hold values from -0.25 to 0.25
- w_second: bfloat16 [1024, 256], replicated, may hold values from -0.1875 to 0.1875
Outputs:
- loss: float32 [2048], P(('query', 'item'))
- query_grad: float32 [2048, 256], P(('query', 'item'))
- w_first_grad: float32 [512, 1024], replicated
- w_second_grad: float32 [1024, 256], replicated
The draws below stay inside these ranges and needn't reach their ends.
Inputs may be any that keep to these rules, and one draw needn't show every extreme that they name: `eligible_tiles`: every row has at least one 1. The block targets[q] // 256 is marked 1 in row q // 64 of eligible_tiles.
All inputs are finite; a program needn't handle non-finite values.
Results may differ from the reference program's by a relative error of at most 0.007.
Values may be sent and summed in bfloat16 or wider, within the bound.
A program may use at most 64 MiB of HBM per device.

```python
import math
import jax
import jax.numpy as jnp
from jax import lax

DIN = 512
HID = 1024
E = 256
Q_DEV = 64
I_DEV = 256
NQ = 2048
ITEMS = 8192
QBLOCKS = 32
IBLOCKS = 32
TILE = 2048
N_ITEM = 4


def eligibility(key):
    key_row, key_col, key_roll, key_force = jax.random.split(jax.random.fold_in(key, 11), 4)
    row_pct = jax.random.randint(key_row, (QBLOCKS, 1), 8, 53)
    col_pct = jax.random.randint(key_col, (1, IBLOCKS), 50, 151)
    rolled = jax.random.randint(key_roll, (QBLOCKS, IBLOCKS), 0, 10000)
    live_set = rolled < row_pct * col_pct
    forced = jax.random.randint(key_force, (QBLOCKS,), 0, IBLOCKS)
    blocks = jnp.arange(IBLOCKS, dtype=jnp.int32)
    live_set = live_set | (blocks[None, :] == forced[:, None])
    return live_set.astype(jnp.int32)


def draw_eligible_tiles(key, part):
    return eligibility(key)


def draw_targets(key, part):
    tiles = eligibility(key)
    key_pick, key_row = jax.random.split(jax.random.fold_in(key, 23))
    per_query = jnp.repeat(tiles, Q_DEV, axis=0)
    blocks = jnp.arange(IBLOCKS, dtype=jnp.int32)
    ranked = jax.random.randint(key_pick, (NQ, IBLOCKS), 0, 1 << 20) * IBLOCKS + blocks[None, :]
    ranked = jnp.where(per_query > 0, ranked, -1)
    chosen = jnp.argmax(ranked, axis=1).astype(jnp.int32)
    offsets = jax.random.randint(key_row, (NQ,), 0, I_DEV)
    return chosen * I_DEV + offsets


def draw_query_emb(key, part):
    key_base = jax.random.fold_in(jax.random.fold_in(key, 37), 0)
    key_shared = jax.random.fold_in(jax.random.fold_in(key, 37), 3)
    values = jax.random.truncated_normal(key_base, -4.0, 4.0, (NQ, E), jnp.float32)
    shared = jax.random.truncated_normal(key_shared, -3.0, 3.0, (1, E), jnp.float32)
    values = values + shared
    return values.astype(jnp.bfloat16)


def block_scale(stream_key, extent, pieces, least, high):
    factor_of = 1.0
    for dim, blocks in pieces:
        draws = jax.random.uniform(jax.random.fold_in(jax.random.fold_in(stream_key, 6), dim), (blocks,), jnp.float32, least / len(pieces), high / len(pieces))
        factor_of = factor_of * jnp.repeat(jnp.exp(draws), extent[dim] // blocks).reshape((-1,) + (1,) * (len(extent) - 1 - dim))
    return factor_of


def normal_values(key, shape, spread, limit, pieces=(), kind=jnp.bfloat16):
    array = jax.random.normal(key, shape, jnp.float32) * spread
    if len(pieces) > 0:
        array = block_scale(key, shape, pieces, -0.22, 0.18) * array
    return jnp.clip(array, min=-limit, max=limit).astype(kind)


def setup_inputs(seed: int = 0) -> dict:
    splits = jax.random.split(jax.random.key(seed), 7)
    query_emb = draw_query_emb(jax.random.fold_in(splits[6], 71), 0)
    targets = draw_targets(jax.random.fold_in(splits[6], 71), 0)
    eligible_tiles = draw_eligible_tiles(jax.random.fold_in(splits[6], 71), 0)
    item_feats = normal_values(splits[3], (N_ITEM, TILE, DIN), 1.0, 6.0, ((0, 4), (1, 8)))
    w_first = normal_values(splits[4], (DIN, HID), DIN ** -0.5, 0.25)
    w_second = normal_values(splits[5], (HID, E), HID ** -0.5, 0.1875)
    return {"query_emb": query_emb, "targets": targets, "eligible_tiles": eligible_tiles, "item_feats": item_feats, "w_first": w_first, "w_second": w_second}


def reference(query_emb, targets, eligible_tiles, item_feats, w_first, w_second):
    tokens = item_feats.reshape(ITEMS, DIN)
    tok_wide = tokens.astype(jnp.float32)
    pre_act = jnp.dot(tok_wide, w_first.astype(jnp.float32), preferred_element_type=jnp.float32)
    hidden = lax.optimization_barrier(jax.nn.silu(pre_act).astype(jnp.bfloat16)).astype(jnp.float32)
    item_emb = jnp.dot(hidden, w_second.astype(jnp.float32), preferred_element_type=jnp.float32)
    emb_wide = lax.optimization_barrier(item_emb.astype(jnp.bfloat16)).astype(jnp.float32)
    columns = jnp.arange(ITEMS, dtype=jnp.int32)

    def one_block(emb_grad, block_idx):
        queries = lax.dynamic_slice_in_dim(query_emb, block_idx * Q_DEV, Q_DEV, 0).astype(jnp.float32)
        wanted = lax.dynamic_slice_in_dim(targets, block_idx * Q_DEV, Q_DEV, 0)
        live_cols = jnp.repeat(eligible_tiles[block_idx] > 0, I_DEV)[None, :]
        scores = 0.25 * jnp.dot(queries, emb_wide.T, preferred_element_type=jnp.float32)
        masked = jnp.where(live_cols, scores, -1e+30)
        run_max = lax.optimization_barrier(jnp.max(masked, axis=1))
        run_sum = lax.optimization_barrier(jnp.sum(jnp.where(live_cols, jnp.exp(masked - run_max[:, None]), 0.0), axis=1))
        log_norm = run_max + jnp.log(run_sum)
        is_target = columns[None, :] == wanted[:, None]
        positive = lax.optimization_barrier(jnp.sum(jnp.where(is_target, scores, 0.0), axis=1))
        softmax_w = jnp.where(live_cols, jnp.exp(masked - log_norm[:, None]), 0.0)
        coeffs = softmax_w - is_target.astype(jnp.float32)
        coeffs = lax.optimization_barrier(coeffs.astype(jnp.bfloat16)).astype(jnp.float32)
        q_grads = 0.25 * jnp.dot(coeffs, emb_wide, preferred_element_type=jnp.float32)
        emb_grad = emb_grad + 0.25 * jnp.dot(coeffs.T, queries, preferred_element_type=jnp.float32)
        return (emb_grad, (log_norm - positive, q_grads))
    start_grad = jnp.zeros((ITEMS, E), jnp.float32)
    emb_grad, outputs = lax.scan(one_block, start_grad, jnp.arange(QBLOCKS, dtype=jnp.int32))
    loss = outputs[0].reshape(NQ)
    query_grad = outputs[1].reshape(NQ, E)
    grad_b = lax.optimization_barrier(emb_grad.astype(jnp.bfloat16)).astype(jnp.float32)
    grad_scale = 1.0 / math.sqrt(ITEMS)
    w_second_grad = jnp.dot(hidden.T, grad_b, preferred_element_type=jnp.float32) * grad_scale
    hid_grad = jnp.dot(grad_b, w_second.astype(jnp.float32).T, preferred_element_type=jnp.float32)
    gate_sig = jax.nn.sigmoid(pre_act)
    pre_grad = hid_grad * gate_sig * (1.0 + pre_act * (1.0 - gate_sig))
    pre_grad = lax.optimization_barrier(pre_grad.astype(jnp.bfloat16)).astype(jnp.float32)
    w_first_grad = jnp.dot(tok_wide.T, pre_grad, preferred_element_type=jnp.float32) * grad_scale
    return (loss, query_grad, w_first_grad, w_second_grad)
```

```python
import functools
import math

import jax
import jax.numpy as jnp
from jax import lax
from jax.experimental import pallas as pl
from jax.experimental.pallas import tpu as pltpu
from jax.sharding import PartitionSpec as P

F32 = jnp.float32
BF16 = jnp.bfloat16


def dot(a, b, contract):
    return lax.dot_general(a, b, ((contract[:1], contract[1:]), ((), ())), preferred_element_type=F32)


def rows(start, size):
    return pl.ds(pl.multiple_of(start, math.gcd(size, 256)), size)


def window_kernel(
    shape,
    query_ref, targets_ref, flags_ref, tokens_hbm, w1_hbm, w2_hbm,
    loss_ref, qgrad_ref, a_out, b_out,
    tokens_ref, w1_ref, w2_ref, q_all, raw_in, meta_in, emb_all, flags_all, scores, coeffs, stats_all,
    e_acc, e_recv_c, e_recv_x, q_acc, q_recv_y, q_recv_l, q_recv_h,
    pre_act, hidden, a_acc, b_acc, core_recv, x_recv, y_recv, l_recv, h_recv,
    send_sems, recv_sems, load_sems,
):
    nq, ni, grad_scale = shape
    gx, gz = ni // 2, nq // 2
    q, i = lax.axis_index("query"), lax.axis_index("item")
    core, x = lax.rem(i, 2), lax.div(i, 2)
    y, z = lax.rem(q, 2), lax.div(q, 2)
    zl, zh = lax.rem(z, 2), lax.div(z, 2)
    gh = gz // 2
    q_rows, width = query_ref.shape
    n_q = nq * q_rows
    block = tokens_ref.shape[0]
    used = [0]
    loads = [
        pltpu.make_async_copy(src, dst, load_sems.at[n])
        for n, (src, dst) in enumerate(((tokens_hbm, tokens_ref), (w1_hbm, w1_ref), (w2_hbm, w2_ref)))
    ]
    for load in loads:
        load.start()

    def send(src, dst, peer):
        slot = used[0]
        used[0] += 1
        copy = pltpu.make_async_remote_copy(
            src_ref=src, dst_ref=dst, send_sem=send_sems.at[slot], recv_sem=recv_sems.at[slot],
            device_id=peer, device_id_type=pl.DeviceIdType.MESH,
        )
        copy.start()
        return copy

    def finish(copies):
        for copy in copies:
            copy.wait()

    axes = {
        "core": (2, core, lambda t: {"item": x * 2 + t}),
        "x": (gx, x, lambda t: {"item": t * 2 + core}),
        "y": (2, y, lambda t: {"query": z * 2 + t}),
        "z": (gz, z, lambda t: {"query": t * 2 + y}),
        "zl": (2, zl, lambda t: {"query": (zh * 2 + t) * 2 + y}),
        "zh": (gh, zh, lambda t: {"query": (t * 2 + zl) * 2 + y}),
    }

    def reduce_start(acc, recv, base, size, axis):
        group, own, peer = axes[axis]
        copies = []
        for k in range(1, group):
            there = lax.rem(own + k, group)
            copies.append(
                send(acc.at[rows(base + there * size, size)], recv.at[rows((k - 1) * size, size)], peer(there))
            )
        return copies

    def reduce_finish(copies, acc, recv, base, size, axis):
        group, own, _ = axes[axis]
        finish(copies)
        here = rows(base + own * size, size)
        total = acc[here, :]
        for k in range(1, group):
            total = total + recv[rows((k - 1) * size, size), :]
        acc[here, :] = total
        return base + own * size

    def gather_start(buf, base, size, axis):
        group, own, peer = axes[axis]
        here = buf.at[rows(base + own * size, size)]
        return [send(here, here, peer(lax.rem(own + k, group))) for k in range(1, group)]

    barrier = pltpu.get_barrier_semaphore()
    for k in range(1, nq):
        pl.semaphore_signal(
            barrier, inc=1, device_id={"query": lax.rem(q + k, nq)}, device_id_type=pl.DeviceIdType.MESH
        )
    for k in range(1, ni):
        pl.semaphore_signal(
            barrier, inc=1, device_id={"item": lax.rem(i + k, ni)}, device_id_type=pl.DeviceIdType.MESH
        )
    pl.semaphore_wait(barrier, nq + ni - 2)

    q_pos = (y * 2 + zl) * gh + zh
    query_copies = []
    for k in range(1, nq):
        there = lax.rem(q + k, nq)
        query_copies.append(send(query_ref, q_all.at[rows(q_pos * q_rows, q_rows)], {"query": there}))
    per = 128 // q_rows
    meta_rows = raw_in.shape[1]
    raw_in[i] = jnp.zeros((meta_rows, 128), jnp.int32)
    raw_in[i, 0:ni, 0:nq] = (flags_ref[...] > 0).astype(jnp.int32)
    raw_copies = [send(raw_in.at[i], raw_in.at[i], {"item": lax.rem(i + k, ni)}) for k in range(1, ni)]
    q_all[rows(q_pos * q_rows, q_rows), :] = query_ref[...]
    lane_row = lax.broadcasted_iota(jnp.int32, (1, 128), 1)
    first_lane = pl.multiple_of(lax.div(i, per) * 128, 128)
    found = targets_ref[:, pl.ds(first_lane, 128)]
    shift = lax.rem(q_pos - i + per * nq * ni, per)
    moved = found
    for h in range(1, per):
        moved = jnp.where(shift == h, pltpu.roll(found, h * q_rows, 1), moved)
    inside = lax.div(lane_row, q_rows) == lax.rem(q_pos, per)
    own_targets = jnp.where(inside, moved, 0)
    loads[0].wait()
    loads[1].wait()
    tokens = tokens_ref[...]
    pre = dot(tokens, w1_ref[...], (1, 0))
    pre_act[...] = pre
    finish(raw_copies)
    parts = [raw_in[t, pl.ds(i, 1), :] for t in range(ni)] + [own_targets]
    if meta_rows > ni + 1:
        parts.append(jnp.zeros((meta_rows - ni - 1, 128), jnp.int32))
    meta_in[q_pos] = jnp.concatenate(parts, axis=0)
    for k in range(1, nq):
        query_copies.append(send(meta_in.at[q_pos], meta_in.at[q_pos], {"query": lax.rem(q + k, nq)}))
    loads[2].wait()
    hidden[...] = jax.nn.silu(pre).astype(BF16)
    i_pos = core * gx + x
    emb_all[rows(i_pos * block, block), :] = dot(hidden[...], w2_ref[...], (1, 0)).astype(BF16)

    finish(gather_start(emb_all, core * gx * block, block, "x"))
    finish(gather_start(emb_all, 0, gx * block, "core"))

    finish(query_copies)
    lane = lax.broadcasted_iota(jnp.int32, (meta_rows, 128), 1)
    want_tiles, flag_tiles = [], []
    for t in range(nq // per):
        want = jnp.zeros((1, 128), jnp.int32)
        flag = jnp.zeros((meta_rows, 128), F32)
        for h in range(per):
            sent = meta_in[t * per + h]
            want = want + sent[ni : ni + 1, :]
            column = jnp.sum(jnp.where(lane == q, sent, 0).astype(F32), axis=1, keepdims=True)
            inside = (lane >= h * q_rows) & (lane < (h + 1) * q_rows)
            flag = flag + jnp.where(inside, column, 0.0)
        want_tiles.append(want)
        flag_tiles.append(flag)
    wanted = jnp.concatenate(want_tiles, axis=1)
    flags_all[...] = jnp.concatenate(flag_tiles, axis=1)

    def located(p):
        item = lax.rem(p, gx) * 2 + lax.div(p, gx)
        first = (item * nq + q) * block
        ids = lax.broadcasted_iota(jnp.int32, (block, n_q), 0)
        hit = ids == (wanted - first)
        live = flags_all[pl.ds(item, 1), :] > 0.5
        return hit, live

    def score_block(p, carried):
        top, total, positive = carried
        hit, live = located(p)
        s = 0.25 * dot(emb_all[rows(p * block, block), :], q_all[...], (1, 1))
        scores[rows(p * block, block), :] = s
        here = jnp.max(s, axis=0, keepdims=True)
        added = jnp.sum(jnp.exp(s - here), axis=0, keepdims=True)
        positive = positive + jnp.sum(jnp.where(hit, s, 0.0), axis=0, keepdims=True)
        here = jnp.where(live, here, -1e30)
        new_top = jnp.maximum(top, here)
        total = total * jnp.exp(top - new_top) + jnp.where(live, added * jnp.exp(here - new_top), 0.0)
        return new_top, total, positive

    start = (jnp.full((1, n_q), -1e30, F32), jnp.zeros((1, n_q), F32), jnp.zeros((1, n_q), F32))
    top, total, positive = lax.fori_loop(0, ni, score_block, start)
    stats_all[0] = jnp.concatenate([top, total, positive, jnp.zeros((5, n_q), F32)], axis=0)
    finish([
        send(stats_all.at[0], stats_all.at[k], {"query": lax.rem(q + k, nq)}) for k in range(1, nq)
    ])
    top = stats_all[0, 0:1, :]
    for k in range(1, nq):
        top = jnp.maximum(top, stats_all[k, 0:1, :])
    total = jnp.zeros((1, n_q), F32)
    positive = jnp.zeros((1, n_q), F32)
    for k in range(nq):
        total = total + stats_all[k, 1:2, :] * jnp.exp(stats_all[k, 0:1, :] - top)
        positive = positive + stats_all[k, 2:3, :]
    log_norm = top + jnp.log(total)
    stats_all[0, 0:1, :] = log_norm - positive
    found = stats_all[0, 0:1, pl.ds(pl.multiple_of(lax.div(q_pos, per) * 128, 128), 128)]
    moved = found
    for h in range(1, per):
        moved = jnp.where(lax.rem(q_pos, per) == h, pltpu.roll(found, (per - h) * q_rows, 1), moved)
    loss_ref[...] = moved[:, :q_rows]

    def grad_block(p, carried):
        hit, live = located(p)
        s = scores[rows(p * block, block), :]
        weights = jnp.where(live, jnp.exp(s - log_norm), 0.0)
        c = (weights - hit.astype(F32)).astype(BF16)
        coeffs[rows(p * block, block), :] = c
        e_acc[rows(p * block, block), :] = 0.25 * dot(c, q_all[...], (1, 0))
        return carried

    e_size = gx * block
    pairs = []
    for k in list(range(1, gx)) + [0]:
        t = lax.rem(x + k, gx)
        grad_block((1 - core) * gx + t, 0)
        leaving = rows(((1 - core) * gx + t) * block, block)
        landed = e_recv_c.at[rows(t * block, block)]
        pairs.append(send(e_acc.at[leaving], landed, {"item": x * 2 + 1 - core}))
        grad_block(core * gx + t, 0)
        if k > 0:
            here = rows((core * gx + t) * block, block)
            pairs[-1].wait()
            e_acc[here, :] = e_acc[here, :] + e_recv_c[rows(t * block, block), :]
            pairs[-1] = send(e_acc.at[here], e_recv_x.at[rows((k - 1) * block, block)], {"item": t * 2 + core})
    q_acc[...] = 0.25 * dot(coeffs[...], emb_all[...], (0, 0))
    q_copies = reduce_start(q_acc, q_recv_y, 0, gz * q_rows, "y")
    e_base = (core * gx + x) * block
    pairs[-1].wait()
    e_acc[rows(e_base, block), :] = e_acc[rows(e_base, block), :] + e_recv_c[rows(x * block, block), :]
    e_base = reduce_finish(pairs[:-1], e_acc, e_recv_x, core * gx * block, block, "x")
    own_grad = e_acc[rows(e_base, block), :].astype(BF16)

    hid, din = w2_ref.shape[0], tokens.shape[1]
    part = b_acc.shape[0]
    chains = [
        {"acc": a_acc, "out": a_out, "first": 0, "order": ("core", "x", "y", "z")},
        {"acc": a_acc, "out": a_out, "first": part, "order": ("core", "y", "x", "z")},
        {"acc": b_acc, "out": b_out, "first": 0, "order": ("core", "zl", "zh", "x", "y")},
    ]
    landing = {"core": core_recv, "x": x_recv, "y": y_recv, "zl": l_recv, "zh": h_recv, "z": h_recv}

    def descend(n):
        chain = chains[n]
        level = chain.setdefault("level", 0)
        if level == 0:
            chain["base"], chain["size"] = chain["first"], part
        else:
            chain["base"] = reduce_finish(
                chain["copies"], chain["acc"], landing[chain["order"][level - 1]].at[n],
                chain["base"], chain["size"], chain["order"][level - 1],
            )
        if level < len(chain["order"]):
            axis = chain["order"][level]
            chain["size"] = chain["size"] // axes[axis][0]
            chain["copies"] = reduce_start(
                chain["acc"], landing[axis].at[n], chain["base"], chain["size"], axis
            )
            chain["level"] = level + 1
        else:
            here = rows(chain["base"], chain["size"])
            chain["out"][here, :] = (chain["acc"][here, :] * grad_scale).astype(chain["out"].dtype)
            chain["copies"] = []

    def ascend(n):
        chain = chains[n]
        finish(chain["copies"])
        level = chain["level"] - 1
        chain["level"] = level
        if level < 0:
            return
        group, own, _ = axes[chain["order"][level]]
        chain["base"] = chain["base"] - own * chain["size"]
        chain["copies"] = gather_start(
            chain["out"], chain["base"], chain["size"], chain["order"][level]
        )
        chain["size"] = chain["size"] * group

    second = dot(hidden[...], own_grad, (0, 0))
    for j in range(width // 128):
        b_acc[j * hid : (j + 1) * hid, :] = second[:, j * 128 : (j + 1) * 128]
    descend(2)
    q_base = reduce_finish(q_copies, q_acc, q_recv_y, 0, gz * q_rows, "y")
    q_copies = reduce_start(q_acc, q_recv_l, q_base, gh * q_rows, "zl")
    hid_grad = dot(own_grad, w2_ref[...], (1, 1))
    pre = pre_act[...]
    sig = jax.nn.sigmoid(pre)
    pre_grad = (hid_grad * sig * (1.0 + pre * (1.0 - sig))).astype(BF16)
    half = hid // 2
    for n in range(2):
        first = dot(tokens, pre_grad[:, n * half : (n + 1) * half], (0, 0))
        for j in range(half // 128):
            start_row = n * part + j * din
            a_acc[start_row : start_row + din, :] = first[:, j * 128 : (j + 1) * 128]
        descend(n)
        if n == 0:
            descend(2)
            q_base = reduce_finish(q_copies, q_acc, q_recv_l, q_base, gh * q_rows, "zl")
            q_copies = reduce_start(q_acc, q_recv_h, q_base, q_rows, "zh")
    for n in (0, 1, 2, 0, 1):
        descend(n)
    q_base = reduce_finish(q_copies, q_acc, q_recv_h, q_base, q_rows, "zh")
    qgrad_ref[...] = q_acc[rows(q_base, q_rows), :]
    for n in (0, 1, 2, 2, 2):
        descend(n)
    ascend(2)
    for n in (0, 1):
        descend(n)
        ascend(n)
    for n in (2, 0, 1, 2, 0, 1, 2, 0, 1, 2, 0, 1, 2):
        ascend(n)


def on_device(query_emb, targets, eligible_tiles, item_feats, w_first, w_second):
    q_rows, width = query_emb.shape
    ni, nq = lax.axis_size("item"), lax.axis_size("query")
    gx, gz = ni // 2, nq // 2
    tokens = item_feats.reshape(item_feats.shape[1], item_feats.shape[2])
    block, din = tokens.shape
    hid = w_first.shape[1]
    n_q = nq * q_rows
    meta_rows = -(-(ni + 1) // 8) * 8
    a_rows, b_rows = din * hid // 128, hid * width // 128
    part = b_rows
    out_dtype = BF16 if part // (nq * ni) % 16 == 0 else F32
    n_copies = 3 * (nq - 1) + (ni - 1) + 2 * gx + gx + gz + 3 * 2 * (3 + gx - 1 + gz - 1)
    vmem = pltpu.VMEM
    loss, query_grad, g1, g2 = pl.pallas_call(
        functools.partial(window_kernel, (nq, ni, 1.0 / math.sqrt(block * nq * ni))),
        out_shape=(
            jax.ShapeDtypeStruct((1, q_rows), F32),
            jax.ShapeDtypeStruct((q_rows, width), F32),
            jax.ShapeDtypeStruct((a_rows, 128), out_dtype),
            jax.ShapeDtypeStruct((b_rows, 128), out_dtype),
        ),
        in_specs=[pl.BlockSpec(memory_space=vmem)] * 3 + [pl.BlockSpec(memory_space=pl.ANY)] * 3,
        out_specs=(pl.BlockSpec(memory_space=vmem),) * 4,
        scratch_shapes=[
            vmem((block, din), BF16),
            vmem((din, hid), BF16),
            vmem((hid, width), BF16),
            vmem((n_q, width), BF16),
            vmem((ni, meta_rows, 128), jnp.int32),
            vmem((nq, meta_rows, 128), jnp.int32),
            vmem((ni * block, width), BF16),
            vmem((meta_rows, n_q), F32),
            vmem((ni * block, n_q), F32),
            vmem((ni * block, n_q), BF16),
            vmem((nq, 8, n_q), F32),
            vmem((ni * block, width), F32),
            vmem((gx * block, width), F32),
            vmem((max(gx - 1, 1) * block, width), F32),
            vmem((n_q, width), F32),
            vmem((gz * q_rows, width), F32),
            vmem((gz // 2 * q_rows, width), F32),
            vmem((max(gz // 2 - 1, 1) * q_rows, width), F32),
            vmem((block, hid), F32),
            vmem((block, hid), BF16),
            vmem((a_rows, 128), F32),
            vmem((b_rows, 128), F32),
            vmem((3, part // 2, 128), F32),
            vmem((3, part // 2, 128), F32),
            vmem((3, part // 4, 128), F32),
            vmem((3, part // 4, 128), F32),
            vmem((3, part // 4, 128), F32),
            pltpu.SemaphoreType.DMA((n_copies,)),
            pltpu.SemaphoreType.DMA((n_copies,)),
            pltpu.SemaphoreType.DMA((3,)),
        ],
        compiler_params=pltpu.CompilerParams(
            collective_id=0, has_side_effects=True, vmem_limit_bytes=58 * 2**20
        ),
        name="loss_window",
    )(query_emb, targets.reshape(1, -1), eligible_tiles, tokens, w_first, w_second)
    loss = loss.reshape(q_rows)
    g1 = g1.reshape(hid // 128, din, 128).transpose(1, 0, 2).reshape(din, hid).astype(F32)
    g2 = g2.reshape(width // 128, hid, 128).transpose(1, 0, 2).reshape(hid, width).astype(F32)
    return (loss, query_grad, g1, g2)

def small_kernel(
    grad_scale,
    query_ref, targets_ref, flags_ref, tokens_hbm, w1_hbm, w2_hbm,
    loss_ref, qgrad_ref, a_out, b_out,
    tokens_all, w1_ref, w2_ref, q_all, raw_in, meta_in, emb_all, flags_all, scores, coeffs, stats_all,
    e_acc, e_recv_c, e_send, e_recv_x, grad_all, q_acc, q_recv,
    hidden, slope, hid_cols, a_acc, b_acc, a_send, b_send, a_recv, b_recv,
    send_sems, recv_sems, load_sems,
):
    nq, ni, gx, gy, gz = 8, 4, 2, 2, 4
    q, i = lax.axis_index("query"), lax.axis_index("item")
    core, x = lax.rem(i, 2), lax.div(i, 2)
    y, z = lax.rem(q, 2), lax.div(q, 2)
    q_rows, width = query_ref.shape
    n_q = nq * q_rows
    block = tokens_hbm.shape[0]
    hid = w2_ref.shape[0]
    cols = hid // ni
    i_pos = core * gx + x
    loads = [
        pltpu.make_async_copy(src, dst, load_sems.at[n])
        for n, (src, dst) in enumerate((
            (tokens_hbm, tokens_all.at[rows(i_pos * block, block)]), (w1_hbm, w1_ref), (w2_hbm, w2_ref),
        ))
    ]
    for load in loads:
        load.start()

    used = [0]
    started = []

    def send(src, dst, peer):
        slot = used[0]
        used[0] += 1
        copy = pltpu.make_async_remote_copy(
            src_ref=src, dst_ref=dst, send_sem=send_sems.at[slot], recv_sem=recv_sems.at[slot],
            device_id=peer, device_id_type=pl.DeviceIdType.MESH,
        )
        copy.start()
        started.append(copy)
        return copy

    def arrived(copies):
        for copy in copies:
            copy.wait_recv()

    def ring(k):
        return {"query": lax.rem(q + k, nq)}

    def device(c_, x_, y_, z_):
        return {"query": z_ * 2 + y_, "item": x_ * 2 + c_}

    on_core = device(1 - core, x, y, z)
    on_x = device(core, 1 - x, y, z)
    on_cx = device(1 - core, 1 - x, y, z)
    on_y = device(core, x, 1 - y, z)
    on_xy = device(core, 1 - x, 1 - y, z)

    barrier = pltpu.get_barrier_semaphore()
    greeted = [ring(k) for k in range(1, nq)] + [on_core, on_x, on_cx, on_xy]
    for peer in greeted:
        pl.semaphore_signal(barrier, inc=1, device_id=peer, device_id_type=pl.DeviceIdType.MESH)

    q_all[rows(q * q_rows, q_rows), :] = query_ref[...]
    per = 128 // q_rows
    meta_rows = raw_in.shape[1]
    raw_in[i] = jnp.zeros((meta_rows, 128), jnp.int32)
    raw_in[i, 0:ni, 0:nq] = (flags_ref[...] > 0).astype(jnp.int32)
    lane_row = lax.broadcasted_iota(jnp.int32, (1, 128), 1)
    first_lane = pl.multiple_of(lax.div(i, per) * 128, 128)
    found = targets_ref[:, pl.ds(first_lane, 128)]
    shift = lax.rem(q - i + per * nq * ni, per)
    moved = found
    for h in range(1, per):
        moved = jnp.where(shift == h, pltpu.roll(found, h * q_rows, 1), moved)
    inside = lax.div(lane_row, q_rows) == lax.rem(q, per)
    own_targets = jnp.where(inside, moved, 0)

    loads[0].wait()
    loads[1].wait()
    pre = dot(tokens_all[rows(i_pos * block, block), :], w1_ref[...], (1, 0))
    hidden[...] = jax.nn.silu(pre).astype(BF16)
    loads[2].wait()
    emb_all[rows(i_pos * block, block), :] = dot(hidden[...], w2_ref[...], (1, 0)).astype(BF16)
    pl.semaphore_wait(barrier, len(greeted))

    raw_copies = [send(raw_in.at[i], raw_in.at[i], peer) for peer in (on_x, on_cx, on_core)]
    emb_own = emb_all.at[rows(i_pos * block, block)]
    emb_x = send(emb_own, emb_own, on_x)
    emb_c = send(emb_own, emb_own, on_core)
    query_copies = [send(query_ref, q_all.at[rows(q * q_rows, q_rows)], ring(k)) for k in (4, 3, 5, 2, 6, 1, 7)]
    tok_own = tokens_all.at[rows(i_pos * block, block)]
    tok_x = send(tok_own, tok_own, on_x)
    tok_c = send(tok_own, tok_own, on_core)
    arrived(raw_copies)
    parts = [raw_in[t, pl.ds(i, 1), :] for t in range(ni)] + [own_targets]
    parts.append(jnp.zeros((meta_rows - ni - 1, 128), jnp.int32))
    meta_in[q] = jnp.concatenate(parts, axis=0)
    meta_copies = [send(meta_in.at[q], meta_in.at[q], ring(k)) for k in (4, 3, 5, 2, 6, 1, 7)]
    emb_x.wait_recv()
    emb_far = emb_all.at[rows((core * gx + 1 - x) * block, block)]
    emb_f = send(emb_far, emb_far, on_core)

    arrived(meta_copies)
    lane = lax.broadcasted_iota(jnp.int32, (meta_rows, 128), 1)
    want_tiles, flag_tiles = [], []
    for t in range(nq // per):
        want = jnp.zeros((1, 128), jnp.int32)
        flag = jnp.zeros((meta_rows, 128), F32)
        for h in range(per):
            sent = meta_in[t * per + h]
            want = want + sent[ni : ni + 1, :]
            column = jnp.sum(jnp.where(lane == q, sent, 0).astype(F32), axis=1, keepdims=True)
            inside = (lane >= h * q_rows) & (lane < (h + 1) * q_rows)
            flag = flag + jnp.where(inside, column, 0.0)
        want_tiles.append(want)
        flag_tiles.append(flag)
    wanted = jnp.concatenate(want_tiles, axis=1)
    flags_all[...] = jnp.concatenate(flag_tiles, axis=1)

    def located(p):
        item = lax.rem(p, gx) * 2 + lax.div(p, gx)
        first = (item * nq + q) * block
        ids = lax.broadcasted_iota(jnp.int32, (block, n_q), 0)
        hit = ids == (wanted - first)
        live = flags_all[pl.ds(item, 1), :] > 0.5
        return hit, live

    def score_block(p, carried):
        top, total, positive = carried
        hit, live = located(p)
        s = 0.25 * dot(emb_all[rows(p * block, block), :], q_all[...], (1, 1))
        scores[rows(p * block, block), :] = s
        here = jnp.max(s, axis=0, keepdims=True)
        added = jnp.sum(jnp.exp(s - here), axis=0, keepdims=True)
        positive = positive + jnp.sum(jnp.where(hit, s, 0.0), axis=0, keepdims=True)
        here = jnp.where(live, here, -1e30)
        new_top = jnp.maximum(top, here)
        total = total * jnp.exp(top - new_top) + jnp.where(live, added * jnp.exp(here - new_top), 0.0)
        return new_top, total, positive

    arrived(query_copies)
    carried = (jnp.full((1, n_q), -1e30, F32), jnp.zeros((1, n_q), F32), jnp.zeros((1, n_q), F32))
    carried = score_block(i_pos, carried)
    carried = score_block(core * gx + 1 - x, carried)
    emb_c.wait_recv()
    carried = score_block((1 - core) * gx + x, carried)
    emb_f.wait_recv()
    carried = score_block((1 - core) * gx + 1 - x, carried)
    top, total, positive = carried
    part_norm = jnp.where(total > 0.0, top + jnp.log(jnp.maximum(total, 1e-30)), -1e30)
    tiles = n_q // 128

    def stacked(row):
        return [row[:, t * 128 : (t + 1) * 128] for t in range(tiles)]

    stats_all[0] = jnp.concatenate(stacked(part_norm) + stacked(positive), axis=0)
    stats_copies = [send(stats_all.at[0], stats_all.at[k], ring(k)) for k in (4, 3, 5, 2, 6, 1, 7)]
    tok_x.wait_recv()
    tok_far = tokens_all.at[rows((core * gx + 1 - x) * block, block)]
    tok_f = send(tok_far, tok_far, on_core)
    arrived(stats_copies)
    top = stats_all[0, 0:tiles, :]
    positive = stats_all[0, tiles:, :]
    for k in range(1, nq):
        top = jnp.maximum(top, stats_all[k, 0:tiles, :])
        positive = positive + stats_all[k, tiles:, :]
    total = jnp.zeros((tiles, 128), F32)
    for k in range(nq):
        total = total + jnp.exp(stats_all[k, 0:tiles, :] - top)
    norm_tiles = top + jnp.log(total)
    log_norm = jnp.concatenate([norm_tiles[t : t + 1, :] for t in range(tiles)], axis=1)
    losses = norm_tiles - positive
    found = jnp.zeros((1, 128), F32)
    for t in range(tiles):
        found = found + jnp.where(lax.div(q, per) == t, losses[t : t + 1, :], 0.0)
    moved = found
    for h in range(1, per):
        moved = jnp.where(lax.rem(q, per) == h, pltpu.roll(found, (per - h) * q_rows, 1), moved)
    loss_ref[...] = moved[:, :q_rows]

    def grad_block(p):
        hit, live = located(p)
        s = scores[rows(p * block, block), :]
        weights = jnp.where(live, jnp.exp(s - log_norm), 0.0)
        c = (weights - hit.astype(F32)).astype(BF16)
        coeffs[rows(p * block, block), :] = c
        e_acc[rows(p * block, block), :] = 0.25 * dot(c, q_all[...], (1, 0))

    pairs = []
    for t in range(gx):
        p = (1 - core) * gx + t
        grad_block(p)
        pairs.append(send(e_acc.at[rows(p * block, block)], e_recv_c.at[rows(t * block, block)], on_core))
    for t in range(gx):
        grad_block(core * gx + t)
    crossing = []
    for t in range(gx):
        here = rows((core * gx + t) * block, block)
        slot = rows(t * block, block)
        pairs[t].wait_recv()
        part = e_acc[here, :] + e_recv_c[slot, :]
        e_acc[here, :] = part
        e_send[slot, :] = part.astype(BF16)
        crossing.append(send(e_send.at[slot], e_recv_x.at[slot], on_x))
    q_acc[...] = 0.25 * dot(coeffs[...], emb_all[...], (0, 0))
    q_copies = [
        send(
            q_acc.at[rows(lax.rem(q + k, nq) * q_rows, q_rows)],
            q_recv.at[rows((k - 1) * q_rows, q_rows)], ring(k),
        )
        for k in (4, 3, 5, 2, 6, 1, 7)
    ]

    my_cols = pl.ds(pl.multiple_of(i * cols, 128), cols)
    arrived([tok_c, tok_f])
    for p in range(ni):
        part = rows(p * block, block)
        pre = dot(tokens_all[part, :], w1_ref[:, my_cols], (1, 0))
        sig = jax.nn.sigmoid(pre)
        hid_cols[part, :] = jax.nn.silu(pre).astype(BF16)
        slope[part, :] = sig * (1.0 + pre * (1.0 - sig))
    w2_cols = w2_ref[rows(i * cols, cols), :]

    def tower_b(p, first):
        part = rows(p * block, block)
        b = dot(hid_cols[part, :], grad_all[part, :], (0, 0))
        b_acc[...] = b if first else b_acc[...] + b

    def tower_a(p, first):
        part = rows(p * block, block)
        pre_grad = (dot(grad_all[part, :], w2_cols, (1, 1)) * slope[part, :]).astype(BF16)
        a = dot(tokens_all[part, :], pre_grad, (0, 0))
        a_acc[...] = a if first else a_acc[...] + a

    for t in range(gx):
        mine, theirs = core * gx + t, (1 - core) * gx + t
        here = rows(mine * block, block)
        crossing[t].wait_recv()
        grad_all[here, :] = (e_acc[here, :] + e_recv_x[rows(t * block, block), :].astype(F32)).astype(BF16)
        over = send(grad_all.at[here], grad_all.at[here], on_core)
        tower_b(mine, t == 0)
        tower_a(mine, t == 0)
        over.wait_recv()
        tower_b(theirs, False)
        if t == gx - 1:
            b_rows = cols // nq
            b_send[...] = b_acc[...].astype(BF16)
            b_copies = [
                send(
                    b_send.at[rows(lax.rem(q + k, nq) * b_rows, b_rows)],
                    b_recv.at[rows((k - 1) * b_rows, b_rows)], ring(k),
                )
                for k in (4, 3, 5, 2, 6, 1, 7)
            ]
        tower_a(theirs, False)
    a_rows = a_acc.shape[0] // nq
    a_send[...] = a_acc[...].astype(BF16)
    a_copies = [
        send(
            a_send.at[rows(lax.rem(q + k, nq) * a_rows, a_rows)],
            a_recv.at[rows((k - 1) * a_rows, a_rows)], ring(k),
        )
        for k in (4, 3, 5, 2, 6, 1, 7)
    ]

    arrived(q_copies)
    total = q_acc[rows(q * q_rows, q_rows), :]
    for k in range(1, nq):
        total = total + q_recv[rows((k - 1) * q_rows, q_rows), :]
    qgrad_ref[...] = total

    def gather_own(copies, acc, recv, out, size):
        arrived(copies)
        total = acc[rows(q * size, size), :]
        for k in range(1, nq):
            total = total + recv[rows((k - 1) * size, size), :].astype(F32)
        out[x, core, z, y] = (total * grad_scale).astype(BF16)
        own = out.at[x, core, z, y]
        up = [send(own, own, device(core, x, y, lax.rem(z + k, gz))) for k in (2, 1, 3)]
        over = [[send(own, own, peer) for peer in (on_xy, on_x, on_y)]]
        return up, over

    def gather_far(up, over, out):
        for n, k in enumerate((2, 1, 3)):
            up[n].wait_recv()
            far = out.at[x, core, lax.rem(z - k + gz, gz), y]
            over.append([send(far, far, peer) for peer in (on_xy, on_x, on_y)])
        own = out.at[x, core, :, y]
        return [send(own, own, on_core)]

    def gather_core(over, out):
        crossed = []
        for n, (x_, y_) in ((1, (1 - x, y)), (2, (x, 1 - y)), (0, (1 - x, 1 - y))):
            arrived([four[n] for four in over])
            own = out.at[x_, core, :, y_]
            crossed.append(send(own, own, on_core))
        return crossed

    b_up, b_over = gather_own(b_copies, b_acc, b_recv, b_out, b_rows)
    a_up, a_over = gather_own(a_copies, a_acc, a_recv, a_out, a_rows)
    crossed = gather_far(b_up, b_over, b_out)
    crossed += gather_far(a_up, a_over, a_out)
    crossed += gather_core(b_over, b_out)
    crossed += gather_core(a_over, a_out)
    arrived(crossed)
    for copy in started:
        copy.wait_send()


def finish_kernel(loss_in, qgrad_in, a_in, b_in, loss_ref, qgrad_ref, a_ref, b_ref):
    loss_ref[...] = loss_in[...]
    qgrad_ref[...] = qgrad_in[...]
    for t in range(a_in.shape[0]):
        for r in range(a_in.shape[1]):
            size, cols = a_in.shape[2], a_in.shape[3]
            a_ref[r * size : (r + 1) * size, t * cols : (t + 1) * cols] = a_in[t, r].astype(F32)
    b_ref[...] = b_in[...].astype(F32)


def on_device_small(query_emb, targets, eligible_tiles, item_feats, w_first, w_second):
    q_rows, width = query_emb.shape
    ni, nq = lax.axis_size("item"), lax.axis_size("query")
    tokens = item_feats.reshape(item_feats.shape[1], item_feats.shape[2])
    block, din = tokens.shape
    hid = w_first.shape[1]
    n_q, items, cols = nq * q_rows, ni * block, hid // ni
    a_rows, b_rows = din // nq, cols // nq
    vmem = pltpu.VMEM
    out = (2, 2, nq // 2, 2)
    loss, query_grad, g1, g2 = pl.pallas_call(
        functools.partial(small_kernel, 1.0 / math.sqrt(items * nq)),
        out_shape=(
            jax.ShapeDtypeStruct((1, q_rows), F32),
            jax.ShapeDtypeStruct((q_rows, width), F32),
            jax.ShapeDtypeStruct(out + (a_rows, cols), BF16),
            jax.ShapeDtypeStruct(out + (b_rows, width), BF16),
        ),
        in_specs=[pl.BlockSpec(memory_space=vmem)] * 3 + [pl.BlockSpec(memory_space=pl.ANY)] * 3,
        out_specs=(pl.BlockSpec(memory_space=vmem),) * 4,
        scratch_shapes=[
            vmem((items, din), BF16),
            vmem((din, hid), BF16),
            vmem((hid, width), BF16),
            vmem((n_q, width), BF16),
            vmem((ni, 8, 128), jnp.int32),
            vmem((nq, 8, 128), jnp.int32),
            vmem((items, width), BF16),
            vmem((8, n_q), F32),
            vmem((items, n_q), F32),
            vmem((items, n_q), BF16),
            vmem((nq, 2 * n_q // 128, 128), F32),
            vmem((items, width), F32),
            vmem((2 * block, width), F32),
            vmem((2 * block, width), BF16),
            vmem((2 * block, width), BF16),
            vmem((items, width), BF16),
            vmem((n_q, width), F32),
            vmem(((nq - 1) * q_rows, width), F32),
            vmem((block, hid), BF16),
            vmem((items, cols), F32),
            vmem((items, cols), BF16),
            vmem((din, cols), F32),
            vmem((cols, width), F32),
            vmem((din, cols), BF16),
            vmem((cols, width), BF16),
            vmem(((nq - 1) * a_rows, cols), BF16),
            vmem(((nq - 1) * b_rows, width), BF16),
            pltpu.SemaphoreType.DMA((112,)),
            pltpu.SemaphoreType.DMA((112,)),
            pltpu.SemaphoreType.DMA((3,)),
        ],
        compiler_params=pltpu.CompilerParams(
            collective_id=0, has_side_effects=True, vmem_limit_bytes=58 * 2**20
        ),
        name="loss_window",
    )(query_emb, targets.reshape(1, -1), eligible_tiles, tokens, w_first, w_second)
    steps = 4
    loss, query_grad, g1, g2 = pl.pallas_call(
        finish_kernel,
        grid=(steps,),
        out_shape=(
            jax.ShapeDtypeStruct((1, q_rows), F32),
            jax.ShapeDtypeStruct((q_rows, width), F32),
            jax.ShapeDtypeStruct((din, hid), F32),
            jax.ShapeDtypeStruct((ni, nq, b_rows, width), F32),
        ),
        in_specs=[
            pl.BlockSpec((1, q_rows), lambda n: (0, 0)),
            pl.BlockSpec((q_rows // steps, width), lambda n: (n, 0)),
            pl.BlockSpec((ni, nq // steps, a_rows, cols), lambda n: (0, n, 0, 0)),
            pl.BlockSpec((ni, nq // steps, b_rows, width), lambda n: (0, n, 0, 0)),
        ],
        out_specs=(
            pl.BlockSpec((1, q_rows), lambda n: (0, 0)),
            pl.BlockSpec((q_rows // steps, width), lambda n: (n, 0)),
            pl.BlockSpec((din // steps, hid), lambda n: (n, 0)),
            pl.BlockSpec((ni, nq // steps, b_rows, width), lambda n: (0, n, 0, 0)),
        ),
        name="widen",
    )(loss, query_grad, g1.reshape(ni, nq, a_rows, cols), g2.reshape(ni, nq, b_rows, width))
    return loss.reshape(q_rows), query_grad, g1, g2.reshape(hid, width)


def solution(mesh):
    small = mesh.shape["query"] == 8 and mesh.shape["item"] == 4
    return jax.shard_map(
        on_device_small if small else on_device,
        mesh=mesh,
        in_specs=(
            P(("query", "item"), None),
            P("query"),
            P("query", "item"),
            P("item", "query", None),
            P(),
            P(),
        ),
        out_specs=(P(("query", "item")), P(("query", "item"), None), P(), P()),
        check_vma=False,
    )
```

```python
import functools
import math

import jax
import jax.numpy as jnp
from jax import lax
from jax.experimental import pallas as pl
from jax.experimental.pallas import tpu as pltpu
from jax.sharding import PartitionSpec as P

F32 = jnp.float32
BF16 = jnp.bfloat16


def dot(a, b, contract):
    return lax.dot_general(a, b, ((contract[:1], contract[1:]), ((), ())), preferred_element_type=F32)


def rows(start, size):
    return pl.ds(pl.multiple_of(start, math.gcd(size, 256)), size)


def window_kernel(
    shape,
    query_ref, targets_ref, flags_ref, tokens_hbm, w1_hbm, w2_hbm,
    loss_ref, qgrad_ref, a_out, b_out,
    tokens_ref, w1_ref, w2_ref, q_all, raw_in, meta_in, emb_all, flags_all, scores, coeffs, stats_all,
    e_acc, e_recv_c, e_recv_x, q_acc, q_recv_y, q_recv_l, q_recv_h,
    pre_act, hidden, a_acc, b_acc, core_recv, x_recv, y_recv, l_recv, h_recv,
    send_sems, recv_sems, load_sems,
):
    nq, ni, grad_scale = shape
    gx, gz = ni // 2, nq // 2
    q, i = lax.axis_index("query"), lax.axis_index("item")
    core, x = lax.rem(i, 2), lax.div(i, 2)
    y, z = lax.rem(q, 2), lax.div(q, 2)
    zl, zh = lax.rem(z, 2), lax.div(z, 2)
    gh = gz // 2
    q_rows, width = query_ref.shape
    n_q = nq * q_rows
    block = tokens_ref.shape[0]
    used = [0]
    loads = [
        pltpu.make_async_copy(src, dst, load_sems.at[n])
        for n, (src, dst) in enumerate(((tokens_hbm, tokens_ref), (w1_hbm, w1_ref), (w2_hbm, w2_ref)))
    ]
    for load in loads:
        load.start()

    def send(src, dst, peer):
        slot = used[0]
        used[0] += 1
        copy = pltpu.make_async_remote_copy(
            src_ref=src, dst_ref=dst, send_sem=send_sems.at[slot], recv_sem=recv_sems.at[slot],
            device_id=peer, device_id_type=pl.DeviceIdType.MESH,
        )
        copy.start()
        return copy

    def finish(copies):
        for copy in copies:
            copy.wait()

    axes = {
        "core": (2, core, lambda t: {"item": x * 2 + t}),
        "x": (gx, x, lambda t: {"item": t * 2 + core}),
        "y": (2, y, lambda t: {"query": z * 2 + t}),
        "z": (gz, z, lambda t: {"query": t * 2 + y}),
        "zl": (2, zl, lambda t: {"query": (zh * 2 + t) * 2 + y}),
        "zh": (gh, zh, lambda t: {"query": (t * 2 + zl) * 2 + y}),
    }

    def reduce_start(acc, recv, base, size, axis):
        group, own, peer = axes[axis]
        copies = []
        for k in range(1, group):
            there = lax.rem(own + k, group)
            copies.append(
                send(acc.at[rows(base + there * size, size)], recv.at[rows((k - 1) * size, size)], peer(there))
            )
        return copies

    def reduce_finish(copies, acc, recv, base, size, axis):
        group, own, _ = axes[axis]
        finish(copies)
        here = rows(base + own * size, size)
        total = acc[here, :]
        for k in range(1, group):
            total = total + recv[rows((k - 1) * size, size), :]
        acc[here, :] = total
        return base + own * size

    def gather_start(buf, base, size, axis):
        group, own, peer = axes[axis]
        here = buf.at[rows(base + own * size, size)]
        return [send(here, here, peer(lax.rem(own + k, group))) for k in range(1, group)]

    barrier = pltpu.get_barrier_semaphore()
    for k in range(1, nq):
        pl.semaphore_signal(
            barrier, inc=1, device_id={"query": lax.rem(q + k, nq)}, device_id_type=pl.DeviceIdType.MESH
        )
    for k in range(1, ni):
        pl.semaphore_signal(
            barrier, inc=1, device_id={"item": lax.rem(i + k, ni)}, device_id_type=pl.DeviceIdType.MESH
        )
    pl.semaphore_wait(barrier, nq + ni - 2)

    q_pos = (y * 2 + zl) * gh + zh
    query_copies = []
    for k in range(1, nq):
        there = lax.rem(q + k, nq)
        query_copies.append(send(query_ref, q_all.at[rows(q_pos * q_rows, q_rows)], {"query": there}))
    per = 128 // q_rows
    meta_rows = raw_in.shape[1]
    raw_in[i] = jnp.zeros((meta_rows, 128), jnp.int32)
    raw_in[i, 0:ni, 0:nq] = (flags_ref[...] > 0).astype(jnp.int32)
    raw_copies = [send(raw_in.at[i], raw_in.at[i], {"item": lax.rem(i + k, ni)}) for k in range(1, ni)]
    q_all[rows(q_pos * q_rows, q_rows), :] = query_ref[...]
    lane_row = lax.broadcasted_iota(jnp.int32, (1, 128), 1)
    first_lane = pl.multiple_of(lax.div(i, per) * 128, 128)
    found = targets_ref[:, pl.ds(first_lane, 128)]
    shift = lax.rem(q_pos - i + per * nq * ni, per)
    moved = found
    for h in range(1, per):
        moved = jnp.where(shift == h, pltpu.roll(found, h * q_rows, 1), moved)
    inside = lax.div(lane_row, q_rows) == lax.rem(q_pos, per)
    own_targets = jnp.where(inside, moved, 0)
    loads[0].wait()
    loads[1].wait()
    tokens = tokens_ref[...]
    pre = dot(tokens, w1_ref[...], (1, 0))
    pre_act[...] = pre
    finish(raw_copies)
    parts = [raw_in[t, pl.ds(i, 1), :] for t in range(ni)] + [own_targets]
    if meta_rows > ni + 1:
        parts.append(jnp.zeros((meta_rows - ni - 1, 128), jnp.int32))
    meta_in[q_pos] = jnp.concatenate(parts, axis=0)
    for k in range(1, nq):
        query_copies.append(send(meta_in.at[q_pos], meta_in.at[q_pos], {"query": lax.rem(q + k, nq)}))
    loads[2].wait()
    hidden[...] = jax.nn.silu(pre).astype(BF16)
    i_pos = core * gx + x
    emb_all[rows(i_pos * block, block), :] = dot(hidden[...], w2_ref[...], (1, 0)).astype(BF16)

    finish(gather_start(emb_all, core * gx * block, block, "x"))
    finish(gather_start(emb_all, 0, gx * block, "core"))

    finish(query_copies)
    lane = lax.broadcasted_iota(jnp.int32, (meta_rows, 128), 1)
    want_tiles, flag_tiles = [], []
    for t in range(nq // per):
        want = jnp.zeros((1, 128), jnp.int32)
        flag = jnp.zeros((meta_rows, 128), F32)
        for h in range(per):
            sent = meta_in[t * per + h]
            want = want + sent[ni : ni + 1, :]
            column = jnp.sum(jnp.where(lane == q, sent, 0).astype(F32), axis=1, keepdims=True)
            inside = (lane >= h * q_rows) & (lane < (h + 1) * q_rows)
            flag = flag + jnp.where(inside, column, 0.0)
        want_tiles.append(want)
        flag_tiles.append(flag)
    wanted = jnp.concatenate(want_tiles, axis=1)
    flags_all[...] = jnp.concatenate(flag_tiles, axis=1)

    def located(p):
        item = lax.rem(p, gx) * 2 + lax.div(p, gx)
        first = (item * nq + q) * block
        ids = lax.broadcasted_iota(jnp.int32, (block, n_q), 0)
        hit = ids == (wanted - first)
        live = flags_all[pl.ds(item, 1), :] > 0.5
        return hit, live

    def score_block(p, carried):
        top, total, positive = carried
        hit, live = located(p)
        s = 0.25 * dot(emb_all[rows(p * block, block), :], q_all[...], (1, 1))
        scores[rows(p * block, block), :] = s
        here = jnp.max(s, axis=0, keepdims=True)
        added = jnp.sum(jnp.exp(s - here), axis=0, keepdims=True)
        positive = positive + jnp.sum(jnp.where(hit, s, 0.0), axis=0, keepdims=True)
        here = jnp.where(live, here, -1e30)
        new_top = jnp.maximum(top, here)
        total = total * jnp.exp(top - new_top) + jnp.where(live, added * jnp.exp(here - new_top), 0.0)
        return new_top, total, positive

    start = (jnp.full((1, n_q), -1e30, F32), jnp.zeros((1, n_q), F32), jnp.zeros((1, n_q), F32))
    top, total, positive = lax.fori_loop(0, ni, score_block, start)
    stats_all[0] = jnp.concatenate([top, total, positive, jnp.zeros((5, n_q), F32)], axis=0)
    finish([
        send(stats_all.at[0], stats_all.at[k], {"query": lax.rem(q + k, nq)}) for k in range(1, nq)
    ])
    top = stats_all[0, 0:1, :]
    for k in range(1, nq):
        top = jnp.maximum(top, stats_all[k, 0:1, :])
    total = jnp.zeros((1, n_q), F32)
    positive = jnp.zeros((1, n_q), F32)
    for k in range(nq):
        total = total + stats_all[k, 1:2, :] * jnp.exp(stats_all[k, 0:1, :] - top)
        positive = positive + stats_all[k, 2:3, :]
    log_norm = top + jnp.log(total)
    stats_all[0, 0:1, :] = log_norm - positive
    found = stats_all[0, 0:1, pl.ds(pl.multiple_of(lax.div(q_pos, per) * 128, 128), 128)]
    moved = found
    for h in range(1, per):
        moved = jnp.where(lax.rem(q_pos, per) == h, pltpu.roll(found, (per - h) * q_rows, 1), moved)
    loss_ref[...] = moved[:, :q_rows]

    def grad_block(p, carried):
        hit, live = located(p)
        s = scores[rows(p * block, block), :]
        weights = jnp.where(live, jnp.exp(s - log_norm), 0.0)
        c = (weights - hit.astype(F32)).astype(BF16)
        coeffs[rows(p * block, block), :] = c
        e_acc[rows(p * block, block), :] = 0.25 * dot(c, q_all[...], (1, 0))
        return carried

    e_size = gx * block
    pairs = []
    for k in list(range(1, gx)) + [0]:
        t = lax.rem(x + k, gx)
        grad_block((1 - core) * gx + t, 0)
        leaving = rows(((1 - core) * gx + t) * block, block)
        landed = e_recv_c.at[rows(t * block, block)]
        pairs.append(send(e_acc.at[leaving], landed, {"item": x * 2 + 1 - core}))
        grad_block(core * gx + t, 0)
        if k > 0:
            here = rows((core * gx + t) * block, block)
            pairs[-1].wait()
            e_acc[here, :] = e_acc[here, :] + e_recv_c[rows(t * block, block), :]
            pairs[-1] = send(e_acc.at[here], e_recv_x.at[rows((k - 1) * block, block)], {"item": t * 2 + core})
    q_acc[...] = 0.25 * dot(coeffs[...], emb_all[...], (0, 0))
    q_copies = reduce_start(q_acc, q_recv_y, 0, gz * q_rows, "y")
    e_base = (core * gx + x) * block
    pairs[-1].wait()
    e_acc[rows(e_base, block), :] = e_acc[rows(e_base, block), :] + e_recv_c[rows(x * block, block), :]
    e_base = reduce_finish(pairs[:-1], e_acc, e_recv_x, core * gx * block, block, "x")
    own_grad = e_acc[rows(e_base, block), :].astype(BF16)

    hid, din = w2_ref.shape[0], tokens.shape[1]
    part = b_acc.shape[0]
    chains = [
        {"acc": a_acc, "out": a_out, "first": 0, "order": ("core", "x", "y", "z")},
        {"acc": a_acc, "out": a_out, "first": part, "order": ("core", "y", "x", "z")},
        {"acc": b_acc, "out": b_out, "first": 0, "order": ("core", "zl", "zh", "x", "y")},
    ]
    landing = {"core": core_recv, "x": x_recv, "y": y_recv, "zl": l_recv, "zh": h_recv, "z": h_recv}

    def descend(n):
        chain = chains[n]
        level = chain.setdefault("level", 0)
        if level == 0:
            chain["base"], chain["size"] = chain["first"], part
        else:
            chain["base"] = reduce_finish(
                chain["copies"], chain["acc"], landing[chain["order"][level - 1]].at[n],
                chain["base"], chain["size"], chain["order"][level - 1],
            )
        if level < len(chain["order"]):
            axis = chain["order"][level]
            chain["size"] = chain["size"] // axes[axis][0]
            chain["copies"] = reduce_start(
                chain["acc"], landing[axis].at[n], chain["base"], chain["size"], axis
            )
            chain["level"] = level + 1
        else:
            here = rows(chain["base"], chain["size"])
            chain["out"][here, :] = (chain["acc"][here, :] * grad_scale).astype(chain["out"].dtype)
            chain["copies"] = []

    def ascend(n):
        chain = chains[n]
        finish(chain["copies"])
        level = chain["level"] - 1
        chain["level"] = level
        if level < 0:
            return
        group, own, _ = axes[chain["order"][level]]
        chain["base"] = chain["base"] - own * chain["size"]
        chain["copies"] = gather_start(
            chain["out"], chain["base"], chain["size"], chain["order"][level]
        )
        chain["size"] = chain["size"] * group

    second = dot(hidden[...], own_grad, (0, 0))
    for j in range(width // 128):
        b_acc[j * hid : (j + 1) * hid, :] = second[:, j * 128 : (j + 1) * 128]
    descend(2)
    q_base = reduce_finish(q_copies, q_acc, q_recv_y, 0, gz * q_rows, "y")
    q_copies = reduce_start(q_acc, q_recv_l, q_base, gh * q_rows, "zl")
    hid_grad = dot(own_grad, w2_ref[...], (1, 1))
    pre = pre_act[...]
    sig = jax.nn.sigmoid(pre)
    pre_grad = (hid_grad * sig * (1.0 + pre * (1.0 - sig))).astype(BF16)
    half = hid // 2
    for n in range(2):
        first = dot(tokens, pre_grad[:, n * half : (n + 1) * half], (0, 0))
        for j in range(half // 128):
            start_row = n * part + j * din
            a_acc[start_row : start_row + din, :] = first[:, j * 128 : (j + 1) * 128]
        descend(n)
        if n == 0:
            descend(2)
            q_base = reduce_finish(q_copies, q_acc, q_recv_l, q_base, gh * q_rows, "zl")
            q_copies = reduce_start(q_acc, q_recv_h, q_base, q_rows, "zh")
    for n in (0, 1, 2, 0, 1):
        descend(n)
    q_base = reduce_finish(q_copies, q_acc, q_recv_h, q_base, q_rows, "zh")
    qgrad_ref[...] = q_acc[rows(q_base, q_rows), :]
    for n in (0, 1, 2, 2, 2):
        descend(n)
    ascend(2)
    for n in (0, 1):
        descend(n)
        ascend(n)
    for n in (2, 0, 1, 2, 0, 1, 2, 0, 1, 2, 0, 1, 2):
        ascend(n)


def on_device(query_emb, targets, eligible_tiles, item_feats, w_first, w_second):
    q_rows, width = query_emb.shape
    ni, nq = lax.axis_size("item"), lax.axis_size("query")
    gx, gz = ni // 2, nq // 2
    tokens = item_feats.reshape(item_feats.shape[1], item_feats.shape[2])
    block, din = tokens.shape
    hid = w_first.shape[1]
    n_q = nq * q_rows
    meta_rows = -(-(ni + 1) // 8) * 8
    a_rows, b_rows = din * hid // 128, hid * width // 128
    part = b_rows
    out_dtype = BF16 if part // (nq * ni) % 16 == 0 else F32
    n_copies = 3 * (nq - 1) + (ni - 1) + 2 * gx + gx + gz + 3 * 2 * (3 + gx - 1 + gz - 1)
    vmem = pltpu.VMEM
    loss, query_grad, g1, g2 = pl.pallas_call(
        functools.partial(window_kernel, (nq, ni, 1.0 / math.sqrt(block * nq * ni))),
        out_shape=(
            jax.ShapeDtypeStruct((1, q_rows), F32),
            jax.ShapeDtypeStruct((q_rows, width), F32),
            jax.ShapeDtypeStruct((a_rows, 128), out_dtype),
            jax.ShapeDtypeStruct((b_rows, 128), out_dtype),
        ),
        in_specs=[pl.BlockSpec(memory_space=vmem)] * 3 + [pl.BlockSpec(memory_space=pl.ANY)] * 3,
        out_specs=(pl.BlockSpec(memory_space=vmem),) * 4,
        scratch_shapes=[
            vmem((block, din), BF16),
            vmem((din, hid), BF16),
            vmem((hid, width), BF16),
            vmem((n_q, width), BF16),
            vmem((ni, meta_rows, 128), jnp.int32),
            vmem((nq, meta_rows, 128), jnp.int32),
            vmem((ni * block, width), BF16),
            vmem((meta_rows, n_q), F32),
            vmem((ni * block, n_q), F32),
            vmem((ni * block, n_q), BF16),
            vmem((nq, 8, n_q), F32),
            vmem((ni * block, width), F32),
            vmem((gx * block, width), F32),
            vmem((max(gx - 1, 1) * block, width), F32),
            vmem((n_q, width), F32),
            vmem((gz * q_rows, width), F32),
            vmem((gz // 2 * q_rows, width), F32),
            vmem((max(gz // 2 - 1, 1) * q_rows, width), F32),
            vmem((block, hid), F32),
            vmem((block, hid), BF16),
            vmem((a_rows, 128), F32),
            vmem((b_rows, 128), F32),
            vmem((3, part // 2, 128), F32),
            vmem((3, part // 2, 128), F32),
            vmem((3, part // 4, 128), F32),
            vmem((3, part // 4, 128), F32),
            vmem((3, part // 4, 128), F32),
            pltpu.SemaphoreType.DMA((n_copies,)),
            pltpu.SemaphoreType.DMA((n_copies,)),
            pltpu.SemaphoreType.DMA((3,)),
        ],
        compiler_params=pltpu.CompilerParams(
            collective_id=0, has_side_effects=True, vmem_limit_bytes=58 * 2**20
        ),
        name="loss_window",
    )(query_emb, targets.reshape(1, -1), eligible_tiles, tokens, w_first, w_second)
    loss = loss.reshape(q_rows)
    g1 = g1.reshape(hid // 128, din, 128).transpose(1, 0, 2).reshape(din, hid).astype(F32)
    g2 = g2.reshape(width // 128, hid, 128).transpose(1, 0, 2).reshape(hid, width).astype(F32)
    return (loss, query_grad, g1, g2)

def small_kernel(
    grad_scale,
    query_ref, targets_ref, flags_ref, tokens_hbm, w1_hbm, w2_hbm,
    loss_ref, qgrad_ref, a_out, b_out,
    tokens_all, w1_ref, w2_ref, q_all, raw_in, meta_in, emb_all, flags_all, scores, coeffs, stats_all,
    tops, e_acc, e_recv_c, e_send, e_recv_x, grad_all, q_acc, q_send, q_recv,
    hidden, slope, hid_cols, a_acc, b_acc, a_send, b_send, a_recv, b_recv, a_all, b_all,
    send_sems, recv_sems, load_sems,
):
    nq, ni, gx, gy, gz = 8, 4, 2, 2, 4
    q, i = lax.axis_index("query"), lax.axis_index("item")
    core, x = lax.rem(i, 2), lax.div(i, 2)
    y, z = lax.rem(q, 2), lax.div(q, 2)
    q_rows, width = query_ref.shape
    n_q = nq * q_rows
    block = tokens_hbm.shape[0]
    hid = w2_ref.shape[0]
    cols = hid // ni
    i_pos = core * gx + x
    loads = [
        pltpu.make_async_copy(src, dst, load_sems.at[n])
        for n, (src, dst) in enumerate((
            (tokens_hbm, tokens_all.at[rows(i_pos * block, block)]), (w1_hbm, w1_ref), (w2_hbm, w2_ref),
        ))
    ]
    for load in loads:
        load.start()

    used = [0]
    started = []

    def send(src, dst, peer):
        slot = used[0]
        used[0] += 1
        copy = pltpu.make_async_remote_copy(
            src_ref=src, dst_ref=dst, send_sem=send_sems.at[slot], recv_sem=recv_sems.at[slot],
            device_id=peer, device_id_type=pl.DeviceIdType.MESH,
        )
        copy.start()
        started.append(copy)
        return copy

    def arrived(copies):
        for copy in copies:
            copy.wait_recv()

    def ring(k):
        return {"query": lax.rem(q + k, nq)}

    def device(c_, x_, y_, z_):
        return {"query": z_ * 2 + y_, "item": x_ * 2 + c_}

    on_core = device(1 - core, x, y, z)
    on_x = device(core, 1 - x, y, z)
    on_cx = device(1 - core, 1 - x, y, z)
    on_y = device(core, x, 1 - y, z)
    on_xy = device(core, 1 - x, 1 - y, z)

    barrier = pltpu.get_barrier_semaphore()
    greeted = [ring(k) for k in range(1, nq)] + [on_core, on_x, on_cx, on_xy]
    for peer in greeted:
        pl.semaphore_signal(barrier, inc=1, device_id=peer, device_id_type=pl.DeviceIdType.MESH)

    q_all[rows(q * q_rows, q_rows), :] = query_ref[...]
    per = 128 // q_rows
    meta_rows = raw_in.shape[1]
    raw_in[i] = jnp.zeros((meta_rows, 128), jnp.int32)
    raw_in[i, 0:ni, 0:nq] = (flags_ref[...] > 0).astype(jnp.int32)
    lane_row = lax.broadcasted_iota(jnp.int32, (1, 128), 1)
    first_lane = pl.multiple_of(lax.div(i, per) * 128, 128)
    found = targets_ref[:, pl.ds(first_lane, 128)]
    shift = lax.rem(q - i + per * nq * ni, per)
    moved = found
    for h in range(1, per):
        moved = jnp.where(shift == h, pltpu.roll(found, h * q_rows, 1), moved)
    inside = lax.div(lane_row, q_rows) == lax.rem(q, per)
    own_targets = jnp.where(inside, moved, 0)

    loads[0].wait()
    loads[1].wait()
    pre = dot(tokens_all[rows(i_pos * block, block), :], w1_ref[...], (1, 0))
    hidden[...] = jax.nn.silu(pre).astype(BF16)
    loads[2].wait()
    emb_all[rows(i_pos * block, block), :] = dot(hidden[...], w2_ref[...], (1, 0)).astype(BF16)
    pl.semaphore_wait(barrier, len(greeted))

    raw_copies = [send(raw_in.at[i], raw_in.at[i], peer) for peer in (on_x, on_cx, on_core)]
    emb_own = emb_all.at[rows(i_pos * block, block)]
    emb_x = send(emb_own, emb_own, on_x)
    emb_c = send(emb_own, emb_own, on_core)
    query_copies = [send(query_ref, q_all.at[rows(q * q_rows, q_rows)], ring(k)) for k in (4, 3, 5, 2, 6, 1, 7)]
    arrived(raw_copies)
    parts = [raw_in[t, pl.ds(i, 1), :] for t in range(ni)] + [own_targets]
    parts.append(jnp.zeros((meta_rows - ni - 1, 128), jnp.int32))
    meta_in[q] = jnp.concatenate(parts, axis=0)
    meta_copies = [send(meta_in.at[q], meta_in.at[q], ring(k)) for k in (4, 3, 5, 2, 6, 1, 7)]
    emb_x.wait_recv()
    emb_far = emb_all.at[rows((core * gx + 1 - x) * block, block)]
    emb_f = send(emb_far, emb_far, on_core)
    tok_own = tokens_all.at[rows(i_pos * block, block)]
    tok_x = send(tok_own, tok_own, on_x)
    tok_c = send(tok_own, tok_own, on_core)

    arrived(meta_copies)
    lane = lax.broadcasted_iota(jnp.int32, (meta_rows, 128), 1)
    want_tiles, flag_tiles = [], []
    for t in range(nq // per):
        want = jnp.zeros((1, 128), jnp.int32)
        flag = jnp.zeros((meta_rows, 128), F32)
        for h in range(per):
            sent = meta_in[t * per + h]
            want = want + sent[ni : ni + 1, :]
            column = jnp.sum(jnp.where(lane == q, sent, 0).astype(F32), axis=1, keepdims=True)
            inside = (lane >= h * q_rows) & (lane < (h + 1) * q_rows)
            flag = flag + jnp.where(inside, column, 0.0)
        want_tiles.append(want)
        flag_tiles.append(flag)
    wanted = jnp.concatenate(want_tiles, axis=1)
    flags_all[...] = jnp.concatenate(flag_tiles, axis=1)

    def located(p):
        item = lax.rem(p, gx) * 2 + lax.div(p, gx)
        first = (item * nq + q) * block
        ids = lax.broadcasted_iota(jnp.int32, (block, n_q), 0)
        hit = ids == (wanted - first)
        live = flags_all[pl.ds(item, 1), :] > 0.5
        return hit, live

    def score_block(p, carried):
        top, total, positive = carried
        hit, live = located(p)
        s = 0.25 * dot(emb_all[rows(p * block, block), :], q_all[...], (1, 1))
        here = jnp.max(s, axis=0, keepdims=True)
        e = jnp.exp(s - here)
        scores[rows(p * block, block), :] = e
        added = jnp.sum(e, axis=0, keepdims=True)
        positive = positive + jnp.sum(jnp.where(hit, s, 0.0), axis=0, keepdims=True)
        here = jnp.where(live, here, -1e30)
        tops[pl.ds(p, 1), :] = here
        new_top = jnp.maximum(top, here)
        total = total * jnp.exp(top - new_top) + jnp.where(live, added * jnp.exp(here - new_top), 0.0)
        return new_top, total, positive

    arrived(query_copies)
    carried = (jnp.full((1, n_q), -1e30, F32), jnp.zeros((1, n_q), F32), jnp.zeros((1, n_q), F32))
    carried = score_block(i_pos, carried)
    carried = score_block(core * gx + 1 - x, carried)
    emb_c.wait_recv()
    carried = score_block((1 - core) * gx + x, carried)
    emb_f.wait_recv()
    carried = score_block((1 - core) * gx + 1 - x, carried)
    top, total, positive = carried
    part_norm = jnp.where(total > 0.0, top + jnp.log(jnp.maximum(total, 1e-30)), -1e30)
    tiles = n_q // 128

    def stacked(row):
        return [row[:, t * 128 : (t + 1) * 128] for t in range(tiles)]

    stats_all[0] = jnp.concatenate(stacked(part_norm) + stacked(positive), axis=0)
    stats_copies = [send(stats_all.at[0], stats_all.at[k], ring(k)) for k in (4, 3, 5, 2, 6, 1, 7)]
    my_cols = pl.ds(pl.multiple_of(i * cols, 128), cols)

    def forward_cols(p):
        part = rows(p * block, block)
        pre = dot(tokens_all[part, :], w1_ref[:, my_cols], (1, 0))
        sig = jax.nn.sigmoid(pre)
        hid_cols[part, :] = (pre * sig).astype(BF16)
        slope[part, :] = sig * (1.0 + pre * (1.0 - sig))

    w2_cols = w2_ref[rows(i * cols, cols), :]
    forward_cols(i_pos)
    tok_c.wait_recv()
    forward_cols((1 - core) * gx + x)
    arrived(stats_copies)
    top = stats_all[0, 0:tiles, :]
    positive = stats_all[0, tiles:, :]
    for k in range(1, nq):
        top = jnp.maximum(top, stats_all[k, 0:tiles, :])
        positive = positive + stats_all[k, tiles:, :]
    total = jnp.zeros((tiles, 128), F32)
    for k in range(nq):
        total = total + jnp.exp(stats_all[k, 0:tiles, :] - top)
    norm_tiles = top + jnp.log(total)
    log_norm = jnp.concatenate([norm_tiles[t : t + 1, :] for t in range(tiles)], axis=1)
    def grad_block(p):
        hit, _ = located(p)
        factor = jnp.exp(tops[pl.ds(p, 1), :] - log_norm)
        c = (scores[rows(p * block, block), :] * factor - hit.astype(F32)).astype(BF16)
        coeffs[rows(p * block, block), :] = c
        e_acc[rows(p * block, block), :] = 0.25 * dot(c, q_all[...], (1, 0))

    crossing = []
    for t in range(gx):
        p = (1 - core) * gx + t
        slot = rows(t * block, block)
        grad_block(p)
        pair = send(e_acc.at[rows(p * block, block)], e_recv_c.at[slot], on_core)
        grad_block(core * gx + t)
        here = rows((core * gx + t) * block, block)
        pair.wait_recv()
        part = e_acc[here, :] + e_recv_c[slot, :]
        e_acc[here, :] = part
        e_send[slot, :] = part.astype(BF16)
        crossing.append(send(e_send.at[slot], e_recv_x.at[slot], on_x))
    q_acc[...] = 0.25 * dot(coeffs[...], emb_all[...], (0, 0))
    q_send[...] = q_acc[...].astype(BF16)
    q_copies = [
        send(
            q_send.at[rows(lax.rem(q + k, nq) * q_rows, q_rows)],
            q_recv.at[rows((k - 1) * q_rows, q_rows)], ring(k),
        )
        for k in (4, 3, 5, 2, 6, 1, 7)
    ]
    tok_x.wait_recv()
    tok_far = tokens_all.at[rows((core * gx + 1 - x) * block, block)]
    tok_f = send(tok_far, tok_far, on_core)
    forward_cols(core * gx + 1 - x)
    losses = norm_tiles - positive
    found = jnp.zeros((1, 128), F32)
    for t in range(tiles):
        found = found + jnp.where(lax.div(q, per) == t, losses[t : t + 1, :], 0.0)
    moved = found
    for h in range(1, per):
        moved = jnp.where(lax.rem(q, per) == h, pltpu.roll(found, (per - h) * q_rows, 1), moved)
    loss_ref[...] = moved[:, :q_rows]

    tok_f.wait_recv()
    forward_cols((1 - core) * gx + 1 - x)

    def tower_b(p, first):
        part = rows(p * block, block)
        b = dot(hid_cols[part, :], grad_all[part, :], (0, 0))
        b_acc[...] = b if first else b_acc[...] + b

    def tower_a(p, first):
        part = rows(p * block, block)
        pre_grad = (dot(grad_all[part, :], w2_cols, (1, 1)) * slope[part, :]).astype(BF16)
        a = dot(tokens_all[part, :], pre_grad, (0, 0))
        a_acc[...] = a if first else a_acc[...] + a

    for t in range(gx):
        mine, theirs = core * gx + t, (1 - core) * gx + t
        here = rows(mine * block, block)
        crossing[t].wait_recv()
        grad_all[here, :] = (e_acc[here, :] + e_recv_x[rows(t * block, block), :].astype(F32)).astype(BF16)
        over = send(grad_all.at[here], grad_all.at[here], on_core)
        tower_b(mine, t == 0)
        tower_a(mine, t == 0)
        over.wait_recv()
        tower_b(theirs, False)
        if t == gx - 1:
            b_rows = cols // nq
            b_send[...] = b_acc[...].astype(BF16)
            b_copies = [
                send(
                    b_send.at[rows(lax.rem(q + k, nq) * b_rows, b_rows)],
                    b_recv.at[rows((k - 1) * b_rows, b_rows)], ring(k),
                )
                for k in (4, 3, 5, 2, 6, 1, 7)
            ]
        tower_a(theirs, False)
    a_rows = a_acc.shape[0] // nq
    a_send[...] = a_acc[...].astype(BF16)
    a_copies = [
        send(
            a_send.at[rows(lax.rem(q + k, nq) * a_rows, a_rows)],
            a_recv.at[rows((k - 1) * a_rows, a_rows)], ring(k),
        )
        for k in (4, 3, 5, 2, 6, 1, 7)
    ]

    arrived(q_copies)
    total = q_acc[rows(q * q_rows, q_rows), :]
    for k in range(1, nq):
        total = total + q_recv[rows((k - 1) * q_rows, q_rows), :].astype(F32)
    qgrad_ref[...] = total
    kept = []

    def leave(out, x_, y_):
        whole = {id(a_all): a_out, id(b_all): b_out}[id(out)].at[x_, core, :, y_]
        copy = pltpu.make_async_copy(out.at[x_, :, y_], whole, load_sems.at[3 + len(kept)])
        copy.start()
        kept.append(copy)
        return send(out.at[x_, :, y_], whole, on_core)

    def gather_own(copies, acc, recv, out, size):
        arrived(copies)
        total = acc[rows(q * size, size), :]
        for k in range(1, nq):
            total = total + recv[rows((k - 1) * size, size), :].astype(F32)
        out[x, z, y] = (total * grad_scale).astype(BF16)
        own = out.at[x, z, y]
        up = [send(own, own, device(core, x, y, lax.rem(z + k, gz))) for k in (2, 1, 3)]
        over = [[send(own, own, peer) for peer in (on_xy, on_x, on_y)]]
        return up, over

    def gather_far(up, over, out):
        for n, k in enumerate((2, 1, 3)):
            up[n].wait_recv()
            far = out.at[x, lax.rem(z - k + gz, gz), y]
            over.append([send(far, far, peer) for peer in (on_xy, on_x, on_y)])
        return [leave(out, x, y)]

    def gather_core(over, out):
        crossed = []
        for n, (x_, y_) in ((1, (1 - x, y)), (2, (x, 1 - y)), (0, (1 - x, 1 - y))):
            arrived([four[n] for four in over])
            crossed.append(leave(out, x_, y_))
        return crossed

    b_up, b_over = gather_own(b_copies, b_acc, b_recv, b_all, b_rows)
    a_up, a_over = gather_own(a_copies, a_acc, a_recv, a_all, a_rows)
    crossed = gather_far(b_up, b_over, b_all)
    crossed += gather_far(a_up, a_over, a_all)
    crossed += gather_core(b_over, b_all)
    crossed += gather_core(a_over, a_all)
    arrived(crossed)
    for copy in kept:
        copy.wait()
    for copy in started:
        copy.wait_send()


def finish_kernel(loss_in, qgrad_in, a_in, b_in, loss_ref, qgrad_ref, a_ref, b_ref):
    loss_ref[...] = loss_in[...]
    qgrad_ref[...] = qgrad_in[...]
    for t in range(a_in.shape[0]):
        for r in range(a_in.shape[1]):
            size, cols = a_in.shape[2], a_in.shape[3]
            a_ref[r * size : (r + 1) * size, t * cols : (t + 1) * cols] = a_in[t, r].astype(F32)
    b_ref[...] = b_in[...].astype(F32)


def on_device_small(query_emb, targets, eligible_tiles, item_feats, w_first, w_second):
    q_rows, width = query_emb.shape
    ni, nq = lax.axis_size("item"), lax.axis_size("query")
    tokens = item_feats.reshape(item_feats.shape[1], item_feats.shape[2])
    block, din = tokens.shape
    hid = w_first.shape[1]
    n_q, items, cols = nq * q_rows, ni * block, hid // ni
    a_rows, b_rows = din // nq, cols // nq
    vmem = pltpu.VMEM
    out = (2, 2, nq // 2, 2)
    loss, query_grad, g1, g2 = pl.pallas_call(
        functools.partial(small_kernel, 1.0 / math.sqrt(items * nq)),
        out_shape=(
            jax.ShapeDtypeStruct((1, q_rows), F32),
            jax.ShapeDtypeStruct((q_rows, width), F32),
            jax.ShapeDtypeStruct(out + (a_rows, cols), BF16),
            jax.ShapeDtypeStruct(out + (b_rows, width), BF16),
        ),
        in_specs=[pl.BlockSpec(memory_space=vmem)] * 3 + [pl.BlockSpec(memory_space=pl.ANY)] * 3,
        out_specs=(pl.BlockSpec(memory_space=vmem),) * 2 + (pl.BlockSpec(memory_space=pl.ANY),) * 2,
        scratch_shapes=[
            vmem((items, din), BF16),
            vmem((din, hid), BF16),
            vmem((hid, width), BF16),
            vmem((n_q, width), BF16),
            vmem((ni, 8, 128), jnp.int32),
            vmem((nq, 8, 128), jnp.int32),
            vmem((items, width), BF16),
            vmem((8, n_q), F32),
            vmem((items, n_q), F32),
            vmem((items, n_q), BF16),
            vmem((nq, 2 * n_q // 128, 128), F32),
            vmem((8, n_q), F32),
            vmem((items, width), F32),
            vmem((2 * block, width), F32),
            vmem((2 * block, width), BF16),
            vmem((2 * block, width), BF16),
            vmem((items, width), BF16),
            vmem((n_q, width), F32),
            vmem((n_q, width), BF16),
            vmem(((nq - 1) * q_rows, width), BF16),
            vmem((block, hid), BF16),
            vmem((items, cols), F32),
            vmem((items, cols), BF16),
            vmem((din, cols), F32),
            vmem((cols, width), F32),
            vmem((din, cols), BF16),
            vmem((cols, width), BF16),
            vmem(((nq - 1) * a_rows, cols), BF16),
            vmem(((nq - 1) * b_rows, width), BF16),
            vmem((2, nq // 2, 2, a_rows, cols), BF16),
            vmem((2, nq // 2, 2, b_rows, width), BF16),
            pltpu.SemaphoreType.DMA((112,)),
            pltpu.SemaphoreType.DMA((112,)),
            pltpu.SemaphoreType.DMA((11,)),
        ],
        compiler_params=pltpu.CompilerParams(
            collective_id=0, has_side_effects=True, vmem_limit_bytes=58 * 2**20
        ),
        name="loss_window",
    )(query_emb, targets.reshape(1, -1), eligible_tiles, tokens, w_first, w_second)
    steps = 2
    loss, query_grad, g1, g2 = pl.pallas_call(
        finish_kernel,
        grid=(steps,),
        out_shape=(
            jax.ShapeDtypeStruct((1, q_rows), F32),
            jax.ShapeDtypeStruct((q_rows, width), F32),
            jax.ShapeDtypeStruct((din, hid), F32),
            jax.ShapeDtypeStruct((ni, nq, b_rows, width), F32),
        ),
        in_specs=[
            pl.BlockSpec((1, q_rows), lambda n: (0, 0)),
            pl.BlockSpec((q_rows // steps, width), lambda n: (n, 0)),
            pl.BlockSpec((ni, nq // steps, a_rows, cols), lambda n: (0, n, 0, 0)),
            pl.BlockSpec((ni, nq // steps, b_rows, width), lambda n: (0, n, 0, 0)),
        ],
        out_specs=(
            pl.BlockSpec((1, q_rows), lambda n: (0, 0)),
            pl.BlockSpec((q_rows // steps, width), lambda n: (n, 0)),
            pl.BlockSpec((din // steps, hid), lambda n: (n, 0)),
            pl.BlockSpec((ni, nq // steps, b_rows, width), lambda n: (0, n, 0, 0)),
        ),
        name="widen",
    )(loss, query_grad, g1.reshape(ni, nq, a_rows, cols), g2.reshape(ni, nq, b_rows, width))
    return loss.reshape(q_rows), query_grad, g1, g2.reshape(hid, width)


def solution(mesh):
    small = mesh.shape["query"] == 8 and mesh.shape["item"] == 4
    return jax.shard_map(
        on_device_small if small else on_device,
        mesh=mesh,
        in_specs=(
            P(("query", "item"), None),
            P("query"),
            P("query", "item"),
            P("item", "query", None),
            P(),
            P(),
        ),
        out_specs=(P(("query", "item")), P(("query", "item"), None), P(), P()),
        check_vma=False,
    )
```

```python
import functools
import math

import jax
import jax.numpy as jnp
from jax import lax
from jax.experimental import pallas as pl
from jax.experimental.pallas import tpu as pltpu
from jax.sharding import PartitionSpec as P

F32 = jnp.float32
BF16 = jnp.bfloat16


def dot(a, b, contract):
    return lax.dot_general(a, b, ((contract[:1], contract[1:]), ((), ())), preferred_element_type=F32)


def rows(start, size):
    return pl.ds(pl.multiple_of(start, math.gcd(size, 256)), size)


def window_kernel(
    shape,
    query_ref, targets_ref, flags_ref, tokens_hbm, w1_hbm, w2_hbm,
    loss_ref, qgrad_ref, a_out, b_out,
    tokens_ref, w1_ref, w2_ref, q_all, raw_in, meta_in, emb_all, flags_all, scores, coeffs, stats_all,
    e_acc, e_recv_c, e_recv_x, q_acc, q_recv_y, q_recv_l, q_recv_h,
    pre_act, hidden, a_acc, b_acc, core_recv, x_recv, y_recv, l_recv, h_recv,
    send_sems, recv_sems, load_sems,
):
    nq, ni, grad_scale = shape
    gx, gz = ni // 2, nq // 2
    q, i = lax.axis_index("query"), lax.axis_index("item")
    core, x = lax.rem(i, 2), lax.div(i, 2)
    y, z = lax.rem(q, 2), lax.div(q, 2)
    zl, zh = lax.rem(z, 2), lax.div(z, 2)
    gh = gz // 2
    q_rows, width = query_ref.shape
    n_q = nq * q_rows
    block = tokens_ref.shape[0]
    used = [0]
    loads = [
        pltpu.make_async_copy(src, dst, load_sems.at[n])
        for n, (src, dst) in enumerate(((tokens_hbm, tokens_ref), (w1_hbm, w1_ref), (w2_hbm, w2_ref)))
    ]
    for load in loads:
        load.start()

    def send(src, dst, peer):
        slot = used[0]
        used[0] += 1
        copy = pltpu.make_async_remote_copy(
            src_ref=src, dst_ref=dst, send_sem=send_sems.at[slot], recv_sem=recv_sems.at[slot],
            device_id=peer, device_id_type=pl.DeviceIdType.MESH,
        )
        copy.start()
        return copy

    def finish(copies):
        for copy in copies:
            copy.wait()

    axes = {
        "core": (2, core, lambda t: {"item": x * 2 + t}),
        "x": (gx, x, lambda t: {"item": t * 2 + core}),
        "y": (2, y, lambda t: {"query": z * 2 + t}),
        "z": (gz, z, lambda t: {"query": t * 2 + y}),
        "zl": (2, zl, lambda t: {"query": (zh * 2 + t) * 2 + y}),
        "zh": (gh, zh, lambda t: {"query": (t * 2 + zl) * 2 + y}),
    }

    def reduce_start(acc, recv, base, size, axis):
        group, own, peer = axes[axis]
        copies = []
        for k in range(1, group):
            there = lax.rem(own + k, group)
            copies.append(
                send(acc.at[rows(base + there * size, size)], recv.at[rows((k - 1) * size, size)], peer(there))
            )
        return copies

    def reduce_finish(copies, acc, recv, base, size, axis):
        group, own, _ = axes[axis]
        finish(copies)
        here = rows(base + own * size, size)
        total = acc[here, :]
        for k in range(1, group):
            total = total + recv[rows((k - 1) * size, size), :]
        acc[here, :] = total
        return base + own * size

    def gather_start(buf, base, size, axis):
        group, own, peer = axes[axis]
        here = buf.at[rows(base + own * size, size)]
        return [send(here, here, peer(lax.rem(own + k, group))) for k in range(1, group)]

    barrier = pltpu.get_barrier_semaphore()
    for k in range(1, nq):
        pl.semaphore_signal(
            barrier, inc=1, device_id={"query": lax.rem(q + k, nq)}, device_id_type=pl.DeviceIdType.MESH
        )
    for k in range(1, ni):
        pl.semaphore_signal(
            barrier, inc=1, device_id={"item": lax.rem(i + k, ni)}, device_id_type=pl.DeviceIdType.MESH
        )
    pl.semaphore_wait(barrier, nq + ni - 2)

    q_pos = (y * 2 + zl) * gh + zh
    query_copies = []
    for k in range(1, nq):
        there = lax.rem(q + k, nq)
        query_copies.append(send(query_ref, q_all.at[rows(q_pos * q_rows, q_rows)], {"query": there}))
    per = 128 // q_rows
    meta_rows = raw_in.shape[1]
    raw_in[i] = jnp.zeros((meta_rows, 128), jnp.int32)
    raw_in[i, 0:ni, 0:nq] = (flags_ref[...] > 0).astype(jnp.int32)
    raw_copies = [send(raw_in.at[i], raw_in.at[i], {"item": lax.rem(i + k, ni)}) for k in range(1, ni)]
    q_all[rows(q_pos * q_rows, q_rows), :] = query_ref[...]
    lane_row = lax.broadcasted_iota(jnp.int32, (1, 128), 1)
    first_lane = pl.multiple_of(lax.div(i, per) * 128, 128)
    found = targets_ref[:, pl.ds(first_lane, 128)]
    shift = lax.rem(q_pos - i + per * nq * ni, per)
    moved = found
    for h in range(1, per):
        moved = jnp.where(shift == h, pltpu.roll(found, h * q_rows, 1), moved)
    inside = lax.div(lane_row, q_rows) == lax.rem(q_pos, per)
    own_targets = jnp.where(inside, moved, 0)
    loads[0].wait()
    loads[1].wait()
    tokens = tokens_ref[...]
    pre = dot(tokens, w1_ref[...], (1, 0))
    pre_act[...] = pre
    finish(raw_copies)
    parts = [raw_in[t, pl.ds(i, 1), :] for t in range(ni)] + [own_targets]
    if meta_rows > ni + 1:
        parts.append(jnp.zeros((meta_rows - ni - 1, 128), jnp.int32))
    meta_in[q_pos] = jnp.concatenate(parts, axis=0)
    for k in range(1, nq):
        query_copies.append(send(meta_in.at[q_pos], meta_in.at[q_pos], {"query": lax.rem(q + k, nq)}))
    loads[2].wait()
    hidden[...] = jax.nn.silu(pre).astype(BF16)
    i_pos = core * gx + x
    emb_all[rows(i_pos * block, block), :] = dot(hidden[...], w2_ref[...], (1, 0)).astype(BF16)

    finish(gather_start(emb_all, core * gx * block, block, "x"))
    finish(gather_start(emb_all, 0, gx * block, "core"))

    finish(query_copies)
    lane = lax.broadcasted_iota(jnp.int32, (meta_rows, 128), 1)
    want_tiles, flag_tiles = [], []
    for t in range(nq // per):
        want = jnp.zeros((1, 128), jnp.int32)
        flag = jnp.zeros((meta_rows, 128), F32)
        for h in range(per):
            sent = meta_in[t * per + h]
            want = want + sent[ni : ni + 1, :]
            column = jnp.sum(jnp.where(lane == q, sent, 0).astype(F32), axis=1, keepdims=True)
            inside = (lane >= h * q_rows) & (lane < (h + 1) * q_rows)
            flag = flag + jnp.where(inside, column, 0.0)
        want_tiles.append(want)
        flag_tiles.append(flag)
    wanted = jnp.concatenate(want_tiles, axis=1)
    flags_all[...] = jnp.concatenate(flag_tiles, axis=1)

    def located(p):
        item = lax.rem(p, gx) * 2 + lax.div(p, gx)
        first = (item * nq + q) * block
        ids = lax.broadcasted_iota(jnp.int32, (block, n_q), 0)
        hit = ids == (wanted - first)
        live = flags_all[pl.ds(item, 1), :] > 0.5
        return hit, live

    def score_block(p, carried):
        top, total, positive = carried
        hit, live = located(p)
        s = 0.25 * dot(emb_all[rows(p * block, block), :], q_all[...], (1, 1))
        scores[rows(p * block, block), :] = s
        here = jnp.max(s, axis=0, keepdims=True)
        added = jnp.sum(jnp.exp(s - here), axis=0, keepdims=True)
        positive = positive + jnp.sum(jnp.where(hit, s, 0.0), axis=0, keepdims=True)
        here = jnp.where(live, here, -1e30)
        new_top = jnp.maximum(top, here)
        total = total * jnp.exp(top - new_top) + jnp.where(live, added * jnp.exp(here - new_top), 0.0)
        return new_top, total, positive

    start = (jnp.full((1, n_q), -1e30, F32), jnp.zeros((1, n_q), F32), jnp.zeros((1, n_q), F32))
    top, total, positive = lax.fori_loop(0, ni, score_block, start)
    stats_all[0] = jnp.concatenate([top, total, positive, jnp.zeros((5, n_q), F32)], axis=0)
    finish([
        send(stats_all.at[0], stats_all.at[k], {"query": lax.rem(q + k, nq)}) for k in range(1, nq)
    ])
    top = stats_all[0, 0:1, :]
    for k in range(1, nq):
        top = jnp.maximum(top, stats_all[k, 0:1, :])
    total = jnp.zeros((1, n_q), F32)
    positive = jnp.zeros((1, n_q), F32)
    for k in range(nq):
        total = total + stats_all[k, 1:2, :] * jnp.exp(stats_all[k, 0:1, :] - top)
        positive = positive + stats_all[k, 2:3, :]
    log_norm = top + jnp.log(total)
    stats_all[0, 0:1, :] = log_norm - positive
    found = stats_all[0, 0:1, pl.ds(pl.multiple_of(lax.div(q_pos, per) * 128, 128), 128)]
    moved = found
    for h in range(1, per):
        moved = jnp.where(lax.rem(q_pos, per) == h, pltpu.roll(found, (per - h) * q_rows, 1), moved)
    loss_ref[...] = moved[:, :q_rows]

    def grad_block(p, carried):
        hit, live = located(p)
        s = scores[rows(p * block, block), :]
        weights = jnp.where(live, jnp.exp(s - log_norm), 0.0)
        c = (weights - hit.astype(F32)).astype(BF16)
        coeffs[rows(p * block, block), :] = c
        e_acc[rows(p * block, block), :] = 0.25 * dot(c, q_all[...], (1, 0))
        return carried

    e_size = gx * block
    pairs = []
    for k in list(range(1, gx)) + [0]:
        t = lax.rem(x + k, gx)
        grad_block((1 - core) * gx + t, 0)
        leaving = rows(((1 - core) * gx + t) * block, block)
        landed = e_recv_c.at[rows(t * block, block)]
        pairs.append(send(e_acc.at[leaving], landed, {"item": x * 2 + 1 - core}))
        grad_block(core * gx + t, 0)
        if k > 0:
            here = rows((core * gx + t) * block, block)
            pairs[-1].wait()
            e_acc[here, :] = e_acc[here, :] + e_recv_c[rows(t * block, block), :]
            pairs[-1] = send(e_acc.at[here], e_recv_x.at[rows((k - 1) * block, block)], {"item": t * 2 + core})
    q_acc[...] = 0.25 * dot(coeffs[...], emb_all[...], (0, 0))
    q_copies = reduce_start(q_acc, q_recv_y, 0, gz * q_rows, "y")
    e_base = (core * gx + x) * block
    pairs[-1].wait()
    e_acc[rows(e_base, block), :] = e_acc[rows(e_base, block), :] + e_recv_c[rows(x * block, block), :]
    e_base = reduce_finish(pairs[:-1], e_acc, e_recv_x, core * gx * block, block, "x")
    own_grad = e_acc[rows(e_base, block), :].astype(BF16)

    hid, din = w2_ref.shape[0], tokens.shape[1]
    part = b_acc.shape[0]
    chains = [
        {"acc": a_acc, "out": a_out, "first": 0, "order": ("core", "x", "y", "z")},
        {"acc": a_acc, "out": a_out, "first": part, "order": ("core", "y", "x", "z")},
        {"acc": b_acc, "out": b_out, "first": 0, "order": ("core", "zl", "zh", "x", "y")},
    ]
    landing = {"core": core_recv, "x": x_recv, "y": y_recv, "zl": l_recv, "zh": h_recv, "z": h_recv}

    def descend(n):
        chain = chains[n]
        level = chain.setdefault("level", 0)
        if level == 0:
            chain["base"], chain["size"] = chain["first"], part
        else:
            chain["base"] = reduce_finish(
                chain["copies"], chain["acc"], landing[chain["order"][level - 1]].at[n],
                chain["base"], chain["size"], chain["order"][level - 1],
            )
        if level < len(chain["order"]):
            axis = chain["order"][level]
            chain["size"] = chain["size"] // axes[axis][0]
            chain["copies"] = reduce_start(
                chain["acc"], landing[axis].at[n], chain["base"], chain["size"], axis
            )
            chain["level"] = level + 1
        else:
            here = rows(chain["base"], chain["size"])
            chain["out"][here, :] = (chain["acc"][here, :] * grad_scale).astype(chain["out"].dtype)
            chain["copies"] = []

    def ascend(n):
        chain = chains[n]
        finish(chain["copies"])
        level = chain["level"] - 1
        chain["level"] = level
        if level < 0:
            return
        group, own, _ = axes[chain["order"][level]]
        chain["base"] = chain["base"] - own * chain["size"]
        chain["copies"] = gather_start(
            chain["out"], chain["base"], chain["size"], chain["order"][level]
        )
        chain["size"] = chain["size"] * group

    second = dot(hidden[...], own_grad, (0, 0))
    for j in range(width // 128):
        b_acc[j * hid : (j + 1) * hid, :] = second[:, j * 128 : (j + 1) * 128]
    descend(2)
    q_base = reduce_finish(q_copies, q_acc, q_recv_y, 0, gz * q_rows, "y")
    q_copies = reduce_start(q_acc, q_recv_l, q_base, gh * q_rows, "zl")
    hid_grad = dot(own_grad, w2_ref[...], (1, 1))
    pre = pre_act[...]
    sig = jax.nn.sigmoid(pre)
    pre_grad = (hid_grad * sig * (1.0 + pre * (1.0 - sig))).astype(BF16)
    half = hid // 2
    for n in range(2):
        first = dot(tokens, pre_grad[:, n * half : (n + 1) * half], (0, 0))
        for j in range(half // 128):
            start_row = n * part + j * din
            a_acc[start_row : start_row + din, :] = first[:, j * 128 : (j + 1) * 128]
        descend(n)
        if n == 0:
            descend(2)
            q_base = reduce_finish(q_copies, q_acc, q_recv_l, q_base, gh * q_rows, "zl")
            q_copies = reduce_start(q_acc, q_recv_h, q_base, q_rows, "zh")
    for n in (0, 1, 2, 0, 1):
        descend(n)
    q_base = reduce_finish(q_copies, q_acc, q_recv_h, q_base, q_rows, "zh")
    qgrad_ref[...] = q_acc[rows(q_base, q_rows), :]
    for n in (0, 1, 2, 2, 2):
        descend(n)
    ascend(2)
    for n in (0, 1):
        descend(n)
        ascend(n)
    for n in (2, 0, 1, 2, 0, 1, 2, 0, 1, 2, 0, 1, 2):
        ascend(n)


def on_device(query_emb, targets, eligible_tiles, item_feats, w_first, w_second):
    q_rows, width = query_emb.shape
    ni, nq = lax.axis_size("item"), lax.axis_size("query")
    gx, gz = ni // 2, nq // 2
    tokens = item_feats.reshape(item_feats.shape[1], item_feats.shape[2])
    block, din = tokens.shape
    hid = w_first.shape[1]
    n_q = nq * q_rows
    meta_rows = -(-(ni + 1) // 8) * 8
    a_rows, b_rows = din * hid // 128, hid * width // 128
    part = b_rows
    out_dtype = BF16 if part // (nq * ni) % 16 == 0 else F32
    n_copies = 3 * (nq - 1) + (ni - 1) + 2 * gx + gx + gz + 3 * 2 * (3 + gx - 1 + gz - 1)
    vmem = pltpu.VMEM
    loss, query_grad, g1, g2 = pl.pallas_call(
        functools.partial(window_kernel, (nq, ni, 1.0 / math.sqrt(block * nq * ni))),
        out_shape=(
            jax.ShapeDtypeStruct((1, q_rows), F32),
            jax.ShapeDtypeStruct((q_rows, width), F32),
            jax.ShapeDtypeStruct((a_rows, 128), out_dtype),
            jax.ShapeDtypeStruct((b_rows, 128), out_dtype),
        ),
        in_specs=[pl.BlockSpec(memory_space=vmem)] * 3 + [pl.BlockSpec(memory_space=pl.ANY)] * 3,
        out_specs=(pl.BlockSpec(memory_space=vmem),) * 4,
        scratch_shapes=[
            vmem((block, din), BF16),
            vmem((din, hid), BF16),
            vmem((hid, width), BF16),
            vmem((n_q, width), BF16),
            vmem((ni, meta_rows, 128), jnp.int32),
            vmem((nq, meta_rows, 128), jnp.int32),
            vmem((ni * block, width), BF16),
            vmem((meta_rows, n_q), F32),
            vmem((ni * block, n_q), F32),
            vmem((ni * block, n_q), BF16),
            vmem((nq, 8, n_q), F32),
            vmem((ni * block, width), F32),
            vmem((gx * block, width), F32),
            vmem((max(gx - 1, 1) * block, width), F32),
            vmem((n_q, width), F32),
            vmem((gz * q_rows, width), F32),
            vmem((gz // 2 * q_rows, width), F32),
            vmem((max(gz // 2 - 1, 1) * q_rows, width), F32),
            vmem((block, hid), F32),
            vmem((block, hid), BF16),
            vmem((a_rows, 128), F32),
            vmem((b_rows, 128), F32),
            vmem((3, part // 2, 128), F32),
            vmem((3, part // 2, 128), F32),
            vmem((3, part // 4, 128), F32),
            vmem((3, part // 4, 128), F32),
            vmem((3, part // 4, 128), F32),
            pltpu.SemaphoreType.DMA((n_copies,)),
            pltpu.SemaphoreType.DMA((n_copies,)),
            pltpu.SemaphoreType.DMA((3,)),
        ],
        compiler_params=pltpu.CompilerParams(
            collective_id=0, has_side_effects=True, vmem_limit_bytes=58 * 2**20
        ),
        name="loss_window",
    )(query_emb, targets.reshape(1, -1), eligible_tiles, tokens, w_first, w_second)
    loss = loss.reshape(q_rows)
    g1 = g1.reshape(hid // 128, din, 128).transpose(1, 0, 2).reshape(din, hid).astype(F32)
    g2 = g2.reshape(width // 128, hid, 128).transpose(1, 0, 2).reshape(hid, width).astype(F32)
    return (loss, query_grad, g1, g2)

def small_kernel(
    grad_scale,
    query_hbm, targets_hbm, flags_hbm, tokens_hbm, w1_hbm, w2_hbm,
    loss_out, qgrad_out, a_out, b_out,
    targets_ref, flags_ref, loss_ref, qgrad_ref, tokens_all, w1_ref, w2_ref, q_all, raw_in, meta_in, emb_all, flags_all, scores, coeffs, stats_all,
    tops, e_acc, e_recv_c, e_send, e_recv_x, grad_all, q_acc, q_send, q_recv,
    hidden, slope, hid_cols, a_acc, b_acc, a_send, b_send, a_recv, b_recv_y, b_half, b_part, b_recv, a_all, b_all,
    send_sems, recv_sems, load_sems,
):
    nq, ni, gx, gy, gz = 8, 4, 2, 2, 4
    q, i = lax.axis_index("query"), lax.axis_index("item")
    core, x = lax.rem(i, 2), lax.div(i, 2)
    y, z = lax.rem(q, 2), lax.div(q, 2)
    q_rows, width = query_hbm.shape
    n_q = nq * q_rows
    block = tokens_hbm.shape[0]
    hid = w2_ref.shape[0]
    cols = hid // ni
    i_pos = core * gx + x
    used = [0]
    started = []

    def send(src, dst, peer):
        slot = used[0]
        used[0] += 1
        copy = pltpu.make_async_remote_copy(
            src_ref=src, dst_ref=dst, send_sem=send_sems.at[slot], recv_sem=recv_sems.at[slot],
            device_id=peer, device_id_type=pl.DeviceIdType.MESH,
        )
        copy.start()
        started.append(copy)
        return copy

    def arrived(copies):
        for copy in copies:
            copy.wait_recv()

    def ring(k):
        return {"query": lax.rem(q + k, nq)}

    def device(c_, x_, y_, z_):
        return {"query": z_ * 2 + y_, "item": x_ * 2 + c_}

    on_core = device(1 - core, x, y, z)
    on_x = device(core, 1 - x, y, z)
    on_cx = device(1 - core, 1 - x, y, z)
    on_y = device(core, x, 1 - y, z)
    on_xy = device(core, 1 - x, 1 - y, z)

    barrier = pltpu.get_barrier_semaphore()
    greeted = [ring(k) for k in range(1, nq)] + [on_core, on_x, on_cx, on_xy]
    for peer in greeted:
        pl.semaphore_signal(barrier, inc=1, device_id=peer, device_id_type=pl.DeviceIdType.MESH)

    loads = [
        pltpu.make_async_copy(src, dst, load_sems.at[n])
        for n, (src, dst) in enumerate((
            (query_hbm, q_all.at[rows(q * q_rows, q_rows)]), (targets_hbm, targets_ref), (flags_hbm, flags_ref),
            (tokens_hbm, tokens_all.at[rows(i_pos * block, block)]), (w1_hbm, w1_ref), (w2_hbm, w2_ref),
        ))
    ]
    for load in loads:
        load.start()

    for load in loads[:3]:
        load.wait()
    per = 128 // q_rows
    meta_rows = raw_in.shape[1]
    raw_in[i] = jnp.zeros((meta_rows, 128), jnp.int32)
    raw_in[i, 0:ni, 0:nq] = (flags_ref[...] > 0).astype(jnp.int32)
    lane_row = lax.broadcasted_iota(jnp.int32, (1, 128), 1)
    first_lane = pl.multiple_of(lax.div(i, per) * 128, 128)
    found = targets_ref[:, pl.ds(first_lane, 128)]
    shift = lax.rem(q - i + per * nq * ni, per)
    moved = found
    for h in range(1, per):
        moved = jnp.where(shift == h, pltpu.roll(found, h * q_rows, 1), moved)
    inside = lax.div(lane_row, q_rows) == lax.rem(q, per)
    own_targets = jnp.where(inside, moved, 0)

    pl.semaphore_wait(barrier, len(greeted))

    raw_copies = [send(raw_in.at[i], raw_in.at[i], peer) for peer in (on_x, on_cx, on_core)]
    emb_own = emb_all.at[rows(i_pos * block, block)]
    own_queries = q_all.at[rows(q * q_rows, q_rows)]
    query_copies = [send(own_queries, own_queries, ring(k)) for k in (4, 3, 5, 2, 6, 1, 7)]
    loads[3].wait()
    loads[4].wait()
    pre = dot(tokens_all[rows(i_pos * block, block), :], w1_ref[...], (1, 0))
    hidden[...] = jax.nn.silu(pre).astype(BF16)
    loads[5].wait()
    emb_all[rows(i_pos * block, block), :] = dot(hidden[...], w2_ref[...], (1, 0)).astype(BF16)
    emb_x = send(emb_own, emb_own, on_x)
    emb_c = send(emb_own, emb_own, on_core)
    arrived(raw_copies)
    parts = [raw_in[t, pl.ds(i, 1), :] for t in range(ni)] + [own_targets]
    parts.append(jnp.zeros((meta_rows - ni - 1, 128), jnp.int32))
    meta_in[q] = jnp.concatenate(parts, axis=0)
    meta_copies = [send(meta_in.at[q], meta_in.at[q], ring(k)) for k in (4, 3, 5, 2, 6, 1, 7)]
    emb_x.wait_recv()
    emb_far = emb_all.at[rows((core * gx + 1 - x) * block, block)]
    emb_f = send(emb_far, emb_far, on_core)
    tok_own = tokens_all.at[rows(i_pos * block, block)]
    tok_x = send(tok_own, tok_own, on_x)
    tok_c = send(tok_own, tok_own, on_core)

    arrived(meta_copies)
    lane = lax.broadcasted_iota(jnp.int32, (meta_rows, 128), 1)
    want_tiles, flag_tiles = [], []
    for t in range(nq // per):
        want = jnp.zeros((1, 128), jnp.int32)
        flag = jnp.zeros((meta_rows, 128), F32)
        for h in range(per):
            sent = meta_in[t * per + h]
            want = want + sent[ni : ni + 1, :]
            column = jnp.sum(jnp.where(lane == q, sent, 0).astype(F32), axis=1, keepdims=True)
            inside = (lane >= h * q_rows) & (lane < (h + 1) * q_rows)
            flag = flag + jnp.where(inside, column, 0.0)
        want_tiles.append(want)
        flag_tiles.append(flag)
    wanted = jnp.concatenate(want_tiles, axis=1)
    flags_all[...] = jnp.concatenate(flag_tiles, axis=1)

    def located(p):
        item = lax.rem(p, gx) * 2 + lax.div(p, gx)
        first = (item * nq + q) * block
        ids = lax.broadcasted_iota(jnp.int32, (block, n_q), 0)
        hit = ids == (wanted - first)
        live = flags_all[pl.ds(item, 1), :] > 0.5
        return hit, live

    def score_block(p, carried):
        top, total, positive = carried
        hit, live = located(p)
        s = 0.25 * dot(emb_all[rows(p * block, block), :], q_all[...], (1, 1))
        here = jnp.max(s, axis=0, keepdims=True)
        e = jnp.exp(s - here)
        scores[rows(p * block, block), :] = e
        added = jnp.sum(e, axis=0, keepdims=True)
        positive = positive + jnp.sum(jnp.where(hit, s, 0.0), axis=0, keepdims=True)
        here = jnp.where(live, here, -1e30)
        tops[pl.ds(p, 1), :] = here
        new_top = jnp.maximum(top, here)
        total = total * jnp.exp(top - new_top) + jnp.where(live, added * jnp.exp(here - new_top), 0.0)
        return new_top, total, positive

    arrived(query_copies)
    carried = (jnp.full((1, n_q), -1e30, F32), jnp.zeros((1, n_q), F32), jnp.zeros((1, n_q), F32))
    carried = score_block(i_pos, carried)
    carried = score_block(core * gx + 1 - x, carried)
    emb_c.wait_recv()
    carried = score_block((1 - core) * gx + x, carried)
    emb_f.wait_recv()
    carried = score_block((1 - core) * gx + 1 - x, carried)
    top, total, positive = carried
    part_norm = jnp.where(total > 0.0, top + jnp.log(jnp.maximum(total, 1e-30)), -1e30)
    tiles = n_q // 128

    def stacked(row):
        return [row[:, t * 128 : (t + 1) * 128] for t in range(tiles)]

    stats_all[0] = jnp.concatenate(stacked(part_norm) + stacked(positive), axis=0)
    stats_copies = [send(stats_all.at[0], stats_all.at[k], ring(k)) for k in (4, 3, 5, 2, 6, 1, 7)]
    my_cols = pl.ds(pl.multiple_of(i * cols, 128), cols)

    def forward_cols(p):
        part = rows(p * block, block)
        pre = dot(tokens_all[part, :], w1_ref[:, my_cols], (1, 0))
        sig = jax.nn.sigmoid(pre)
        hid_cols[part, :] = (pre * sig).astype(BF16)
        slope[part, :] = sig * (1.0 + pre * (1.0 - sig))

    w2_cols = w2_ref[rows(i * cols, cols), :]
    forward_cols(i_pos)
    tok_c.wait_recv()
    forward_cols((1 - core) * gx + x)
    arrived(stats_copies)
    top = stats_all[0, 0:tiles, :]
    positive = stats_all[0, tiles:, :]
    for k in range(1, nq):
        top = jnp.maximum(top, stats_all[k, 0:tiles, :])
        positive = positive + stats_all[k, tiles:, :]
    total = jnp.zeros((tiles, 128), F32)
    for k in range(nq):
        total = total + jnp.exp(stats_all[k, 0:tiles, :] - top)
    norm_tiles = top + jnp.log(total)
    log_norm = jnp.concatenate([norm_tiles[t : t + 1, :] for t in range(tiles)], axis=1)
    def grad_block(p):
        hit, _ = located(p)
        factor = jnp.exp(tops[pl.ds(p, 1), :] - log_norm)
        c = (scores[rows(p * block, block), :] * factor - hit.astype(F32)).astype(BF16)
        coeffs[rows(p * block, block), :] = c
        e_acc[rows(p * block, block), :] = 0.25 * dot(c, q_all[...], (1, 0))

    crossing = []
    for t in range(gx):
        p = (1 - core) * gx + t
        slot = rows(t * block, block)
        grad_block(p)
        pair = send(e_acc.at[rows(p * block, block)], e_recv_c.at[slot], on_core)
        grad_block(core * gx + t)
        here = rows((core * gx + t) * block, block)
        pair.wait_recv()
        part = e_acc[here, :] + e_recv_c[slot, :]
        e_acc[here, :] = part
        e_send[slot, :] = part.astype(BF16)
        crossing.append(send(e_send.at[slot], e_recv_x.at[slot], on_x))
    q_acc[...] = 0.25 * dot(coeffs[...], emb_all[...], (0, 0))
    q_send[...] = q_acc[...].astype(BF16)
    q_copies = [
        send(
            q_send.at[rows(lax.rem(q + k, nq) * q_rows, q_rows)],
            q_recv.at[rows((k - 1) * q_rows, q_rows)], ring(k),
        )
        for k in (4, 3, 5, 2, 6, 1, 7)
    ]
    tok_x.wait_recv()
    tok_far = tokens_all.at[rows((core * gx + 1 - x) * block, block)]
    tok_f = send(tok_far, tok_far, on_core)
    forward_cols(core * gx + 1 - x)
    losses = norm_tiles - positive
    found = jnp.zeros((1, 128), F32)
    for t in range(tiles):
        found = found + jnp.where(lax.div(q, per) == t, losses[t : t + 1, :], 0.0)
    moved = found
    for h in range(1, per):
        moved = jnp.where(lax.rem(q, per) == h, pltpu.roll(found, (per - h) * q_rows, 1), moved)
    loss_ref[...] = moved[:, :q_rows]

    tok_f.wait_recv()
    forward_cols((1 - core) * gx + 1 - x)

    def tower_b(p, first):
        part = rows(p * block, block)
        b = dot(hid_cols[part, :], grad_all[part, :], (0, 0))
        b = b.reshape(b_acc.shape)
        b_acc[...] = b if first else b_acc[...] + b

    def tower_a(p, first):
        part = rows(p * block, block)
        pre_grad = (dot(grad_all[part, :], w2_cols, (1, 1)) * slope[part, :]).astype(BF16)
        a = dot(tokens_all[part, :], pre_grad, (0, 0))
        a_acc[...] = a if first else a_acc[...] + a

    for t in range(gx):
        mine, theirs = core * gx + t, (1 - core) * gx + t
        here = rows(mine * block, block)
        crossing[t].wait_recv()
        grad_all[here, :] = (e_acc[here, :] + e_recv_x[rows(t * block, block), :].astype(F32)).astype(BF16)
        over = send(grad_all.at[here], grad_all.at[here], on_core)
        tower_b(mine, t == 0)
        tower_a(mine, t == 0)
        over.wait_recv()
        tower_b(theirs, False)
        if t == gx - 1:
            b_send[...] = b_acc[...].astype(BF16)
            b_y = send(b_send.at[:, 1 - y], b_recv_y, on_y)
        tower_a(theirs, False)
    a_rows = a_acc.shape[0] // nq
    a_send[...] = a_acc[...].astype(BF16)
    a_copies = [
        send(
            a_send.at[rows(lax.rem(q + k, nq) * a_rows, a_rows)],
            a_recv.at[rows((k - 1) * a_rows, a_rows)], ring(k),
        )
        for k in (4, 3, 5, 2, 6, 1, 7)
    ]

    b_y.wait_recv()
    b_half[...] = b_acc[:, y] + b_recv_y[...].astype(F32)
    b_part[...] = b_half[...].astype(BF16)
    b_copies = [
        send(b_part.at[lax.rem(z + k, gz)], b_recv.at[k - 1], device(core, x, y, lax.rem(z + k, gz)))
        for k in (2, 1, 3)
    ]
    arrived(q_copies)
    total = q_acc[rows(q * q_rows, q_rows), :]
    for k in range(1, nq):
        total = total + q_recv[rows((k - 1) * q_rows, q_rows), :].astype(F32)
    qgrad_ref[...] = total
    outs = [pltpu.make_async_copy(loss_ref, loss_out, load_sems.at[14]), pltpu.make_async_copy(qgrad_ref, qgrad_out, load_sems.at[15])]
    for copy in outs:
        copy.start()
    kept = []

    def leave(out, x_, y_):
        whole = {id(a_all): a_out, id(b_all): b_out}[id(out)].at[x_, core, :, y_]
        copy = pltpu.make_async_copy(out.at[x_, :, y_], whole, load_sems.at[6 + len(kept)])
        copy.start()
        kept.append(copy)
        return send(out.at[x_, :, y_], whole, on_core)

    def gather_own(copies, parts, out):
        arrived(copies)
        total = parts()
        out[x, z, y] = (total * grad_scale).astype(BF16)
        own = out.at[x, z, y]
        up = [send(own, own, device(core, x, y, lax.rem(z + k, gz))) for k in (2, 1, 3)]
        over = [[send(own, own, peer) for peer in (on_xy, on_x, on_y)]]
        return up, over

    def gather_far(up, over, out):
        for n, k in enumerate((2, 1, 3)):
            up[n].wait_recv()
            far = out.at[x, lax.rem(z - k + gz, gz), y]
            over.append([send(far, far, peer) for peer in (on_xy, on_x, on_y)])
        return [leave(out, x, y)]

    def gather_core(over, out):
        crossed = []
        for n, (x_, y_) in ((1, (1 - x, y)), (2, (x, 1 - y)), (0, (1 - x, 1 - y))):
            arrived([four[n] for four in over])
            crossed.append(leave(out, x_, y_))
        return crossed

    def a_total():
        total = a_acc[rows(q * a_rows, a_rows), :]
        for k in range(1, nq):
            total = total + a_recv[rows((k - 1) * a_rows, a_rows), :].astype(F32)
        return total

    def b_total():
        total = b_half[z]
        for k in range(1, gz):
            total = total + b_recv[k - 1].astype(F32)
        return total

    a_up, a_over = gather_own(a_copies, a_total, a_all)
    b_up, b_over = gather_own(b_copies, b_total, b_all)
    crossed = gather_far(a_up, a_over, a_all)
    crossed += gather_far(b_up, b_over, b_all)
    crossed += gather_core(a_over, a_all)
    crossed += gather_core(b_over, b_all)
    arrived(crossed)
    for copy in kept + outs:
        copy.wait()
    for copy in started:
        copy.wait_send()


def finish_kernel(loss_in, qgrad_in, a_in, b_in, loss_ref, qgrad_ref, a_ref, b_ref):
    loss_ref[...] = loss_in[...]
    qgrad_ref[...] = qgrad_in[...]
    for t in range(a_in.shape[0]):
        for r in range(a_in.shape[1]):
            size, cols = a_in.shape[2], a_in.shape[3]
            a_ref[r * size : (r + 1) * size, t * cols : (t + 1) * cols] = a_in[t, r].astype(F32)
    b_ref[...] = b_in[...].astype(F32)


def on_device_small(query_emb, targets, eligible_tiles, item_feats, w_first, w_second):
    q_rows, width = query_emb.shape
    ni, nq = lax.axis_size("item"), lax.axis_size("query")
    tokens = item_feats.reshape(item_feats.shape[1], item_feats.shape[2])
    block, din = tokens.shape
    hid = w_first.shape[1]
    n_q, items, cols = nq * q_rows, ni * block, hid // ni
    a_rows, b_rows = din // nq, cols // nq
    vmem = pltpu.VMEM
    out = (2, 2, nq // 2, 2)
    loss, query_grad, g1, g2 = pl.pallas_call(
        functools.partial(small_kernel, 1.0 / math.sqrt(items * nq)),
        out_shape=(
            jax.ShapeDtypeStruct((1, q_rows), F32),
            jax.ShapeDtypeStruct((q_rows, width), F32),
            jax.ShapeDtypeStruct(out + (a_rows, cols), BF16),
            jax.ShapeDtypeStruct(out + (b_rows, width), BF16),
        ),
        in_specs=[pl.BlockSpec(memory_space=pl.ANY)] * 6,
        out_specs=(pl.BlockSpec(memory_space=pl.ANY),) * 4,
        scratch_shapes=[
            vmem((1, targets.shape[0]), jnp.int32),
            vmem(eligible_tiles.shape, jnp.int32),
            vmem((1, q_rows), F32),
            vmem((q_rows, width), F32),
            vmem((items, din), BF16),
            vmem((din, hid), BF16),
            vmem((hid, width), BF16),
            vmem((n_q, width), BF16),
            vmem((ni, 8, 128), jnp.int32),
            vmem((nq, 8, 128), jnp.int32),
            vmem((items, width), BF16),
            vmem((8, n_q), F32),
            vmem((items, n_q), F32),
            vmem((items, n_q), BF16),
            vmem((nq, 2 * n_q // 128, 128), F32),
            vmem((8, n_q), F32),
            vmem((items, width), F32),
            vmem((2 * block, width), F32),
            vmem((2 * block, width), BF16),
            vmem((2 * block, width), BF16),
            vmem((items, width), BF16),
            vmem((n_q, width), F32),
            vmem((n_q, width), BF16),
            vmem(((nq - 1) * q_rows, width), BF16),
            vmem((block, hid), BF16),
            vmem((items, cols), F32),
            vmem((items, cols), BF16),
            vmem((din, cols), F32),
            vmem((nq // 2, 2, b_rows, width), F32),
            vmem((din, cols), BF16),
            vmem((nq // 2, 2, b_rows, width), BF16),
            vmem(((nq - 1) * a_rows, cols), BF16),
            vmem((nq // 2, b_rows, width), BF16),
            vmem((nq // 2, b_rows, width), F32),
            vmem((nq // 2, b_rows, width), BF16),
            vmem((nq // 2 - 1, b_rows, width), BF16),
            vmem((2, nq // 2, 2, a_rows, cols), BF16),
            vmem((2, nq // 2, 2, b_rows, width), BF16),
            pltpu.SemaphoreType.DMA((112,)),
            pltpu.SemaphoreType.DMA((112,)),
            pltpu.SemaphoreType.DMA((16,)),
        ],
        compiler_params=pltpu.CompilerParams(
            collective_id=0, has_side_effects=True, vmem_limit_bytes=58 * 2**20
        ),
        name="loss_window",
    )(query_emb, targets.reshape(1, -1), eligible_tiles, tokens, w_first, w_second)
    steps = 2
    loss, query_grad, g1, g2 = pl.pallas_call(
        finish_kernel,
        grid=(steps,),
        out_shape=(
            jax.ShapeDtypeStruct((1, q_rows), F32),
            jax.ShapeDtypeStruct((q_rows, width), F32),
            jax.ShapeDtypeStruct((din, hid), F32),
            jax.ShapeDtypeStruct((ni, nq, b_rows, width), F32),
        ),
        in_specs=[
            pl.BlockSpec((1, q_rows), lambda n: (0, 0)),
            pl.BlockSpec((q_rows // steps, width), lambda n: (n, 0)),
            pl.BlockSpec((ni, nq // steps, a_rows, cols), lambda n: (0, n, 0, 0)),
            pl.BlockSpec((ni, nq // steps, b_rows, width), lambda n: (0, n, 0, 0)),
        ],
        out_specs=(
            pl.BlockSpec((1, q_rows), lambda n: (0, 0)),
            pl.BlockSpec((q_rows // steps, width), lambda n: (n, 0)),
            pl.BlockSpec((din // steps, hid), lambda n: (n, 0)),
            pl.BlockSpec((ni, nq // steps, b_rows, width), lambda n: (0, n, 0, 0)),
        ),
        name="widen",
    )(loss, query_grad, g1.reshape(ni, nq, a_rows, cols), g2.reshape(ni, nq, b_rows, width))
    return loss.reshape(q_rows), query_grad, g1, g2.reshape(hid, width)


def solution(mesh):
    small = mesh.shape["query"] == 8 and mesh.shape["item"] == 4
    return jax.shard_map(
        on_device_small if small else on_device,
        mesh=mesh,
        in_specs=(
            P(("query", "item"), None),
            P("query"),
            P("query", "item"),
            P("item", "query", None),
            P(),
            P(),
        ),
        out_specs=(P(("query", "item")), P(("query", "item"), None), P(), P()),
        check_vma=False,
    )
```

```python
import functools
import math

import jax
import jax.numpy as jnp
from jax import lax
from jax.experimental import pallas as pl
from jax.experimental.pallas import tpu as pltpu
from jax.sharding import PartitionSpec as P

F32 = jnp.float32
BF16 = jnp.bfloat16


def dot(a, b, contract):
    return lax.dot_general(a, b, ((contract[:1], contract[1:]), ((), ())), preferred_element_type=F32)


def rows(start, size):
    return pl.ds(pl.multiple_of(start, math.gcd(size, 256)), size)


def window_kernel(
    shape,
    query_ref, targets_ref, flags_ref, tokens_hbm, w1_hbm, w2_hbm,
    loss_ref, qgrad_ref, a_out, b_out,
    tokens_ref, w1_ref, w2_ref, q_all, raw_in, meta_in, emb_all, flags_all, scores, coeffs, stats_all,
    e_acc, e_recv_c, e_recv_x, q_acc, q_recv_y, q_recv_l, q_recv_h,
    pre_act, hidden, a_acc, b_acc, core_recv, x_recv, y_recv, l_recv, h_recv,
    send_sems, recv_sems, load_sems,
):
    nq, ni, grad_scale = shape
    gx, gz = ni // 2, nq // 2
    q, i = lax.axis_index("query"), lax.axis_index("item")
    core, x = lax.rem(i, 2), lax.div(i, 2)
    y, z = lax.rem(q, 2), lax.div(q, 2)
    zl, zh = lax.rem(z, 2), lax.div(z, 2)
    gh = gz // 2
    q_rows, width = query_ref.shape
    n_q = nq * q_rows
    block = tokens_ref.shape[0]
    used = [0]
    loads = [
        pltpu.make_async_copy(src, dst, load_sems.at[n])
        for n, (src, dst) in enumerate(((tokens_hbm, tokens_ref), (w1_hbm, w1_ref), (w2_hbm, w2_ref)))
    ]
    for load in loads:
        load.start()

    def send(src, dst, peer):
        slot = used[0]
        used[0] += 1
        copy = pltpu.make_async_remote_copy(
            src_ref=src, dst_ref=dst, send_sem=send_sems.at[slot], recv_sem=recv_sems.at[slot],
            device_id=peer, device_id_type=pl.DeviceIdType.MESH,
        )
        copy.start()
        return copy

    def finish(copies):
        for copy in copies:
            copy.wait()

    axes = {
        "core": (2, core, lambda t: {"item": x * 2 + t}),
        "x": (gx, x, lambda t: {"item": t * 2 + core}),
        "y": (2, y, lambda t: {"query": z * 2 + t}),
        "z": (gz, z, lambda t: {"query": t * 2 + y}),
        "zl": (2, zl, lambda t: {"query": (zh * 2 + t) * 2 + y}),
        "zh": (gh, zh, lambda t: {"query": (t * 2 + zl) * 2 + y}),
    }

    def reduce_start(acc, recv, base, size, axis):
        group, own, peer = axes[axis]
        copies = []
        for k in range(1, group):
            there = lax.rem(own + k, group)
            copies.append(
                send(acc.at[rows(base + there * size, size)], recv.at[rows((k - 1) * size, size)], peer(there))
            )
        return copies

    def reduce_finish(copies, acc, recv, base, size, axis):
        group, own, _ = axes[axis]
        finish(copies)
        here = rows(base + own * size, size)
        total = acc[here, :]
        for k in range(1, group):
            total = total + recv[rows((k - 1) * size, size), :]
        acc[here, :] = total
        return base + own * size

    def gather_start(buf, base, size, axis):
        group, own, peer = axes[axis]
        here = buf.at[rows(base + own * size, size)]
        return [send(here, here, peer(lax.rem(own + k, group))) for k in range(1, group)]

    barrier = pltpu.get_barrier_semaphore()
    for k in range(1, nq):
        pl.semaphore_signal(
            barrier, inc=1, device_id={"query": lax.rem(q + k, nq)}, device_id_type=pl.DeviceIdType.MESH
        )
    for k in range(1, ni):
        pl.semaphore_signal(
            barrier, inc=1, device_id={"item": lax.rem(i + k, ni)}, device_id_type=pl.DeviceIdType.MESH
        )
    pl.semaphore_wait(barrier, nq + ni - 2)

    q_pos = (y * 2 + zl) * gh + zh
    query_copies = []
    for k in range(1, nq):
        there = lax.rem(q + k, nq)
        query_copies.append(send(query_ref, q_all.at[rows(q_pos * q_rows, q_rows)], {"query": there}))
    per = 128 // q_rows
    meta_rows = raw_in.shape[1]
    raw_in[i] = jnp.zeros((meta_rows, 128), jnp.int32)
    raw_in[i, 0:ni, 0:nq] = (flags_ref[...] > 0).astype(jnp.int32)
    raw_copies = [send(raw_in.at[i], raw_in.at[i], {"item": lax.rem(i + k, ni)}) for k in range(1, ni)]
    q_all[rows(q_pos * q_rows, q_rows), :] = query_ref[...]
    lane_row = lax.broadcasted_iota(jnp.int32, (1, 128), 1)
    first_lane = pl.multiple_of(lax.div(i, per) * 128, 128)
    found = targets_ref[:, pl.ds(first_lane, 128)]
    shift = lax.rem(q_pos - i + per * nq * ni, per)
    moved = found
    for h in range(1, per):
        moved = jnp.where(shift == h, pltpu.roll(found, h * q_rows, 1), moved)
    inside = lax.div(lane_row, q_rows) == lax.rem(q_pos, per)
    own_targets = jnp.where(inside, moved, 0)
    loads[0].wait()
    loads[1].wait()
    tokens = tokens_ref[...]
    pre = dot(tokens, w1_ref[...], (1, 0))
    pre_act[...] = pre
    finish(raw_copies)
    parts = [raw_in[t, pl.ds(i, 1), :] for t in range(ni)] + [own_targets]
    if meta_rows > ni + 1:
        parts.append(jnp.zeros((meta_rows - ni - 1, 128), jnp.int32))
    meta_in[q_pos] = jnp.concatenate(parts, axis=0)
    for k in range(1, nq):
        query_copies.append(send(meta_in.at[q_pos], meta_in.at[q_pos], {"query": lax.rem(q + k, nq)}))
    loads[2].wait()
    hidden[...] = jax.nn.silu(pre).astype(BF16)
    i_pos = core * gx + x
    emb_all[rows(i_pos * block, block), :] = dot(hidden[...], w2_ref[...], (1, 0)).astype(BF16)

    finish(gather_start(emb_all, core * gx * block, block, "x"))
    finish(gather_start(emb_all, 0, gx * block, "core"))

    finish(query_copies)
    lane = lax.broadcasted_iota(jnp.int32, (meta_rows, 128), 1)
    want_tiles, flag_tiles = [], []
    for t in range(nq // per):
        want = jnp.zeros((1, 128), jnp.int32)
        flag = jnp.zeros((meta_rows, 128), F32)
        for h in range(per):
            sent = meta_in[t * per + h]
            want = want + sent[ni : ni + 1, :]
            column = jnp.sum(jnp.where(lane == q, sent, 0).astype(F32), axis=1, keepdims=True)
            inside = (lane >= h * q_rows) & (lane < (h + 1) * q_rows)
            flag = flag + jnp.where(inside, column, 0.0)
        want_tiles.append(want)
        flag_tiles.append(flag)
    wanted = jnp.concatenate(want_tiles, axis=1)
    flags_all[...] = jnp.concatenate(flag_tiles, axis=1)

    def located(p):
        item = lax.rem(p, gx) * 2 + lax.div(p, gx)
        first = (item * nq + q) * block
        ids = lax.broadcasted_iota(jnp.int32, (block, n_q), 0)
        hit = ids == (wanted - first)
        live = flags_all[pl.ds(item, 1), :] > 0.5
        return hit, live

    def score_block(p, carried):
        top, total, positive = carried
        hit, live = located(p)
        s = 0.25 * dot(emb_all[rows(p * block, block), :], q_all[...], (1, 1))
        scores[rows(p * block, block), :] = s
        here = jnp.max(s, axis=0, keepdims=True)
        added = jnp.sum(jnp.exp(s - here), axis=0, keepdims=True)
        positive = positive + jnp.sum(jnp.where(hit, s, 0.0), axis=0, keepdims=True)
        here = jnp.where(live, here, -1e30)
        new_top = jnp.maximum(top, here)
        total = total * jnp.exp(top - new_top) + jnp.where(live, added * jnp.exp(here - new_top), 0.0)
        return new_top, total, positive

    start = (jnp.full((1, n_q), -1e30, F32), jnp.zeros((1, n_q), F32), jnp.zeros((1, n_q), F32))
    top, total, positive = lax.fori_loop(0, ni, score_block, start)
    stats_all[0] = jnp.concatenate([top, total, positive, jnp.zeros((5, n_q), F32)], axis=0)
    finish([
        send(stats_all.at[0], stats_all.at[k], {"query": lax.rem(q + k, nq)}) for k in range(1, nq)
    ])
    top = stats_all[0, 0:1, :]
    for k in range(1, nq):
        top = jnp.maximum(top, stats_all[k, 0:1, :])
    total = jnp.zeros((1, n_q), F32)
    positive = jnp.zeros((1, n_q), F32)
    for k in range(nq):
        total = total + stats_all[k, 1:2, :] * jnp.exp(stats_all[k, 0:1, :] - top)
        positive = positive + stats_all[k, 2:3, :]
    log_norm = top + jnp.log(total)
    stats_all[0, 0:1, :] = log_norm - positive
    found = stats_all[0, 0:1, pl.ds(pl.multiple_of(lax.div(q_pos, per) * 128, 128), 128)]
    moved = found
    for h in range(1, per):
        moved = jnp.where(lax.rem(q_pos, per) == h, pltpu.roll(found, (per - h) * q_rows, 1), moved)
    loss_ref[...] = moved[:, :q_rows]

    def grad_block(p, carried):
        hit, live = located(p)
        s = scores[rows(p * block, block), :]
        weights = jnp.where(live, jnp.exp(s - log_norm), 0.0)
        c = (weights - hit.astype(F32)).astype(BF16)
        coeffs[rows(p * block, block), :] = c
        e_acc[rows(p * block, block), :] = 0.25 * dot(c, q_all[...], (1, 0))
        return carried

    e_size = gx * block
    pairs = []
    for k in list(range(1, gx)) + [0]:
        t = lax.rem(x + k, gx)
        grad_block((1 - core) * gx + t, 0)
        leaving = rows(((1 - core) * gx + t) * block, block)
        landed = e_recv_c.at[rows(t * block, block)]
        pairs.append(send(e_acc.at[leaving], landed, {"item": x * 2 + 1 - core}))
        grad_block(core * gx + t, 0)
        if k > 0:
            here = rows((core * gx + t) * block, block)
            pairs[-1].wait()
            e_acc[here, :] = e_acc[here, :] + e_recv_c[rows(t * block, block), :]
            pairs[-1] = send(e_acc.at[here], e_recv_x.at[rows((k - 1) * block, block)], {"item": t * 2 + core})
    q_acc[...] = 0.25 * dot(coeffs[...], emb_all[...], (0, 0))
    q_copies = reduce_start(q_acc, q_recv_y, 0, gz * q_rows, "y")
    e_base = (core * gx + x) * block
    pairs[-1].wait()
    e_acc[rows(e_base, block), :] = e_acc[rows(e_base, block), :] + e_recv_c[rows(x * block, block), :]
    e_base = reduce_finish(pairs[:-1], e_acc, e_recv_x, core * gx * block, block, "x")
    own_grad = e_acc[rows(e_base, block), :].astype(BF16)

    hid, din = w2_ref.shape[0], tokens.shape[1]
    part = b_acc.shape[0]
    chains = [
        {"acc": a_acc, "out": a_out, "first": 0, "order": ("core", "x", "y", "z")},
        {"acc": a_acc, "out": a_out, "first": part, "order": ("core", "y", "x", "z")},
        {"acc": b_acc, "out": b_out, "first": 0, "order": ("core", "zl", "zh", "x", "y")},
    ]
    landing = {"core": core_recv, "x": x_recv, "y": y_recv, "zl": l_recv, "zh": h_recv, "z": h_recv}

    def descend(n):
        chain = chains[n]
        level = chain.setdefault("level", 0)
        if level == 0:
            chain["base"], chain["size"] = chain["first"], part
        else:
            chain["base"] = reduce_finish(
                chain["copies"], chain["acc"], landing[chain["order"][level - 1]].at[n],
                chain["base"], chain["size"], chain["order"][level - 1],
            )
        if level < len(chain["order"]):
            axis = chain["order"][level]
            chain["size"] = chain["size"] // axes[axis][0]
            chain["copies"] = reduce_start(
                chain["acc"], landing[axis].at[n], chain["base"], chain["size"], axis
            )
            chain["level"] = level + 1
        else:
            here = rows(chain["base"], chain["size"])
            chain["out"][here, :] = (chain["acc"][here, :] * grad_scale).astype(chain["out"].dtype)
            chain["copies"] = []

    def ascend(n):
        chain = chains[n]
        finish(chain["copies"])
        level = chain["level"] - 1
        chain["level"] = level
        if level < 0:
            return
        group, own, _ = axes[chain["order"][level]]
        chain["base"] = chain["base"] - own * chain["size"]
        chain["copies"] = gather_start(
            chain["out"], chain["base"], chain["size"], chain["order"][level]
        )
        chain["size"] = chain["size"] * group

    second = dot(hidden[...], own_grad, (0, 0))
    for j in range(width // 128):
        b_acc[j * hid : (j + 1) * hid, :] = second[:, j * 128 : (j + 1) * 128]
    descend(2)
    q_base = reduce_finish(q_copies, q_acc, q_recv_y, 0, gz * q_rows, "y")
    q_copies = reduce_start(q_acc, q_recv_l, q_base, gh * q_rows, "zl")
    hid_grad = dot(own_grad, w2_ref[...], (1, 1))
    pre = pre_act[...]
    sig = jax.nn.sigmoid(pre)
    pre_grad = (hid_grad * sig * (1.0 + pre * (1.0 - sig))).astype(BF16)
    half = hid // 2
    for n in range(2):
        first = dot(tokens, pre_grad[:, n * half : (n + 1) * half], (0, 0))
        for j in range(half // 128):
            start_row = n * part + j * din
            a_acc[start_row : start_row + din, :] = first[:, j * 128 : (j + 1) * 128]
        descend(n)
        if n == 0:
            descend(2)
            q_base = reduce_finish(q_copies, q_acc, q_recv_l, q_base, gh * q_rows, "zl")
            q_copies = reduce_start(q_acc, q_recv_h, q_base, q_rows, "zh")
    for n in (0, 1, 2, 0, 1):
        descend(n)
    q_base = reduce_finish(q_copies, q_acc, q_recv_h, q_base, q_rows, "zh")
    qgrad_ref[...] = q_acc[rows(q_base, q_rows), :]
    for n in (0, 1, 2, 2, 2):
        descend(n)
    ascend(2)
    for n in (0, 1):
        descend(n)
        ascend(n)
    for n in (2, 0, 1, 2, 0, 1, 2, 0, 1, 2, 0, 1, 2):
        ascend(n)


def on_device(query_emb, targets, eligible_tiles, item_feats, w_first, w_second):
    q_rows, width = query_emb.shape
    ni, nq = lax.axis_size("item"), lax.axis_size("query")
    gx, gz = ni // 2, nq // 2
    tokens = item_feats.reshape(item_feats.shape[1], item_feats.shape[2])
    block, din = tokens.shape
    hid = w_first.shape[1]
    n_q = nq * q_rows
    meta_rows = -(-(ni + 1) // 8) * 8
    a_rows, b_rows = din * hid // 128, hid * width // 128
    part = b_rows
    out_dtype = BF16 if part // (nq * ni) % 16 == 0 else F32
    n_copies = 3 * (nq - 1) + (ni - 1) + 2 * gx + gx + gz + 3 * 2 * (3 + gx - 1 + gz - 1)
    vmem = pltpu.VMEM
    loss, query_grad, g1, g2 = pl.pallas_call(
        functools.partial(window_kernel, (nq, ni, 1.0 / math.sqrt(block * nq * ni))),
        out_shape=(
            jax.ShapeDtypeStruct((1, q_rows), F32),
            jax.ShapeDtypeStruct((q_rows, width), F32),
            jax.ShapeDtypeStruct((a_rows, 128), out_dtype),
            jax.ShapeDtypeStruct((b_rows, 128), out_dtype),
        ),
        in_specs=[pl.BlockSpec(memory_space=vmem)] * 3 + [pl.BlockSpec(memory_space=pl.ANY)] * 3,
        out_specs=(pl.BlockSpec(memory_space=vmem),) * 4,
        scratch_shapes=[
            vmem((block, din), BF16),
            vmem((din, hid), BF16),
            vmem((hid, width), BF16),
            vmem((n_q, width), BF16),
            vmem((ni, meta_rows, 128), jnp.int32),
            vmem((nq, meta_rows, 128), jnp.int32),
            vmem((ni * block, width), BF16),
            vmem((meta_rows, n_q), F32),
            vmem((ni * block, n_q), F32),
            vmem((ni * block, n_q), BF16),
            vmem((nq, 8, n_q), F32),
            vmem((ni * block, width), F32),
            vmem((gx * block, width), F32),
            vmem((max(gx - 1, 1) * block, width), F32),
            vmem((n_q, width), F32),
            vmem((gz * q_rows, width), F32),
            vmem((gz // 2 * q_rows, width), F32),
            vmem((max(gz // 2 - 1, 1) * q_rows, width), F32),
            vmem((block, hid), F32),
            vmem((block, hid), BF16),
            vmem((a_rows, 128), F32),
            vmem((b_rows, 128), F32),
            vmem((3, part // 2, 128), F32),
            vmem((3, part // 2, 128), F32),
            vmem((3, part // 4, 128), F32),
            vmem((3, part // 4, 128), F32),
            vmem((3, part // 4, 128), F32),
            pltpu.SemaphoreType.DMA((n_copies,)),
            pltpu.SemaphoreType.DMA((n_copies,)),
            pltpu.SemaphoreType.DMA((3,)),
        ],
        compiler_params=pltpu.CompilerParams(
            collective_id=0, has_side_effects=True, vmem_limit_bytes=58 * 2**20
        ),
        name="loss_window",
    )(query_emb, targets.reshape(1, -1), eligible_tiles, tokens, w_first, w_second)
    loss = loss.reshape(q_rows)
    g1 = g1.reshape(hid // 128, din, 128).transpose(1, 0, 2).reshape(din, hid).astype(F32)
    g2 = g2.reshape(width // 128, hid, 128).transpose(1, 0, 2).reshape(hid, width).astype(F32)
    return (loss, query_grad, g1, g2)

def small_kernel(
    grad_scale,
    query_hbm, targets_hbm, flags_hbm, tokens_hbm, w1_hbm, w2_hbm,
    loss_out, qgrad_out, a_out, b_out,
    targets_ref, flags_ref, loss_ref, qgrad_ref, tokens_all, w1_ref, w2_ref, q_all, raw_in, meta_in, emb_all, flags_all, scores, coeffs, stats_all,
    tops, e_acc, e_recv_c, e_send, e_recv_x, grad_all, q_acc, q_send, q_recv,
    hidden, slope, hid_cols, a_acc, b_acc, a_send, b_send, a_recv, b_recv_y, b_half, b_part, b_recv, a_all, b_all,
    send_sems, recv_sems, load_sems,
):
    nq, ni, gx, gy, gz = 8, 4, 2, 2, 4
    q, i = lax.axis_index("query"), lax.axis_index("item")
    core, x = lax.rem(i, 2), lax.div(i, 2)
    y, z = lax.rem(q, 2), lax.div(q, 2)
    q_rows, width = query_hbm.shape
    n_q = nq * q_rows
    block = tokens_hbm.shape[0]
    hid = w2_ref.shape[0]
    cols = hid // ni
    i_pos = core * gx + x
    used = [0]
    started = []

    def send(src, dst, peer):
        slot = used[0]
        used[0] += 1
        copy = pltpu.make_async_remote_copy(
            src_ref=src, dst_ref=dst, send_sem=send_sems.at[slot], recv_sem=recv_sems.at[slot],
            device_id=peer, device_id_type=pl.DeviceIdType.MESH,
        )
        copy.start()
        started.append(copy)
        return copy

    def arrived(copies):
        for copy in copies:
            copy.wait_recv()

    def ring(k):
        return {"query": lax.rem(q + k, nq)}

    def device(c_, x_, y_, z_):
        return {"query": z_ * 2 + y_, "item": x_ * 2 + c_}

    on_core = device(1 - core, x, y, z)
    on_x = device(core, 1 - x, y, z)
    on_cx = device(1 - core, 1 - x, y, z)
    on_y = device(core, x, 1 - y, z)
    on_xy = device(core, 1 - x, 1 - y, z)

    barrier = pltpu.get_barrier_semaphore()
    greeted = [ring(k) for k in range(1, nq)] + [on_core, on_x, on_cx, on_xy]
    for peer in greeted:
        pl.semaphore_signal(barrier, inc=1, device_id=peer, device_id_type=pl.DeviceIdType.MESH)

    loads = [
        pltpu.make_async_copy(src, dst, load_sems.at[n])
        for n, (src, dst) in enumerate((
            (query_hbm, q_all.at[rows(q * q_rows, q_rows)]), (targets_hbm, targets_ref), (flags_hbm, flags_ref),
            (tokens_hbm, tokens_all.at[rows(i_pos * block, block)]), (w1_hbm, w1_ref), (w2_hbm, w2_ref),
        ))
    ]
    for load in loads:
        load.start()

    for load in loads[:3]:
        load.wait()
    per = 128 // q_rows
    meta_rows = raw_in.shape[1]
    raw_in[i] = jnp.zeros((meta_rows, 128), jnp.int32)
    raw_in[i, 0:ni, 0:nq] = (flags_ref[...] > 0).astype(jnp.int32)
    lane_row = lax.broadcasted_iota(jnp.int32, (1, 128), 1)
    first_lane = pl.multiple_of(lax.div(i, per) * 128, 128)
    found = targets_ref[:, pl.ds(first_lane, 128)]
    shift = lax.rem(q - i + per * nq * ni, per)
    moved = found
    for h in range(1, per):
        moved = jnp.where(shift == h, pltpu.roll(found, h * q_rows, 1), moved)
    inside = lax.div(lane_row, q_rows) == lax.rem(q, per)
    own_targets = jnp.where(inside, moved, 0)

    pl.semaphore_wait(barrier, len(greeted))

    raw_copies = [send(raw_in.at[i], raw_in.at[i], peer) for peer in (on_x, on_cx, on_core)]
    emb_own = emb_all.at[rows(i_pos * block, block)]
    own_queries = q_all.at[rows(q * q_rows, q_rows)]
    query_copies = [send(own_queries, own_queries, ring(k)) for k in (4, 3, 5, 2, 6, 1, 7)]
    loads[3].wait()
    loads[4].wait()
    pre = dot(tokens_all[rows(i_pos * block, block), :], w1_ref[...], (1, 0))
    hidden[...] = jax.nn.silu(pre).astype(BF16)
    loads[5].wait()
    emb_all[rows(i_pos * block, block), :] = dot(hidden[...], w2_ref[...], (1, 0)).astype(BF16)
    emb_x = send(emb_own, emb_own, on_x)
    emb_c = send(emb_own, emb_own, on_core)
    arrived(raw_copies)
    packed = jnp.zeros((1, 128), jnp.int32)
    for t in range(ni):
        row = raw_in[t, pl.ds(i, 1), :]
        row = jnp.where(lane_row < nq, row, 0)
        low = pltpu.roll(row, t * nq, 1) if t else row
        packed = packed + jnp.where(lax.rem(q, 2) == 1, low, pltpu.roll(row, q_rows + t * nq, 1))
    meta_in[q] = packed + own_targets
    meta_copies = [send(meta_in.at[q], meta_in.at[q], ring(k)) for k in (4, 3, 5, 2, 6, 1, 7)]
    emb_x.wait_recv()
    emb_far = emb_all.at[rows((core * gx + 1 - x) * block, block)]
    emb_f = send(emb_far, emb_far, on_core)
    tok_own = tokens_all.at[rows(i_pos * block, block)]
    tok_x = send(tok_own, tok_own, on_x)
    tok_c = send(tok_own, tok_own, on_core)

    arrived(meta_copies)
    lane = lax.broadcasted_iota(jnp.int32, (meta_rows, 128), 1)
    sub = lax.broadcasted_iota(jnp.int32, (meta_rows, 128), 0)
    want_tiles, flag_tiles = [], []
    for t in range(nq // per):
        even, odd = meta_in[t * per], meta_in[t * per + 1]
        want_tiles.append(jnp.where(lane_row < q_rows, even, odd))
        flag = jnp.zeros((meta_rows, 128), F32)
        for h, sent in ((0, even), (1, odd)):
            at = sub * nq + q + (q_rows if h == 0 else 0)
            ours = (lane == at) & (sub < ni)
            column = jnp.sum(jnp.where(ours, sent, 0).astype(F32), axis=1, keepdims=True)
            inside = (lane >= h * q_rows) & (lane < (h + 1) * q_rows)
            flag = flag + jnp.where(inside, column, 0.0)
        flag_tiles.append(flag)
    wanted = jnp.concatenate(want_tiles, axis=1)
    flags_all[...] = jnp.concatenate(flag_tiles, axis=1)

    def located(p):
        item = lax.rem(p, gx) * 2 + lax.div(p, gx)
        first = (item * nq + q) * block
        ids = lax.broadcasted_iota(jnp.int32, (block, n_q), 0)
        hit = ids == (wanted - first)
        live = flags_all[pl.ds(item, 1), :] > 0.5
        return hit, live

    def score_block(p, carried):
        top, total, positive = carried
        hit, live = located(p)
        s = 0.25 * dot(emb_all[rows(p * block, block), :], q_all[...], (1, 1))
        here = jnp.max(s, axis=0, keepdims=True)
        e = jnp.exp(s - here)
        scores[rows(p * block, block), :] = e
        added = jnp.sum(e, axis=0, keepdims=True)
        positive = positive + jnp.sum(jnp.where(hit, s, 0.0), axis=0, keepdims=True)
        here = jnp.where(live, here, -1e30)
        tops[pl.ds(p, 1), :] = here
        new_top = jnp.maximum(top, here)
        total = total * jnp.exp(top - new_top) + jnp.where(live, added * jnp.exp(here - new_top), 0.0)
        return new_top, total, positive

    arrived(query_copies)
    carried = (jnp.full((1, n_q), -1e30, F32), jnp.zeros((1, n_q), F32), jnp.zeros((1, n_q), F32))
    carried = score_block(i_pos, carried)
    carried = score_block(core * gx + 1 - x, carried)
    emb_c.wait_recv()
    carried = score_block((1 - core) * gx + x, carried)
    emb_f.wait_recv()
    carried = score_block((1 - core) * gx + 1 - x, carried)
    top, total, positive = carried
    part_norm = jnp.where(total > 0.0, top + jnp.log(jnp.maximum(total, 1e-30)), -1e30)
    tiles = n_q // 128

    def stacked(row):
        return [row[:, t * 128 : (t + 1) * 128] for t in range(tiles)]

    stats_all[0] = jnp.concatenate(stacked(part_norm) + stacked(positive), axis=0)
    stats_copies = [send(stats_all.at[0], stats_all.at[k], ring(k)) for k in (4, 3, 5, 2, 6, 1, 7)]
    my_cols = pl.ds(pl.multiple_of(i * cols, 128), cols)

    def forward_cols(p):
        part = rows(p * block, block)
        pre = dot(tokens_all[part, :], w1_ref[:, my_cols], (1, 0))
        sig = jax.nn.sigmoid(pre)
        hid_cols[part, :] = (pre * sig).astype(BF16)
        slope[part, :] = sig * (1.0 + pre * (1.0 - sig))

    w2_cols = w2_ref[rows(i * cols, cols), :]
    forward_cols(i_pos)
    tok_c.wait_recv()
    forward_cols((1 - core) * gx + x)
    arrived(stats_copies)
    top = stats_all[0, 0:tiles, :]
    positive = stats_all[0, tiles:, :]
    for k in range(1, nq):
        top = jnp.maximum(top, stats_all[k, 0:tiles, :])
        positive = positive + stats_all[k, tiles:, :]
    total = jnp.zeros((tiles, 128), F32)
    for k in range(nq):
        total = total + jnp.exp(stats_all[k, 0:tiles, :] - top)
    norm_tiles = top + jnp.log(total)
    log_norm = jnp.concatenate([norm_tiles[t : t + 1, :] for t in range(tiles)], axis=1)
    def grad_block(p):
        hit, _ = located(p)
        factor = jnp.exp(tops[pl.ds(p, 1), :] - log_norm)
        c = (scores[rows(p * block, block), :] * factor - hit.astype(F32)).astype(BF16)
        coeffs[rows(p * block, block), :] = c
        e_acc[rows(p * block, block), :] = 0.25 * dot(c, q_all[...], (1, 0))

    crossing = []
    for t in range(gx):
        p = (1 - core) * gx + t
        slot = rows(t * block, block)
        grad_block(p)
        pair = send(e_acc.at[rows(p * block, block)], e_recv_c.at[slot], on_core)
        grad_block(core * gx + t)
        here = rows((core * gx + t) * block, block)
        pair.wait_recv()
        part = e_acc[here, :] + e_recv_c[slot, :]
        e_acc[here, :] = part
        e_send[slot, :] = part.astype(BF16)
        crossing.append(send(e_send.at[slot], e_recv_x.at[slot], on_x))
    q_acc[...] = 0.25 * dot(coeffs[...], emb_all[...], (0, 0))
    q_send[...] = q_acc[...].astype(BF16)
    q_copies = [
        send(
            q_send.at[rows(lax.rem(q + k, nq) * q_rows, q_rows)],
            q_recv.at[rows((k - 1) * q_rows, q_rows)], ring(k),
        )
        for k in (4, 3, 5, 2, 6, 1, 7)
    ]
    tok_x.wait_recv()
    tok_far = tokens_all.at[rows((core * gx + 1 - x) * block, block)]
    tok_f = send(tok_far, tok_far, on_core)
    forward_cols(core * gx + 1 - x)
    losses = norm_tiles - positive
    found = jnp.zeros((1, 128), F32)
    for t in range(tiles):
        found = found + jnp.where(lax.div(q, per) == t, losses[t : t + 1, :], 0.0)
    moved = found
    for h in range(1, per):
        moved = jnp.where(lax.rem(q, per) == h, pltpu.roll(found, (per - h) * q_rows, 1), moved)
    loss_ref[...] = moved[:, :q_rows]

    tok_f.wait_recv()
    forward_cols((1 - core) * gx + 1 - x)

    def tower_b(p, first):
        part = rows(p * block, block)
        b = dot(hid_cols[part, :], grad_all[part, :], (0, 0))
        b = b.reshape(b_acc.shape)
        b_acc[...] = b if first else b_acc[...] + b

    def tower_a(p, first):
        part = rows(p * block, block)
        pre_grad = (dot(grad_all[part, :], w2_cols, (1, 1)) * slope[part, :]).astype(BF16)
        a = dot(tokens_all[part, :], pre_grad, (0, 0))
        a_acc[...] = a if first else a_acc[...] + a

    for t in range(gx):
        mine, theirs = core * gx + t, (1 - core) * gx + t
        here = rows(mine * block, block)
        crossing[t].wait_recv()
        grad_all[here, :] = (e_acc[here, :] + e_recv_x[rows(t * block, block), :].astype(F32)).astype(BF16)
        over = send(grad_all.at[here], grad_all.at[here], on_core)
        tower_b(mine, t == 0)
        tower_a(mine, t == 0)
        over.wait_recv()
        tower_b(theirs, False)
        if t == gx - 1:
            b_send[...] = b_acc[...].astype(BF16)
            b_y = send(b_send.at[:, 1 - y], b_recv_y, on_y)
        tower_a(theirs, False)
    a_rows = a_acc.shape[0] // nq
    a_send[...] = a_acc[...].astype(BF16)
    a_copies = [
        send(
            a_send.at[rows(lax.rem(q + k, nq) * a_rows, a_rows)],
            a_recv.at[rows((k - 1) * a_rows, a_rows)], ring(k),
        )
        for k in (4, 3, 5, 2, 6, 1, 7)
    ]

    b_y.wait_recv()
    b_half[...] = b_acc[:, y] + b_recv_y[...].astype(F32)
    b_part[...] = b_half[...].astype(BF16)
    b_copies = [
        send(b_part.at[lax.rem(z + k, gz)], b_recv.at[k - 1], device(core, x, y, lax.rem(z + k, gz)))
        for k in (2, 1, 3)
    ]
    arrived(q_copies)
    total = q_acc[rows(q * q_rows, q_rows), :]
    for k in range(1, nq):
        total = total + q_recv[rows((k - 1) * q_rows, q_rows), :].astype(F32)
    qgrad_ref[...] = total
    outs = [pltpu.make_async_copy(loss_ref, loss_out, load_sems.at[14]), pltpu.make_async_copy(qgrad_ref, qgrad_out, load_sems.at[15])]
    for copy in outs:
        copy.start()
    kept = []

    def leave(out, x_, y_):
        whole = {id(a_all): a_out, id(b_all): b_out}[id(out)].at[x_, core, :, y_]
        copy = pltpu.make_async_copy(out.at[x_, :, y_], whole, load_sems.at[6 + len(kept)])
        copy.start()
        kept.append(copy)
        return send(out.at[x_, :, y_], whole, on_core)

    def gather_own(copies, parts, out, split):
        arrived(copies)
        total = parts()
        out[x, z, y] = (total * grad_scale).astype(BF16)
        own = out.at[x, z, y]
        first = out.at[x, z, y, pl.ds(0, split)]
        up = [send(first, first, device(core, x, y, lax.rem(z + k, gz))) for k in (2, 1, 3)]
        return up, [[send(own, own, peer) for peer in (on_xy, on_x, on_y)]]

    def gather_rest(over, out, split):
        size = out.shape[3] - split
        if size == 0:
            return []
        arrived(over.pop(0))
        rest = out.at[:, z, :, pl.ds(split, size)]
        return [send(rest, rest, device(core, x, y, lax.rem(z + k, gz))) for k in (2, 1, 3)]

    def gather_far(up, over, out, split):
        for n, k in enumerate((2, 1, 3)):
            up[n].wait_recv()
            far = out.at[x, lax.rem(z - k + gz, gz), y, pl.ds(0, split)]
            over.append([send(far, far, peer) for peer in (on_xy, on_x, on_y)])

    def gather_core(over, rest, out):
        arrived(rest)
        crossed = [leave(out, x, y)]
        for n, (x_, y_) in ((1, (1 - x, y)), (2, (x, 1 - y)), (0, (1 - x, 1 - y))):
            arrived([four[n] for four in over])
            crossed.append(leave(out, x_, y_))
        return crossed

    def a_total():
        total = a_acc[rows(q * a_rows, a_rows), :]
        for k in range(1, nq):
            total = total + a_recv[rows((k - 1) * a_rows, a_rows), :].astype(F32)
        return total

    def b_total():
        total = b_half[z]
        for k in range(1, gz):
            total = total + b_recv[k - 1].astype(F32)
        return total

    a_split, b_split = a_rows * 3 // 4, b_all.shape[3]
    a_up, a_over = gather_own(a_copies, a_total, a_all, a_split)
    b_up, b_over = gather_own(b_copies, b_total, b_all, b_split)
    b_rest = gather_rest(b_over, b_all, b_split)
    a_rest = gather_rest(a_over, a_all, a_split)
    gather_far(a_up, a_over, a_all, a_split)
    gather_far(b_up, b_over, b_all, b_split)
    crossed = gather_core(a_over, a_rest, a_all)
    crossed += gather_core(b_over, b_rest, b_all)
    arrived(crossed)
    for copy in kept + outs:
        copy.wait()
    for copy in started:
        copy.wait_send()


def finish_kernel(loss_in, qgrad_in, a_in, b_in, loss_ref, qgrad_ref, a_ref, b_ref):
    loss_ref[...] = loss_in[...]
    qgrad_ref[...] = qgrad_in[...]
    for t in range(a_in.shape[0]):
        for r in range(a_in.shape[1]):
            size, cols = a_in.shape[2], a_in.shape[3]
            a_ref[r * size : (r + 1) * size, t * cols : (t + 1) * cols] = a_in[t, r].astype(F32)
    b_ref[...] = b_in[...].astype(F32)


def on_device_small(query_emb, targets, eligible_tiles, item_feats, w_first, w_second):
    q_rows, width = query_emb.shape
    ni, nq = lax.axis_size("item"), lax.axis_size("query")
    tokens = item_feats.reshape(item_feats.shape[1], item_feats.shape[2])
    block, din = tokens.shape
    hid = w_first.shape[1]
    n_q, items, cols = nq * q_rows, ni * block, hid // ni
    a_rows, b_rows = din // nq, cols // nq
    vmem = pltpu.VMEM
    out = (2, 2, nq // 2, 2)
    loss, query_grad, g1, g2 = pl.pallas_call(
        functools.partial(small_kernel, 1.0 / math.sqrt(items * nq)),
        out_shape=(
            jax.ShapeDtypeStruct((1, q_rows), F32),
            jax.ShapeDtypeStruct((q_rows, width), F32),
            jax.ShapeDtypeStruct(out + (a_rows, cols), BF16),
            jax.ShapeDtypeStruct(out + (b_rows, width), BF16),
        ),
        in_specs=[pl.BlockSpec(memory_space=pl.ANY)] * 6,
        out_specs=(pl.BlockSpec(memory_space=pl.ANY),) * 4,
        scratch_shapes=[
            vmem((1, targets.shape[0]), jnp.int32),
            vmem(eligible_tiles.shape, jnp.int32),
            vmem((1, q_rows), F32),
            vmem((q_rows, width), F32),
            vmem((items, din), BF16),
            vmem((din, hid), BF16),
            vmem((hid, width), BF16),
            vmem((n_q, width), BF16),
            vmem((ni, 8, 128), jnp.int32),
            vmem((nq, 1, 128), jnp.int32),
            vmem((items, width), BF16),
            vmem((8, n_q), F32),
            vmem((items, n_q), F32),
            vmem((items, n_q), BF16),
            vmem((nq, 2 * n_q // 128, 128), F32),
            vmem((8, n_q), F32),
            vmem((items, width), F32),
            vmem((2 * block, width), F32),
            vmem((2 * block, width), BF16),
            vmem((2 * block, width), BF16),
            vmem((items, width), BF16),
            vmem((n_q, width), F32),
            vmem((n_q, width), BF16),
            vmem(((nq - 1) * q_rows, width), BF16),
            vmem((block, hid), BF16),
            vmem((items, cols), F32),
            vmem((items, cols), BF16),
            vmem((din, cols), F32),
            vmem((nq // 2, 2, b_rows, width), F32),
            vmem((din, cols), BF16),
            vmem((nq // 2, 2, b_rows, width), BF16),
            vmem(((nq - 1) * a_rows, cols), BF16),
            vmem((nq // 2, b_rows, width), BF16),
            vmem((nq // 2, b_rows, width), F32),
            vmem((nq // 2, b_rows, width), BF16),
            vmem((nq // 2 - 1, b_rows, width), BF16),
            vmem((2, nq // 2, 2, a_rows, cols), BF16),
            vmem((2, nq // 2, 2, b_rows, width), BF16),
            pltpu.SemaphoreType.DMA((112,)),
            pltpu.SemaphoreType.DMA((112,)),
            pltpu.SemaphoreType.DMA((16,)),
        ],
        compiler_params=pltpu.CompilerParams(
            collective_id=0, has_side_effects=True, vmem_limit_bytes=58 * 2**20
        ),
        name="loss_window",
    )(query_emb, targets.reshape(1, -1), eligible_tiles, tokens, w_first, w_second)
    steps = 2
    loss, query_grad, g1, g2 = pl.pallas_call(
        finish_kernel,
        grid=(steps,),
        out_shape=(
            jax.ShapeDtypeStruct((1, q_rows), F32),
            jax.ShapeDtypeStruct((q_rows, width), F32),
            jax.ShapeDtypeStruct((din, hid), F32),
            jax.ShapeDtypeStruct((ni, nq, b_rows, width), F32),
        ),
        in_specs=[
            pl.BlockSpec((1, q_rows), lambda n: (0, 0)),
            pl.BlockSpec((q_rows // steps, width), lambda n: (n, 0)),
            pl.BlockSpec((ni, nq // steps, a_rows, cols), lambda n: (0, n, 0, 0)),
            pl.BlockSpec((ni, nq // steps, b_rows, width), lambda n: (0, n, 0, 0)),
        ],
        out_specs=(
            pl.BlockSpec((1, q_rows), lambda n: (0, 0)),
            pl.BlockSpec((q_rows // steps, width), lambda n: (n, 0)),
            pl.BlockSpec((din // steps, hid), lambda n: (n, 0)),
            pl.BlockSpec((ni, nq // steps, b_rows, width), lambda n: (0, n, 0, 0)),
        ),
        name="widen",
    )(loss, query_grad, g1.reshape(ni, nq, a_rows, cols), g2.reshape(ni, nq, b_rows, width))
    return loss.reshape(q_rows), query_grad, g1, g2.reshape(hid, width)


def solution(mesh):
    small = mesh.shape["query"] == 8 and mesh.shape["item"] == 4
    return jax.shard_map(
        on_device_small if small else on_device,
        mesh=mesh,
        in_specs=(
            P(("query", "item"), None),
            P("query"),
            P("query", "item"),
            P("item", "query", None),
            P(),
            P(),
        ),
        out_specs=(P(("query", "item")), P(("query", "item"), None), P(), P()),
        check_vma=False,
    )
```

```python
import functools
import math

import jax
import jax.numpy as jnp
from jax import lax
from jax.experimental import pallas as pl
from jax.experimental.pallas import tpu as pltpu
from jax.sharding import PartitionSpec as P

F32 = jnp.float32
BF16 = jnp.bfloat16


def dot(a, b, contract):
    return lax.dot_general(a, b, ((contract[:1], contract[1:]), ((), ())), preferred_element_type=F32)


def rows(start, size):
    return pl.ds(pl.multiple_of(start, math.gcd(size, 256)), size)


def window_kernel(
    shape,
    query_ref, targets_ref, flags_ref, tokens_hbm, w1_hbm, w2_hbm,
    loss_ref, qgrad_ref, a_out, b_out,
    tokens_ref, w1_ref, w2_ref, q_all, raw_in, meta_in, emb_all, flags_all, scores, coeffs, stats_all,
    e_acc, e_recv_c, e_recv_x, q_acc, q_recv_y, q_recv_l, q_recv_h,
    pre_act, hidden, a_acc, b_acc, core_recv, x_recv, y_recv, l_recv, h_recv,
    send_sems, recv_sems, load_sems,
):
    nq, ni, grad_scale = shape
    gx, gz = ni // 2, nq // 2
    q, i = lax.axis_index("query"), lax.axis_index("item")
    core, x = lax.rem(i, 2), lax.div(i, 2)
    y, z = lax.rem(q, 2), lax.div(q, 2)
    zl, zh = lax.rem(z, 2), lax.div(z, 2)
    gh = gz // 2
    q_rows, width = query_ref.shape
    n_q = nq * q_rows
    block = tokens_ref.shape[0]
    used = [0]
    loads = [
        pltpu.make_async_copy(src, dst, load_sems.at[n])
        for n, (src, dst) in enumerate(((tokens_hbm, tokens_ref), (w1_hbm, w1_ref), (w2_hbm, w2_ref)))
    ]
    for load in loads:
        load.start()

    def send(src, dst, peer):
        slot = used[0]
        used[0] += 1
        copy = pltpu.make_async_remote_copy(
            src_ref=src, dst_ref=dst, send_sem=send_sems.at[slot], recv_sem=recv_sems.at[slot],
            device_id=peer, device_id_type=pl.DeviceIdType.MESH,
        )
        copy.start()
        return copy

    def finish(copies):
        for copy in copies:
            copy.wait()

    axes = {
        "core": (2, core, lambda t: {"item": x * 2 + t}),
        "x": (gx, x, lambda t: {"item": t * 2 + core}),
        "y": (2, y, lambda t: {"query": z * 2 + t}),
        "z": (gz, z, lambda t: {"query": t * 2 + y}),
        "zl": (2, zl, lambda t: {"query": (zh * 2 + t) * 2 + y}),
        "zh": (gh, zh, lambda t: {"query": (t * 2 + zl) * 2 + y}),
    }

    def reduce_start(acc, recv, base, size, axis):
        group, own, peer = axes[axis]
        copies = []
        for k in range(1, group):
            there = lax.rem(own + k, group)
            copies.append(
                send(acc.at[rows(base + there * size, size)], recv.at[rows((k - 1) * size, size)], peer(there))
            )
        return copies

    def reduce_finish(copies, acc, recv, base, size, axis):
        group, own, _ = axes[axis]
        finish(copies)
        here = rows(base + own * size, size)
        total = acc[here, :]
        for k in range(1, group):
            total = total + recv[rows((k - 1) * size, size), :]
        acc[here, :] = total
        return base + own * size

    def gather_start(buf, base, size, axis):
        group, own, peer = axes[axis]
        here = buf.at[rows(base + own * size, size)]
        return [send(here, here, peer(lax.rem(own + k, group))) for k in range(1, group)]

    barrier = pltpu.get_barrier_semaphore()
    for k in range(1, nq):
        pl.semaphore_signal(
            barrier, inc=1, device_id={"query": lax.rem(q + k, nq)}, device_id_type=pl.DeviceIdType.MESH
        )
    for k in range(1, ni):
        pl.semaphore_signal(
            barrier, inc=1, device_id={"item": lax.rem(i + k, ni)}, device_id_type=pl.DeviceIdType.MESH
        )
    pl.semaphore_wait(barrier, nq + ni - 2)

    q_pos = (y * 2 + zl) * gh + zh
    query_copies = []
    for k in range(1, nq):
        there = lax.rem(q + k, nq)
        query_copies.append(send(query_ref, q_all.at[rows(q_pos * q_rows, q_rows)], {"query": there}))
    per = 128 // q_rows
    meta_rows = raw_in.shape[1]
    raw_in[i] = jnp.zeros((meta_rows, 128), jnp.int32)
    raw_in[i, 0:ni, 0:nq] = (flags_ref[...] > 0).astype(jnp.int32)
    raw_copies = [send(raw_in.at[i], raw_in.at[i], {"item": lax.rem(i + k, ni)}) for k in range(1, ni)]
    q_all[rows(q_pos * q_rows, q_rows), :] = query_ref[...]
    lane_row = lax.broadcasted_iota(jnp.int32, (1, 128), 1)
    first_lane = pl.multiple_of(lax.div(i, per) * 128, 128)
    found = targets_ref[:, pl.ds(first_lane, 128)]
    shift = lax.rem(q_pos - i + per * nq * ni, per)
    moved = found
    for h in range(1, per):
        moved = jnp.where(shift == h, pltpu.roll(found, h * q_rows, 1), moved)
    inside = lax.div(lane_row, q_rows) == lax.rem(q_pos, per)
    own_targets = jnp.where(inside, moved, 0)
    loads[0].wait()
    loads[1].wait()
    tokens = tokens_ref[...]
    pre = dot(tokens, w1_ref[...], (1, 0))
    pre_act[...] = pre
    finish(raw_copies)
    parts = [raw_in[t, pl.ds(i, 1), :] for t in range(ni)] + [own_targets]
    if meta_rows > ni + 1:
        parts.append(jnp.zeros((meta_rows - ni - 1, 128), jnp.int32))
    meta_in[q_pos] = jnp.concatenate(parts, axis=0)
    for k in range(1, nq):
        query_copies.append(send(meta_in.at[q_pos], meta_in.at[q_pos], {"query": lax.rem(q + k, nq)}))
    loads[2].wait()
    hidden[...] = jax.nn.silu(pre).astype(BF16)
    i_pos = core * gx + x
    emb_all[rows(i_pos * block, block), :] = dot(hidden[...], w2_ref[...], (1, 0)).astype(BF16)

    finish(gather_start(emb_all, core * gx * block, block, "x"))
    finish(gather_start(emb_all, 0, gx * block, "core"))

    finish(query_copies)
    lane = lax.broadcasted_iota(jnp.int32, (meta_rows, 128), 1)
    want_tiles, flag_tiles = [], []
    for t in range(nq // per):
        want = jnp.zeros((1, 128), jnp.int32)
        flag = jnp.zeros((meta_rows, 128), F32)
        for h in range(per):
            sent = meta_in[t * per + h]
            want = want + sent[ni : ni + 1, :]
            column = jnp.sum(jnp.where(lane == q, sent, 0).astype(F32), axis=1, keepdims=True)
            inside = (lane >= h * q_rows) & (lane < (h + 1) * q_rows)
            flag = flag + jnp.where(inside, column, 0.0)
        want_tiles.append(want)
        flag_tiles.append(flag)
    wanted = jnp.concatenate(want_tiles, axis=1)
    flags_all[...] = jnp.concatenate(flag_tiles, axis=1)

    def located(p):
        item = lax.rem(p, gx) * 2 + lax.div(p, gx)
        first = (item * nq + q) * block
        ids = lax.broadcasted_iota(jnp.int32, (block, n_q), 0)
        hit = ids == (wanted - first)
        live = flags_all[pl.ds(item, 1), :] > 0.5
        return hit, live

    def score_block(p, carried):
        top, total, positive = carried
        hit, live = located(p)
        s = 0.25 * dot(emb_all[rows(p * block, block), :], q_all[...], (1, 1))
        scores[rows(p * block, block), :] = s
        here = jnp.max(s, axis=0, keepdims=True)
        added = jnp.sum(jnp.exp(s - here), axis=0, keepdims=True)
        positive = positive + jnp.sum(jnp.where(hit, s, 0.0), axis=0, keepdims=True)
        here = jnp.where(live, here, -1e30)
        new_top = jnp.maximum(top, here)
        total = total * jnp.exp(top - new_top) + jnp.where(live, added * jnp.exp(here - new_top), 0.0)
        return new_top, total, positive

    start = (jnp.full((1, n_q), -1e30, F32), jnp.zeros((1, n_q), F32), jnp.zeros((1, n_q), F32))
    top, total, positive = lax.fori_loop(0, ni, score_block, start)
    stats_all[0] = jnp.concatenate([top, total, positive, jnp.zeros((5, n_q), F32)], axis=0)
    finish([
        send(stats_all.at[0], stats_all.at[k], {"query": lax.rem(q + k, nq)}) for k in range(1, nq)
    ])
    top = stats_all[0, 0:1, :]
    for k in range(1, nq):
        top = jnp.maximum(top, stats_all[k, 0:1, :])
    total = jnp.zeros((1, n_q), F32)
    positive = jnp.zeros((1, n_q), F32)
    for k in range(nq):
        total = total + stats_all[k, 1:2, :] * jnp.exp(stats_all[k, 0:1, :] - top)
        positive = positive + stats_all[k, 2:3, :]
    log_norm = top + jnp.log(total)
    stats_all[0, 0:1, :] = log_norm - positive
    found = stats_all[0, 0:1, pl.ds(pl.multiple_of(lax.div(q_pos, per) * 128, 128), 128)]
    moved = found
    for h in range(1, per):
        moved = jnp.where(lax.rem(q_pos, per) == h, pltpu.roll(found, (per - h) * q_rows, 1), moved)
    loss_ref[...] = moved[:, :q_rows]

    def grad_block(p, carried):
        hit, live = located(p)
        s = scores[rows(p * block, block), :]
        weights = jnp.where(live, jnp.exp(s - log_norm), 0.0)
        c = (weights - hit.astype(F32)).astype(BF16)
        coeffs[rows(p * block, block), :] = c
        e_acc[rows(p * block, block), :] = 0.25 * dot(c, q_all[...], (1, 0))
        return carried

    e_size = gx * block
    pairs = []
    for k in list(range(1, gx)) + [0]:
        t = lax.rem(x + k, gx)
        grad_block((1 - core) * gx + t, 0)
        leaving = rows(((1 - core) * gx + t) * block, block)
        landed = e_recv_c.at[rows(t * block, block)]
        pairs.append(send(e_acc.at[leaving], landed, {"item": x * 2 + 1 - core}))
        grad_block(core * gx + t, 0)
        if k > 0:
            here = rows((core * gx + t) * block, block)
            pairs[-1].wait()
            e_acc[here, :] = e_acc[here, :] + e_recv_c[rows(t * block, block), :]
            pairs[-1] = send(e_acc.at[here], e_recv_x.at[rows((k - 1) * block, block)], {"item": t * 2 + core})
    q_acc[...] = 0.25 * dot(coeffs[...], emb_all[...], (0, 0))
    q_copies = reduce_start(q_acc, q_recv_y, 0, gz * q_rows, "y")
    e_base = (core * gx + x) * block
    pairs[-1].wait()
    e_acc[rows(e_base, block), :] = e_acc[rows(e_base, block), :] + e_recv_c[rows(x * block, block), :]
    e_base = reduce_finish(pairs[:-1], e_acc, e_recv_x, core * gx * block, block, "x")
    own_grad = e_acc[rows(e_base, block), :].astype(BF16)

    hid, din = w2_ref.shape[0], tokens.shape[1]
    part = b_acc.shape[0]
    chains = [
        {"acc": a_acc, "out": a_out, "first": 0, "order": ("core", "x", "y", "z")},
        {"acc": a_acc, "out": a_out, "first": part, "order": ("core", "y", "x", "z")},
        {"acc": b_acc, "out": b_out, "first": 0, "order": ("core", "zl", "zh", "x", "y")},
    ]
    landing = {"core": core_recv, "x": x_recv, "y": y_recv, "zl": l_recv, "zh": h_recv, "z": h_recv}

    def descend(n):
        chain = chains[n]
        level = chain.setdefault("level", 0)
        if level == 0:
            chain["base"], chain["size"] = chain["first"], part
        else:
            chain["base"] = reduce_finish(
                chain["copies"], chain["acc"], landing[chain["order"][level - 1]].at[n],
                chain["base"], chain["size"], chain["order"][level - 1],
            )
        if level < len(chain["order"]):
            axis = chain["order"][level]
            chain["size"] = chain["size"] // axes[axis][0]
            chain["copies"] = reduce_start(
                chain["acc"], landing[axis].at[n], chain["base"], chain["size"], axis
            )
            chain["level"] = level + 1
        else:
            here = rows(chain["base"], chain["size"])
            chain["out"][here, :] = (chain["acc"][here, :] * grad_scale).astype(chain["out"].dtype)
            chain["copies"] = []

    def ascend(n):
        chain = chains[n]
        finish(chain["copies"])
        level = chain["level"] - 1
        chain["level"] = level
        if level < 0:
            return
        group, own, _ = axes[chain["order"][level]]
        chain["base"] = chain["base"] - own * chain["size"]
        chain["copies"] = gather_start(
            chain["out"], chain["base"], chain["size"], chain["order"][level]
        )
        chain["size"] = chain["size"] * group

    second = dot(hidden[...], own_grad, (0, 0))
    for j in range(width // 128):
        b_acc[j * hid : (j + 1) * hid, :] = second[:, j * 128 : (j + 1) * 128]
    descend(2)
    q_base = reduce_finish(q_copies, q_acc, q_recv_y, 0, gz * q_rows, "y")
    q_copies = reduce_start(q_acc, q_recv_l, q_base, gh * q_rows, "zl")
    hid_grad = dot(own_grad, w2_ref[...], (1, 1))
    pre = pre_act[...]
    sig = jax.nn.sigmoid(pre)
    pre_grad = (hid_grad * sig * (1.0 + pre * (1.0 - sig))).astype(BF16)
    half = hid // 2
    for n in range(2):
        first = dot(tokens, pre_grad[:, n * half : (n + 1) * half], (0, 0))
        for j in range(half // 128):
            start_row = n * part + j * din
            a_acc[start_row : start_row + din, :] = first[:, j * 128 : (j + 1) * 128]
        descend(n)
        if n == 0:
            descend(2)
            q_base = reduce_finish(q_copies, q_acc, q_recv_l, q_base, gh * q_rows, "zl")
            q_copies = reduce_start(q_acc, q_recv_h, q_base, q_rows, "zh")
    for n in (0, 1, 2, 0, 1):
        descend(n)
    q_base = reduce_finish(q_copies, q_acc, q_recv_h, q_base, q_rows, "zh")
    qgrad_ref[...] = q_acc[rows(q_base, q_rows), :]
    for n in (0, 1, 2, 2, 2):
        descend(n)
    ascend(2)
    for n in (0, 1):
        descend(n)
        ascend(n)
    for n in (2, 0, 1, 2, 0, 1, 2, 0, 1, 2, 0, 1, 2):
        ascend(n)


def on_device(query_emb, targets, eligible_tiles, item_feats, w_first, w_second):
    q_rows, width = query_emb.shape
    ni, nq = lax.axis_size("item"), lax.axis_size("query")
    gx, gz = ni // 2, nq // 2
    tokens = item_feats.reshape(item_feats.shape[1], item_feats.shape[2])
    block, din = tokens.shape
    hid = w_first.shape[1]
    n_q = nq * q_rows
    meta_rows = -(-(ni + 1) // 8) * 8
    a_rows, b_rows = din * hid // 128, hid * width // 128
    part = b_rows
    out_dtype = BF16 if part // (nq * ni) % 16 == 0 else F32
    n_copies = 3 * (nq - 1) + (ni - 1) + 2 * gx + gx + gz + 3 * 2 * (3 + gx - 1 + gz - 1)
    vmem = pltpu.VMEM
    loss, query_grad, g1, g2 = pl.pallas_call(
        functools.partial(window_kernel, (nq, ni, 1.0 / math.sqrt(block * nq * ni))),
        out_shape=(
            jax.ShapeDtypeStruct((1, q_rows), F32),
            jax.ShapeDtypeStruct((q_rows, width), F32),
            jax.ShapeDtypeStruct((a_rows, 128), out_dtype),
            jax.ShapeDtypeStruct((b_rows, 128), out_dtype),
        ),
        in_specs=[pl.BlockSpec(memory_space=vmem)] * 3 + [pl.BlockSpec(memory_space=pl.ANY)] * 3,
        out_specs=(pl.BlockSpec(memory_space=vmem),) * 4,
        scratch_shapes=[
            vmem((block, din), BF16),
            vmem((din, hid), BF16),
            vmem((hid, width), BF16),
            vmem((n_q, width), BF16),
            vmem((ni, meta_rows, 128), jnp.int32),
            vmem((nq, meta_rows, 128), jnp.int32),
            vmem((ni * block, width), BF16),
            vmem((meta_rows, n_q), F32),
            vmem((ni * block, n_q), F32),
            vmem((ni * block, n_q), BF16),
            vmem((nq, 8, n_q), F32),
            vmem((ni * block, width), F32),
            vmem((gx * block, width), F32),
            vmem((max(gx - 1, 1) * block, width), F32),
            vmem((n_q, width), F32),
            vmem((gz * q_rows, width), F32),
            vmem((gz // 2 * q_rows, width), F32),
            vmem((max(gz // 2 - 1, 1) * q_rows, width), F32),
            vmem((block, hid), F32),
            vmem((block, hid), BF16),
            vmem((a_rows, 128), F32),
            vmem((b_rows, 128), F32),
            vmem((3, part // 2, 128), F32),
            vmem((3, part // 2, 128), F32),
            vmem((3, part // 4, 128), F32),
            vmem((3, part // 4, 128), F32),
            vmem((3, part // 4, 128), F32),
            pltpu.SemaphoreType.DMA((n_copies,)),
            pltpu.SemaphoreType.DMA((n_copies,)),
            pltpu.SemaphoreType.DMA((3,)),
        ],
        compiler_params=pltpu.CompilerParams(
            collective_id=0, has_side_effects=True, vmem_limit_bytes=58 * 2**20
        ),
        name="loss_window",
    )(query_emb, targets.reshape(1, -1), eligible_tiles, tokens, w_first, w_second)
    loss = loss.reshape(q_rows)
    g1 = g1.reshape(hid // 128, din, 128).transpose(1, 0, 2).reshape(din, hid).astype(F32)
    g2 = g2.reshape(width // 128, hid, 128).transpose(1, 0, 2).reshape(hid, width).astype(F32)
    return (loss, query_grad, g1, g2)

def small_kernel(
    grad_scale,
    query_hbm, targets_hbm, flags_hbm, tokens_hbm, w1_hbm, w2_hbm,
    loss_out, qgrad_out, a_out, b_out,
    targets_ref, flags_ref, loss_ref, qgrad_ref, tokens_all, w1_ref, w2_ref, q_all, raw_in, meta_in, emb_all, flags_all, scores, coeffs, stats_all,
    tops, e_acc, e_recv_c, e_send, e_recv_x, grad_all, q_acc, q_send, q_recv,
    hidden, slope, hid_cols, a_acc, b_acc, a_send, b_send, a_recv, b_recv_y, b_half, b_part, b_recv, a_all, b_all,
    send_sems, recv_sems, load_sems,
):
    nq, ni, gx, gy, gz = 8, 4, 2, 2, 4
    q, i = lax.axis_index("query"), lax.axis_index("item")
    core, x = lax.rem(i, 2), lax.div(i, 2)
    y, z = lax.rem(q, 2), lax.div(q, 2)
    q_rows, width = query_hbm.shape
    n_q = nq * q_rows
    block = tokens_hbm.shape[0]
    hid = w2_ref.shape[0]
    cols = hid // ni
    i_pos = core * gx + x
    used = [0]
    started = []

    def send(src, dst, peer):
        slot = used[0]
        used[0] += 1
        copy = pltpu.make_async_remote_copy(
            src_ref=src, dst_ref=dst, send_sem=send_sems.at[slot], recv_sem=recv_sems.at[slot],
            device_id=peer, device_id_type=pl.DeviceIdType.MESH,
        )
        copy.start()
        started.append(copy)
        return copy

    def arrived(copies):
        for copy in copies:
            copy.wait_recv()

    def ring(k):
        return {"query": lax.rem(q + k, nq)}

    def device(c_, x_, y_, z_):
        return {"query": z_ * 2 + y_, "item": x_ * 2 + c_}

    on_core = device(1 - core, x, y, z)
    on_x = device(core, 1 - x, y, z)
    on_cx = device(1 - core, 1 - x, y, z)
    on_y = device(core, x, 1 - y, z)
    on_xy = device(core, 1 - x, 1 - y, z)

    barrier = pltpu.get_barrier_semaphore()
    greeted = [ring(k) for k in range(1, nq)] + [on_core, on_x, on_cx, on_xy]
    for peer in greeted:
        pl.semaphore_signal(barrier, inc=1, device_id=peer, device_id_type=pl.DeviceIdType.MESH)

    loads = [
        pltpu.make_async_copy(src, dst, load_sems.at[n])
        for n, (src, dst) in enumerate((
            (query_hbm, q_all.at[rows(q * q_rows, q_rows)]), (targets_hbm, targets_ref), (flags_hbm, flags_ref),
            (tokens_hbm, tokens_all.at[rows(i_pos * block, block)]), (w1_hbm, w1_ref), (w2_hbm, w2_ref),
        ))
    ]
    for load in loads:
        load.start()

    for load in loads[:3]:
        load.wait()
    mine = rows(q * q_rows, q_rows)
    q_all[mine, :] = (0.25 * q_all[mine, :].astype(F32)).astype(BF16)
    per = 128 // q_rows
    meta_rows = raw_in.shape[1]
    raw_in[i] = jnp.zeros((meta_rows, 128), jnp.int32)
    raw_in[i, 0:ni, 0:nq] = (flags_ref[...] > 0).astype(jnp.int32)
    lane_row = lax.broadcasted_iota(jnp.int32, (1, 128), 1)
    first_lane = pl.multiple_of(lax.div(i, per) * 128, 128)
    found = targets_ref[:, pl.ds(first_lane, 128)]
    shift = lax.rem(q - i + per * nq * ni, per)
    moved = found
    for h in range(1, per):
        moved = jnp.where(shift == h, pltpu.roll(found, h * q_rows, 1), moved)
    inside = lax.div(lane_row, q_rows) == lax.rem(q, per)
    own_targets = jnp.where(inside, moved, 0)

    pl.semaphore_wait(barrier, len(greeted))

    raw_copies = [send(raw_in.at[i], raw_in.at[i], peer) for peer in (on_x, on_cx, on_core)]
    emb_own = emb_all.at[rows(i_pos * block, block)]
    own_queries = q_all.at[rows(q * q_rows, q_rows)]
    query_copies = [send(own_queries, own_queries, ring(k)) for k in (4, 3, 5, 2, 6, 1, 7)]
    loads[3].wait()
    loads[4].wait()
    pre = dot(tokens_all[rows(i_pos * block, block), :], w1_ref[...], (1, 0))
    hidden[...] = jax.nn.silu(pre).astype(BF16)
    loads[5].wait()
    emb_all[rows(i_pos * block, block), :] = dot(hidden[...], w2_ref[...], (1, 0)).astype(BF16)
    emb_x = send(emb_own, emb_own, on_x)
    emb_c = send(emb_own, emb_own, on_core)
    arrived(raw_copies)
    packed = jnp.zeros((1, 128), jnp.int32)
    for t in range(ni):
        row = raw_in[t, pl.ds(i, 1), :]
        row = jnp.where(lane_row < nq, row, 0)
        low = pltpu.roll(row, t * nq, 1) if t else row
        packed = packed + jnp.where(lax.rem(q, 2) == 1, low, pltpu.roll(row, q_rows + t * nq, 1))
    meta_in[q] = packed + own_targets
    meta_copies = [send(meta_in.at[q], meta_in.at[q], ring(k)) for k in (4, 3, 5, 2, 6, 1, 7)]
    emb_x.wait_recv()
    emb_far = emb_all.at[rows((core * gx + 1 - x) * block, block)]
    emb_f = send(emb_far, emb_far, on_core)
    tok_own = tokens_all.at[rows(i_pos * block, block)]
    tok_x = send(tok_own, tok_own, on_x)
    tok_c = send(tok_own, tok_own, on_core)

    arrived(meta_copies)
    lane = lax.broadcasted_iota(jnp.int32, (meta_rows, 128), 1)
    sub = lax.broadcasted_iota(jnp.int32, (meta_rows, 128), 0)
    want_tiles, flag_tiles = [], []
    for t in range(nq // per):
        even, odd = meta_in[t * per], meta_in[t * per + 1]
        want_tiles.append(jnp.where(lane_row < q_rows, even, odd))
        flag = jnp.zeros((meta_rows, 128), F32)
        for h, sent in ((0, even), (1, odd)):
            at = sub * nq + q + (q_rows if h == 0 else 0)
            ours = (lane == at) & (sub < ni)
            column = jnp.sum(jnp.where(ours, sent, 0).astype(F32), axis=1, keepdims=True)
            inside = (lane >= h * q_rows) & (lane < (h + 1) * q_rows)
            flag = flag + jnp.where(inside, column, 0.0)
        flag_tiles.append(flag)
    wanted = jnp.concatenate(want_tiles, axis=1)
    flags_all[...] = jnp.concatenate(flag_tiles, axis=1)

    def located(p):
        item = lax.rem(p, gx) * 2 + lax.div(p, gx)
        first = (item * nq + q) * block
        ids = lax.broadcasted_iota(jnp.int32, (block, n_q), 0)
        hit = ids == (wanted - first)
        live = flags_all[pl.ds(item, 1), :] > 0.5
        return hit, live

    def score_block(p, carried):
        top, total, positive = carried
        hit, live = located(p)
        s = dot(emb_all[rows(p * block, block), :], q_all[...], (1, 1))
        here = jnp.max(s, axis=0, keepdims=True)
        e = jnp.exp(s - here)
        scores[rows(p * block, block), :] = e
        added = jnp.sum(e, axis=0, keepdims=True)
        positive = positive + jnp.sum(jnp.where(hit, s, 0.0), axis=0, keepdims=True)
        here = jnp.where(live, here, -1e30)
        tops[pl.ds(p, 1), :] = here
        new_top = jnp.maximum(top, here)
        total = total * jnp.exp(top - new_top) + jnp.where(live, added * jnp.exp(here - new_top), 0.0)
        return new_top, total, positive

    arrived(query_copies)
    carried = (jnp.full((1, n_q), -1e30, F32), jnp.zeros((1, n_q), F32), jnp.zeros((1, n_q), F32))
    carried = score_block(i_pos, carried)
    carried = score_block(core * gx + 1 - x, carried)
    emb_c.wait_recv()
    carried = score_block((1 - core) * gx + x, carried)
    emb_f.wait_recv()
    carried = score_block((1 - core) * gx + 1 - x, carried)
    top, total, positive = carried
    part_norm = jnp.where(total > 0.0, top + jnp.log(jnp.maximum(total, 1e-30)), -1e30)
    tiles = n_q // 128

    def stacked(row):
        return [row[:, t * 128 : (t + 1) * 128] for t in range(tiles)]

    stats_all[0] = jnp.concatenate(stacked(part_norm) + stacked(positive), axis=0)
    stats_copies = [send(stats_all.at[0], stats_all.at[k], ring(k)) for k in (4, 3, 5, 2, 6, 1, 7)]
    my_cols = pl.ds(pl.multiple_of(i * cols, 128), cols)

    def forward_cols(p):
        part = rows(p * block, block)
        pre = dot(tokens_all[part, :], w1_ref[:, my_cols], (1, 0))
        sig = jax.nn.sigmoid(pre)
        hid_cols[part, :] = (pre * sig).astype(BF16)
        slope[part, :] = sig * (1.0 + pre * (1.0 - sig))

    w2_cols = w2_ref[rows(i * cols, cols), :]
    forward_cols(i_pos)
    tok_c.wait_recv()
    forward_cols((1 - core) * gx + x)
    arrived(stats_copies)
    top = stats_all[0, 0:tiles, :]
    positive = stats_all[0, tiles:, :]
    for k in range(1, nq):
        top = jnp.maximum(top, stats_all[k, 0:tiles, :])
        positive = positive + stats_all[k, tiles:, :]
    total = jnp.zeros((tiles, 128), F32)
    for k in range(nq):
        total = total + jnp.exp(stats_all[k, 0:tiles, :] - top)
    norm_tiles = top + jnp.log(total)
    log_norm = jnp.concatenate([norm_tiles[t : t + 1, :] for t in range(tiles)], axis=1)
    def grad_block(p):
        hit, _ = located(p)
        factor = jnp.exp(tops[pl.ds(p, 1), :] - log_norm)
        c = (scores[rows(p * block, block), :] * factor - hit.astype(F32)).astype(BF16)
        coeffs[rows(p * block, block), :] = c
        e_acc[rows(p * block, block), :] = dot(c, q_all[...], (1, 0))

    crossing = []
    for t in range(gx):
        p = (1 - core) * gx + t
        slot = rows(t * block, block)
        grad_block(p)
        pair = send(e_acc.at[rows(p * block, block)], e_recv_c.at[slot], on_core)
        grad_block(core * gx + t)
        here = rows((core * gx + t) * block, block)
        pair.wait_recv()
        part = e_acc[here, :] + e_recv_c[slot, :]
        e_acc[here, :] = part
        e_send[slot, :] = part.astype(BF16)
        crossing.append(send(e_send.at[slot], e_recv_x.at[slot], on_x))
    q_acc[...] = 0.25 * dot(coeffs[...], emb_all[...], (0, 0))
    q_send[...] = q_acc[...].astype(BF16)
    q_copies = [
        send(
            q_send.at[rows(lax.rem(q + k, nq) * q_rows, q_rows)],
            q_recv.at[rows((k - 1) * q_rows, q_rows)], ring(k),
        )
        for k in (4, 3, 5, 2, 6, 1, 7)
    ]
    tok_x.wait_recv()
    tok_far = tokens_all.at[rows((core * gx + 1 - x) * block, block)]
    tok_f = send(tok_far, tok_far, on_core)
    forward_cols(core * gx + 1 - x)
    losses = norm_tiles - positive
    found = jnp.zeros((1, 128), F32)
    for t in range(tiles):
        found = found + jnp.where(lax.div(q, per) == t, losses[t : t + 1, :], 0.0)
    moved = found
    for h in range(1, per):
        moved = jnp.where(lax.rem(q, per) == h, pltpu.roll(found, (per - h) * q_rows, 1), moved)
    loss_ref[...] = moved[:, :q_rows]

    tok_f.wait_recv()
    forward_cols((1 - core) * gx + 1 - x)

    def tower_b(p, first):
        part = rows(p * block, block)
        b = dot(hid_cols[part, :], grad_all[part, :], (0, 0))
        b = b.reshape(b_acc.shape)
        b_acc[...] = b if first else b_acc[...] + b

    def tower_a(p, first):
        part = rows(p * block, block)
        pre_grad = (dot(grad_all[part, :], w2_cols, (1, 1)) * slope[part, :]).astype(BF16)
        a = dot(tokens_all[part, :], pre_grad, (0, 0))
        a_acc[...] = a if first else a_acc[...] + a

    for t in range(gx):
        mine, theirs = core * gx + t, (1 - core) * gx + t
        here = rows(mine * block, block)
        crossing[t].wait_recv()
        grad_all[here, :] = (e_acc[here, :] + e_recv_x[rows(t * block, block), :].astype(F32)).astype(BF16)
        over = send(grad_all.at[here], grad_all.at[here], on_core)
        tower_b(mine, t == 0)
        tower_a(mine, t == 0)
        over.wait_recv()
        tower_b(theirs, False)
        if t == gx - 1:
            b_send[...] = b_acc[...].astype(BF16)
            b_y = send(b_send.at[:, 1 - y], b_recv_y, on_y)
        tower_a(theirs, False)
    a_rows = a_acc.shape[0] // nq
    a_send[...] = a_acc[...].astype(BF16)
    a_copies = [
        send(
            a_send.at[rows(lax.rem(q + k, nq) * a_rows, a_rows)],
            a_recv.at[rows((k - 1) * a_rows, a_rows)], ring(k),
        )
        for k in (4, 3, 5, 2, 6, 1, 7)
    ]

    b_y.wait_recv()
    b_half[...] = b_acc[:, y] + b_recv_y[...].astype(F32)
    b_part[...] = b_half[...].astype(BF16)
    b_copies = [
        send(b_part.at[lax.rem(z + k, gz)], b_recv.at[k - 1], device(core, x, y, lax.rem(z + k, gz)))
        for k in (2, 1, 3)
    ]
    arrived(q_copies)
    total = q_acc[rows(q * q_rows, q_rows), :]
    for k in range(1, nq):
        total = total + q_recv[rows((k - 1) * q_rows, q_rows), :].astype(F32)
    qgrad_ref[...] = total
    outs = [pltpu.make_async_copy(loss_ref, loss_out, load_sems.at[14]), pltpu.make_async_copy(qgrad_ref, qgrad_out, load_sems.at[15])]
    for copy in outs:
        copy.start()
    kept = []

    def leave(out, x_, y_):
        whole = {id(a_all): a_out, id(b_all): b_out}[id(out)].at[x_, core, :, y_]
        return send(out.at[x_, :, y_], whole, on_core)

    def keep(out):
        whole = {id(a_all): a_out, id(b_all): b_out}[id(out)].at[:, core]
        copy = pltpu.make_async_copy(out, whole, load_sems.at[6 + len(kept)])
        copy.start()
        kept.append(copy)

    def gather_own(copies, parts, out, split):
        arrived(copies)
        total = parts()
        out[x, z, y] = (total * grad_scale).astype(BF16)
        own = out.at[x, z, y]
        first = out.at[x, z, y, pl.ds(0, split)]
        up = [send(first, first, device(core, x, y, lax.rem(z + k, gz))) for k in (2, 1, 3)]
        return up, [[send(own, own, peer) for peer in (on_xy, on_x, on_y)]]

    def gather_rest(over, out, split):
        size = out.shape[3] - split
        if size == 0:
            return []
        arrived(over.pop(0))
        rest = out.at[:, z, :, pl.ds(split, size)]
        return [send(rest, rest, device(core, x, y, lax.rem(z + k, gz))) for k in (2, 1, 3)]

    def gather_far(up, over, out, split):
        for n, k in enumerate((2, 1, 3)):
            up[n].wait_recv()
            far = out.at[x, lax.rem(z - k + gz, gz), y, pl.ds(0, split)]
            over.append([send(far, far, peer) for peer in (on_xy, on_x, on_y)])

    def gather_core(over, rest, out):
        arrived(rest)
        crossed = []
        for ns, (x_, y_) in (((1,), (slice(None), y)), ((2, 0), (slice(None), 1 - y))):
            arrived([four[n] for n in ns for four in over])
            crossed.append(leave(out, x_, y_))
        keep(out)
        return crossed

    def a_total():
        total = a_acc[rows(q * a_rows, a_rows), :]
        for k in range(1, nq):
            total = total + a_recv[rows((k - 1) * a_rows, a_rows), :].astype(F32)
        return total

    def b_total():
        total = b_half[z]
        for k in range(1, gz):
            total = total + b_recv[k - 1].astype(F32)
        return total

    a_split, b_split = a_rows * 3 // 4, b_all.shape[3]
    a_up, a_over = gather_own(a_copies, a_total, a_all, a_split)
    b_up, b_over = gather_own(b_copies, b_total, b_all, b_split)
    b_rest = gather_rest(b_over, b_all, b_split)
    a_rest = gather_rest(a_over, a_all, a_split)
    gather_far(a_up, a_over, a_all, a_split)
    gather_far(b_up, b_over, b_all, b_split)
    crossed = gather_core(a_over, a_rest, a_all)
    crossed += gather_core(b_over, b_rest, b_all)
    arrived(crossed)
    for copy in kept + outs:
        copy.wait()
    for copy in started:
        copy.wait_send()


def finish_kernel(loss_in, qgrad_in, a_in, b_in, loss_ref, qgrad_ref, a_ref, b_ref):
    loss_ref[...] = loss_in[...]
    qgrad_ref[...] = qgrad_in[...]
    for t in range(a_in.shape[0]):
        for r in range(a_in.shape[1]):
            size, cols = a_in.shape[2], a_in.shape[3]
            a_ref[r * size : (r + 1) * size, t * cols : (t + 1) * cols] = a_in[t, r].astype(F32)
    b_ref[...] = b_in[...].astype(F32)


def on_device_small(query_emb, targets, eligible_tiles, item_feats, w_first, w_second):
    q_rows, width = query_emb.shape
    ni, nq = lax.axis_size("item"), lax.axis_size("query")
    tokens = item_feats.reshape(item_feats.shape[1], item_feats.shape[2])
    block, din = tokens.shape
    hid = w_first.shape[1]
    n_q, items, cols = nq * q_rows, ni * block, hid // ni
    a_rows, b_rows = din // nq, cols // nq
    vmem = pltpu.VMEM
    out = (2, 2, nq // 2, 2)
    loss, query_grad, g1, g2 = pl.pallas_call(
        functools.partial(small_kernel, 1.0 / math.sqrt(items * nq)),
        out_shape=(
            jax.ShapeDtypeStruct((1, q_rows), F32),
            jax.ShapeDtypeStruct((q_rows, width), F32),
            jax.ShapeDtypeStruct(out + (a_rows, cols), BF16),
            jax.ShapeDtypeStruct(out + (b_rows, width), BF16),
        ),
        in_specs=[pl.BlockSpec(memory_space=pl.ANY)] * 6,
        out_specs=(pl.BlockSpec(memory_space=pl.ANY),) * 4,
        scratch_shapes=[
            vmem((1, targets.shape[0]), jnp.int32),
            vmem(eligible_tiles.shape, jnp.int32),
            vmem((1, q_rows), F32),
            vmem((q_rows, width), F32),
            vmem((items, din), BF16),
            vmem((din, hid), BF16),
            vmem((hid, width), BF16),
            vmem((n_q, width), BF16),
            vmem((ni, 8, 128), jnp.int32),
            vmem((nq, 1, 128), jnp.int32),
            vmem((items, width), BF16),
            vmem((8, n_q), F32),
            vmem((items, n_q), F32),
            vmem((items, n_q), BF16),
            vmem((nq, 2 * n_q // 128, 128), F32),
            vmem((8, n_q), F32),
            vmem((items, width), F32),
            vmem((2 * block, width), F32),
            vmem((2 * block, width), BF16),
            vmem((2 * block, width), BF16),
            vmem((items, width), BF16),
            vmem((n_q, width), F32),
            vmem((n_q, width), BF16),
            vmem(((nq - 1) * q_rows, width), BF16),
            vmem((block, hid), BF16),
            vmem((items, cols), F32),
            vmem((items, cols), BF16),
            vmem((din, cols), F32),
            vmem((nq // 2, 2, b_rows, width), F32),
            vmem((din, cols), BF16),
            vmem((nq // 2, 2, b_rows, width), BF16),
            vmem(((nq - 1) * a_rows, cols), BF16),
            vmem((nq // 2, b_rows, width), BF16),
            vmem((nq // 2, b_rows, width), F32),
            vmem((nq // 2, b_rows, width), BF16),
            vmem((nq // 2 - 1, b_rows, width), BF16),
            vmem((2, nq // 2, 2, a_rows, cols), BF16),
            vmem((2, nq // 2, 2, b_rows, width), BF16),
            pltpu.SemaphoreType.DMA((112,)),
            pltpu.SemaphoreType.DMA((112,)),
            pltpu.SemaphoreType.DMA((16,)),
        ],
        compiler_params=pltpu.CompilerParams(
            collective_id=0, has_side_effects=True, vmem_limit_bytes=58 * 2**20
        ),
        name="loss_window",
    )(query_emb, targets.reshape(1, -1), eligible_tiles, tokens, w_first, w_second)
    steps = 2
    loss, query_grad, g1, g2 = pl.pallas_call(
        finish_kernel,
        grid=(steps,),
        out_shape=(
            jax.ShapeDtypeStruct((1, q_rows), F32),
            jax.ShapeDtypeStruct((q_rows, width), F32),
            jax.ShapeDtypeStruct((din, hid), F32),
            jax.ShapeDtypeStruct((ni, nq, b_rows, width), F32),
        ),
        in_specs=[
            pl.BlockSpec((1, q_rows), lambda n: (0, 0)),
            pl.BlockSpec((q_rows // steps, width), lambda n: (n, 0)),
            pl.BlockSpec((ni, nq // steps, a_rows, cols), lambda n: (0, n, 0, 0)),
            pl.BlockSpec((ni, nq // steps, b_rows, width), lambda n: (0, n, 0, 0)),
        ],
        out_specs=(
            pl.BlockSpec((1, q_rows), lambda n: (0, 0)),
            pl.BlockSpec((q_rows // steps, width), lambda n: (n, 0)),
            pl.BlockSpec((din // steps, hid), lambda n: (n, 0)),
            pl.BlockSpec((ni, nq // steps, b_rows, width), lambda n: (0, n, 0, 0)),
        ),
        name="widen",
    )(loss, query_grad, g1.reshape(ni, nq, a_rows, cols), g2.reshape(ni, nq, b_rows, width))
    return loss.reshape(q_rows), query_grad, g1, g2.reshape(hid, width)


def solution(mesh):
    small = mesh.shape["query"] == 8 and mesh.shape["item"] == 4
    return jax.shard_map(
        on_device_small if small else on_device,
        mesh=mesh,
        in_specs=(
            P(("query", "item"), None),
            P("query"),
            P("query", "item"),
            P("item", "query", None),
            P(),
            P(),
        ),
        out_specs=(P(("query", "item")), P(("query", "item"), None), P(), P()),
        check_vma=False,
    )
```

```python
import functools
import math

import jax
import jax.numpy as jnp
from jax import lax
from jax.experimental import pallas as pl
from jax.experimental.pallas import tpu as pltpu
from jax.sharding import PartitionSpec as P

F32 = jnp.float32
BF16 = jnp.bfloat16


def dot(a, b, contract):
    return lax.dot_general(a, b, ((contract[:1], contract[1:]), ((), ())), preferred_element_type=F32)


def rows(start, size):
    return pl.ds(pl.multiple_of(start, math.gcd(size, 256)), size)


def window_kernel(
    shape,
    query_ref, targets_ref, flags_ref, tokens_hbm, w1_hbm, w2_hbm,
    loss_ref, qgrad_ref, a_out, b_out,
    tokens_ref, w1_ref, w2_ref, q_all, raw_in, meta_in, emb_all, flags_all, scores, coeffs, stats_all,
    e_acc, e_recv_c, e_recv_x, q_acc, q_recv_y, q_recv_l, q_recv_h,
    pre_act, hidden, a_acc, b_acc, core_recv, x_recv, y_recv, l_recv, h_recv,
    send_sems, recv_sems, load_sems,
):
    nq, ni, grad_scale = shape
    gx, gz = ni // 2, nq // 2
    q, i = lax.axis_index("query"), lax.axis_index("item")
    core, x = lax.rem(i, 2), lax.div(i, 2)
    y, z = lax.rem(q, 2), lax.div(q, 2)
    zl, zh = lax.rem(z, 2), lax.div(z, 2)
    gh = gz // 2
    q_rows, width = query_ref.shape
    n_q = nq * q_rows
    block = tokens_ref.shape[0]
    used = [0]
    loads = [
        pltpu.make_async_copy(src, dst, load_sems.at[n])
        for n, (src, dst) in enumerate(((tokens_hbm, tokens_ref), (w1_hbm, w1_ref), (w2_hbm, w2_ref)))
    ]
    for load in loads:
        load.start()

    def send(src, dst, peer):
        slot = used[0]
        used[0] += 1
        copy = pltpu.make_async_remote_copy(
            src_ref=src, dst_ref=dst, send_sem=send_sems.at[slot], recv_sem=recv_sems.at[slot],
            device_id=peer, device_id_type=pl.DeviceIdType.MESH,
        )
        copy.start()
        return copy

    def finish(copies):
        for copy in copies:
            copy.wait()

    axes = {
        "core": (2, core, lambda t: {"item": x * 2 + t}),
        "x": (gx, x, lambda t: {"item": t * 2 + core}),
        "y": (2, y, lambda t: {"query": z * 2 + t}),
        "z": (gz, z, lambda t: {"query": t * 2 + y}),
        "zl": (2, zl, lambda t: {"query": (zh * 2 + t) * 2 + y}),
        "zh": (gh, zh, lambda t: {"query": (t * 2 + zl) * 2 + y}),
    }

    def reduce_start(acc, recv, base, size, axis):
        group, own, peer = axes[axis]
        copies = []
        for k in range(1, group):
            there = lax.rem(own + k, group)
            copies.append(
                send(acc.at[rows(base + there * size, size)], recv.at[rows((k - 1) * size, size)], peer(there))
            )
        return copies

    def reduce_finish(copies, acc, recv, base, size, axis):
        group, own, _ = axes[axis]
        finish(copies)
        here = rows(base + own * size, size)
        total = acc[here, :]
        for k in range(1, group):
            total = total + recv[rows((k - 1) * size, size), :]
        acc[here, :] = total
        return base + own * size

    def gather_start(buf, base, size, axis):
        group, own, peer = axes[axis]
        here = buf.at[rows(base + own * size, size)]
        return [send(here, here, peer(lax.rem(own + k, group))) for k in range(1, group)]

    barrier = pltpu.get_barrier_semaphore()
    for k in range(1, nq):
        pl.semaphore_signal(
            barrier, inc=1, device_id={"query": lax.rem(q + k, nq)}, device_id_type=pl.DeviceIdType.MESH
        )
    for k in range(1, ni):
        pl.semaphore_signal(
            barrier, inc=1, device_id={"item": lax.rem(i + k, ni)}, device_id_type=pl.DeviceIdType.MESH
        )
    pl.semaphore_wait(barrier, nq + ni - 2)

    q_pos = (y * 2 + zl) * gh + zh
    query_copies = []
    for k in range(1, nq):
        there = lax.rem(q + k, nq)
        query_copies.append(send(query_ref, q_all.at[rows(q_pos * q_rows, q_rows)], {"query": there}))
    per = 128 // q_rows
    meta_rows = raw_in.shape[1]
    raw_in[i] = jnp.zeros((meta_rows, 128), jnp.int32)
    raw_in[i, 0:ni, 0:nq] = (flags_ref[...] > 0).astype(jnp.int32)
    raw_copies = [send(raw_in.at[i], raw_in.at[i], {"item": lax.rem(i + k, ni)}) for k in range(1, ni)]
    q_all[rows(q_pos * q_rows, q_rows), :] = query_ref[...]
    lane_row = lax.broadcasted_iota(jnp.int32, (1, 128), 1)
    first_lane = pl.multiple_of(lax.div(i, per) * 128, 128)
    found = targets_ref[:, pl.ds(first_lane, 128)]
    shift = lax.rem(q_pos - i + per * nq * ni, per)
    moved = found
    for h in range(1, per):
        moved = jnp.where(shift == h, pltpu.roll(found, h * q_rows, 1), moved)
    inside = lax.div(lane_row, q_rows) == lax.rem(q_pos, per)
    own_targets = jnp.where(inside, moved, 0)
    loads[0].wait()
    loads[1].wait()
    tokens = tokens_ref[...]
    pre = dot(tokens, w1_ref[...], (1, 0))
    pre_act[...] = pre
    finish(raw_copies)
    parts = [raw_in[t, pl.ds(i, 1), :] for t in range(ni)] + [own_targets]
    if meta_rows > ni + 1:
        parts.append(jnp.zeros((meta_rows - ni - 1, 128), jnp.int32))
    meta_in[q_pos] = jnp.concatenate(parts, axis=0)
    for k in range(1, nq):
        query_copies.append(send(meta_in.at[q_pos], meta_in.at[q_pos], {"query": lax.rem(q + k, nq)}))
    loads[2].wait()
    hidden[...] = jax.nn.silu(pre).astype(BF16)
    i_pos = core * gx + x
    emb_all[rows(i_pos * block, block), :] = dot(hidden[...], w2_ref[...], (1, 0)).astype(BF16)

    finish(gather_start(emb_all, core * gx * block, block, "x"))
    finish(gather_start(emb_all, 0, gx * block, "core"))

    finish(query_copies)
    lane = lax.broadcasted_iota(jnp.int32, (meta_rows, 128), 1)
    want_tiles, flag_tiles = [], []
    for t in range(nq // per):
        want = jnp.zeros((1, 128), jnp.int32)
        flag = jnp.zeros((meta_rows, 128), F32)
        for h in range(per):
            sent = meta_in[t * per + h]
            want = want + sent[ni : ni + 1, :]
            column = jnp.sum(jnp.where(lane == q, sent, 0).astype(F32), axis=1, keepdims=True)
            inside = (lane >= h * q_rows) & (lane < (h + 1) * q_rows)
            flag = flag + jnp.where(inside, column, 0.0)
        want_tiles.append(want)
        flag_tiles.append(flag)
    wanted = jnp.concatenate(want_tiles, axis=1)
    flags_all[...] = jnp.concatenate(flag_tiles, axis=1)

    def located(p):
        item = lax.rem(p, gx) * 2 + lax.div(p, gx)
        first = (item * nq + q) * block
        ids = lax.broadcasted_iota(jnp.int32, (block, n_q), 0)
        hit = ids == (wanted - first)
        live = flags_all[pl.ds(item, 1), :] > 0.5
        return hit, live

    def score_block(p, carried):
        top, total, positive = carried
        hit, live = located(p)
        s = 0.25 * dot(emb_all[rows(p * block, block), :], q_all[...], (1, 1))
        scores[rows(p * block, block), :] = s
        here = jnp.max(s, axis=0, keepdims=True)
        added = jnp.sum(jnp.exp(s - here), axis=0, keepdims=True)
        positive = positive + jnp.sum(jnp.where(hit, s, 0.0), axis=0, keepdims=True)
        here = jnp.where(live, here, -1e30)
        new_top = jnp.maximum(top, here)
        total = total * jnp.exp(top - new_top) + jnp.where(live, added * jnp.exp(here - new_top), 0.0)
        return new_top, total, positive

    start = (jnp.full((1, n_q), -1e30, F32), jnp.zeros((1, n_q), F32), jnp.zeros((1, n_q), F32))
    top, total, positive = lax.fori_loop(0, ni, score_block, start)
    stats_all[0] = jnp.concatenate([top, total, positive, jnp.zeros((5, n_q), F32)], axis=0)
    finish([
        send(stats_all.at[0], stats_all.at[k], {"query": lax.rem(q + k, nq)}) for k in range(1, nq)
    ])
    top = stats_all[0, 0:1, :]
    for k in range(1, nq):
        top = jnp.maximum(top, stats_all[k, 0:1, :])
    total = jnp.zeros((1, n_q), F32)
    positive = jnp.zeros((1, n_q), F32)
    for k in range(nq):
        total = total + stats_all[k, 1:2, :] * jnp.exp(stats_all[k, 0:1, :] - top)
        positive = positive + stats_all[k, 2:3, :]
    log_norm = top + jnp.log(total)
    stats_all[0, 0:1, :] = log_norm - positive
    found = stats_all[0, 0:1, pl.ds(pl.multiple_of(lax.div(q_pos, per) * 128, 128), 128)]
    moved = found
    for h in range(1, per):
        moved = jnp.where(lax.rem(q_pos, per) == h, pltpu.roll(found, (per - h) * q_rows, 1), moved)
    loss_ref[...] = moved[:, :q_rows]

    def grad_block(p, carried):
        hit, live = located(p)
        s = scores[rows(p * block, block), :]
        weights = jnp.where(live, jnp.exp(s - log_norm), 0.0)
        c = (weights - hit.astype(F32)).astype(BF16)
        coeffs[rows(p * block, block), :] = c
        e_acc[rows(p * block, block), :] = 0.25 * dot(c, q_all[...], (1, 0))
        return carried

    e_size = gx * block
    pairs = []
    for k in list(range(1, gx)) + [0]:
        t = lax.rem(x + k, gx)
        grad_block((1 - core) * gx + t, 0)
        leaving = rows(((1 - core) * gx + t) * block, block)
        landed = e_recv_c.at[rows(t * block, block)]
        pairs.append(send(e_acc.at[leaving], landed, {"item": x * 2 + 1 - core}))
        grad_block(core * gx + t, 0)
        if k > 0:
            here = rows((core * gx + t) * block, block)
            pairs[-1].wait()
            e_acc[here, :] = e_acc[here, :] + e_recv_c[rows(t * block, block), :]
            pairs[-1] = send(e_acc.at[here], e_recv_x.at[rows((k - 1) * block, block)], {"item": t * 2 + core})
    q_acc[...] = 0.25 * dot(coeffs[...], emb_all[...], (0, 0))
    q_copies = reduce_start(q_acc, q_recv_y, 0, gz * q_rows, "y")
    e_base = (core * gx + x) * block
    pairs[-1].wait()
    e_acc[rows(e_base, block), :] = e_acc[rows(e_base, block), :] + e_recv_c[rows(x * block, block), :]
    e_base = reduce_finish(pairs[:-1], e_acc, e_recv_x, core * gx * block, block, "x")
    own_grad = e_acc[rows(e_base, block), :].astype(BF16)

    hid, din = w2_ref.shape[0], tokens.shape[1]
    part = b_acc.shape[0]
    chains = [
        {"acc": a_acc, "out": a_out, "first": 0, "order": ("core", "x", "y", "z")},
        {"acc": a_acc, "out": a_out, "first": part, "order": ("core", "y", "x", "z")},
        {"acc": b_acc, "out": b_out, "first": 0, "order": ("core", "zl", "zh", "x", "y")},
    ]
    landing = {"core": core_recv, "x": x_recv, "y": y_recv, "zl": l_recv, "zh": h_recv, "z": h_recv}

    def descend(n):
        chain = chains[n]
        level = chain.setdefault("level", 0)
        if level == 0:
            chain["base"], chain["size"] = chain["first"], part
        else:
            chain["base"] = reduce_finish(
                chain["copies"], chain["acc"], landing[chain["order"][level - 1]].at[n],
                chain["base"], chain["size"], chain["order"][level - 1],
            )
        if level < len(chain["order"]):
            axis = chain["order"][level]
            chain["size"] = chain["size"] // axes[axis][0]
            chain["copies"] = reduce_start(
                chain["acc"], landing[axis].at[n], chain["base"], chain["size"], axis
            )
            chain["level"] = level + 1
        else:
            here = rows(chain["base"], chain["size"])
            chain["out"][here, :] = (chain["acc"][here, :] * grad_scale).astype(chain["out"].dtype)
            chain["copies"] = []

    def ascend(n):
        chain = chains[n]
        finish(chain["copies"])
        level = chain["level"] - 1
        chain["level"] = level
        if level < 0:
            return
        group, own, _ = axes[chain["order"][level]]
        chain["base"] = chain["base"] - own * chain["size"]
        chain["copies"] = gather_start(
            chain["out"], chain["base"], chain["size"], chain["order"][level]
        )
        chain["size"] = chain["size"] * group

    second = dot(hidden[...], own_grad, (0, 0))
    for j in range(width // 128):
        b_acc[j * hid : (j + 1) * hid, :] = second[:, j * 128 : (j + 1) * 128]
    descend(2)
    q_base = reduce_finish(q_copies, q_acc, q_recv_y, 0, gz * q_rows, "y")
    q_copies = reduce_start(q_acc, q_recv_l, q_base, gh * q_rows, "zl")
    hid_grad = dot(own_grad, w2_ref[...], (1, 1))
    pre = pre_act[...]
    sig = jax.nn.sigmoid(pre)
    pre_grad = (hid_grad * sig * (1.0 + pre * (1.0 - sig))).astype(BF16)
    half = hid // 2
    for n in range(2):
        first = dot(tokens, pre_grad[:, n * half : (n + 1) * half], (0, 0))
        for j in range(half // 128):
            start_row = n * part + j * din
            a_acc[start_row : start_row + din, :] = first[:, j * 128 : (j + 1) * 128]
        descend(n)
        if n == 0:
            descend(2)
            q_base = reduce_finish(q_copies, q_acc, q_recv_l, q_base, gh * q_rows, "zl")
            q_copies = reduce_start(q_acc, q_recv_h, q_base, q_rows, "zh")
    for n in (0, 1, 2, 0, 1):
        descend(n)
    q_base = reduce_finish(q_copies, q_acc, q_recv_h, q_base, q_rows, "zh")
    qgrad_ref[...] = q_acc[rows(q_base, q_rows), :]
    for n in (0, 1, 2, 2, 2):
        descend(n)
    ascend(2)
    for n in (0, 1):
        descend(n)
        ascend(n)
    for n in (2, 0, 1, 2, 0, 1, 2, 0, 1, 2, 0, 1, 2):
        ascend(n)


def on_device(query_emb, targets, eligible_tiles, item_feats, w_first, w_second):
    q_rows, width = query_emb.shape
    ni, nq = lax.axis_size("item"), lax.axis_size("query")
    gx, gz = ni // 2, nq // 2
    tokens = item_feats.reshape(item_feats.shape[1], item_feats.shape[2])
    block, din = tokens.shape
    hid = w_first.shape[1]
    n_q = nq * q_rows
    meta_rows = -(-(ni + 1) // 8) * 8
    a_rows, b_rows = din * hid // 128, hid * width // 128
    part = b_rows
    out_dtype = BF16 if part // (nq * ni) % 16 == 0 else F32
    n_copies = 3 * (nq - 1) + (ni - 1) + 2 * gx + gx + gz + 3 * 2 * (3 + gx - 1 + gz - 1)
    vmem = pltpu.VMEM
    loss, query_grad, g1, g2 = pl.pallas_call(
        functools.partial(window_kernel, (nq, ni, 1.0 / math.sqrt(block * nq * ni))),
        out_shape=(
            jax.ShapeDtypeStruct((1, q_rows), F32),
            jax.ShapeDtypeStruct((q_rows, width), F32),
            jax.ShapeDtypeStruct((a_rows, 128), out_dtype),
            jax.ShapeDtypeStruct((b_rows, 128), out_dtype),
        ),
        in_specs=[pl.BlockSpec(memory_space=vmem)] * 3 + [pl.BlockSpec(memory_space=pl.ANY)] * 3,
        out_specs=(pl.BlockSpec(memory_space=vmem),) * 4,
        scratch_shapes=[
            vmem((block, din), BF16),
            vmem((din, hid), BF16),
            vmem((hid, width), BF16),
            vmem((n_q, width), BF16),
            vmem((ni, meta_rows, 128), jnp.int32),
            vmem((nq, meta_rows, 128), jnp.int32),
            vmem((ni * block, width), BF16),
            vmem((meta_rows, n_q), F32),
            vmem((ni * block, n_q), F32),
            vmem((ni * block, n_q), BF16),
            vmem((nq, 8, n_q), F32),
            vmem((ni * block, width), F32),
            vmem((gx * block, width), F32),
            vmem((max(gx - 1, 1) * block, width), F32),
            vmem((n_q, width), F32),
            vmem((gz * q_rows, width), F32),
            vmem((gz // 2 * q_rows, width), F32),
            vmem((max(gz // 2 - 1, 1) * q_rows, width), F32),
            vmem((block, hid), F32),
            vmem((block, hid), BF16),
            vmem((a_rows, 128), F32),
            vmem((b_rows, 128), F32),
            vmem((3, part // 2, 128), F32),
            vmem((3, part // 2, 128), F32),
            vmem((3, part // 4, 128), F32),
            vmem((3, part // 4, 128), F32),
            vmem((3, part // 4, 128), F32),
            pltpu.SemaphoreType.DMA((n_copies,)),
            pltpu.SemaphoreType.DMA((n_copies,)),
            pltpu.SemaphoreType.DMA((3,)),
        ],
        compiler_params=pltpu.CompilerParams(
            collective_id=0, has_side_effects=True, vmem_limit_bytes=58 * 2**20
        ),
        name="loss_window",
    )(query_emb, targets.reshape(1, -1), eligible_tiles, tokens, w_first, w_second)
    loss = loss.reshape(q_rows)
    g1 = g1.reshape(hid // 128, din, 128).transpose(1, 0, 2).reshape(din, hid).astype(F32)
    g2 = g2.reshape(width // 128, hid, 128).transpose(1, 0, 2).reshape(hid, width).astype(F32)
    return (loss, query_grad, g1, g2)

def small_kernel(
    grad_scale,
    query_hbm, targets_hbm, flags_hbm, tokens_hbm, w1_hbm, w2_hbm,
    loss_out, qgrad_out, a_out, b_out,
    targets_ref, flags_ref, loss_ref, qgrad_ref, tokens_all, w1_ref, w2_ref, q_all, raw_in, meta_in, emb_all, flags_all, scores, coeffs, stats_all,
    tops, e_acc, e_recv_c, e_send, e_recv_x, grad_all, q_acc, q_send, q_recv,
    hidden, slope, hid_cols, a_acc, b_acc, a_send, b_send, a_recv, b_recv_y, b_half, b_part, b_recv, a_all, b_all,
    send_sems, recv_sems, load_sems,
):
    nq, ni, gx, gy, gz = 8, 4, 2, 2, 4
    q, i = lax.axis_index("query"), lax.axis_index("item")
    core, x = lax.rem(i, 2), lax.div(i, 2)
    y, z = lax.rem(q, 2), lax.div(q, 2)
    q_rows, width = query_hbm.shape
    n_q = nq * q_rows
    block = tokens_hbm.shape[0]
    hid = w2_ref.shape[0]
    cols = hid // ni
    i_pos = core * gx + x
    used = [0]
    started = []

    def send(src, dst, peer):
        slot = used[0]
        used[0] += 1
        copy = pltpu.make_async_remote_copy(
            src_ref=src, dst_ref=dst, send_sem=send_sems.at[slot], recv_sem=recv_sems.at[slot],
            device_id=peer, device_id_type=pl.DeviceIdType.MESH,
        )
        copy.start()
        started.append(copy)
        return copy

    def arrived(copies):
        for copy in copies:
            copy.wait_recv()

    def ring(k):
        return {"query": lax.rem(q + k, nq)}

    def device(c_, x_, y_, z_):
        return {"query": z_ * 2 + y_, "item": x_ * 2 + c_}

    on_core = device(1 - core, x, y, z)
    on_x = device(core, 1 - x, y, z)
    on_cx = device(1 - core, 1 - x, y, z)
    on_y = device(core, x, 1 - y, z)
    on_xy = device(core, 1 - x, 1 - y, z)

    barrier = pltpu.get_barrier_semaphore()
    greeted = [ring(k) for k in range(1, nq)] + [on_core, on_x, on_cx, on_xy]
    for peer in greeted:
        pl.semaphore_signal(barrier, inc=1, device_id=peer, device_id_type=pl.DeviceIdType.MESH)

    loads = [
        pltpu.make_async_copy(src, dst, load_sems.at[n])
        for n, (src, dst) in enumerate((
            (query_hbm, q_all.at[rows(q * q_rows, q_rows)]), (targets_hbm, targets_ref), (flags_hbm, flags_ref),
            (tokens_hbm, tokens_all.at[rows(i_pos * block, block)]), (w1_hbm, w1_ref), (w2_hbm, w2_ref),
        ))
    ]
    for load in loads:
        load.start()

    for load in loads[:3]:
        load.wait()
    per = 128 // q_rows
    meta_rows = raw_in.shape[1]
    raw_in[i] = jnp.zeros((meta_rows, 128), jnp.int32)
    raw_in[i, 0:ni, 0:nq] = (flags_ref[...] > 0).astype(jnp.int32)
    lane_row = lax.broadcasted_iota(jnp.int32, (1, 128), 1)
    first_lane = pl.multiple_of(lax.div(i, per) * 128, 128)
    found = targets_ref[:, pl.ds(first_lane, 128)]
    shift = lax.rem(q - i + per * nq * ni, per)
    moved = found
    for h in range(1, per):
        moved = jnp.where(shift == h, pltpu.roll(found, h * q_rows, 1), moved)
    inside = lax.div(lane_row, q_rows) == lax.rem(q, per)
    own_targets = jnp.where(inside, moved, 0)

    pl.semaphore_wait(barrier, len(greeted))

    raw_copies = [send(raw_in.at[i], raw_in.at[i], peer) for peer in (on_x, on_cx, on_core)]
    emb_own = emb_all.at[rows(i_pos * block, block)]
    own_queries = q_all.at[rows(q * q_rows, q_rows)]
    query_copies = [send(own_queries, own_queries, ring(k)) for k in (4, 3, 5, 2, 6, 1, 7)]
    loads[3].wait()
    loads[4].wait()
    pre = dot(tokens_all[rows(i_pos * block, block), :], w1_ref[...], (1, 0))
    hidden[...] = jax.nn.silu(pre).astype(BF16)
    loads[5].wait()
    emb_all[rows(i_pos * block, block), :] = dot(hidden[...], w2_ref[...], (1, 0)).astype(BF16)
    emb_x = send(emb_own, emb_own, on_x)
    emb_c = send(emb_own, emb_own, on_core)
    arrived(raw_copies)
    packed = jnp.zeros((1, 128), jnp.int32)
    for t in range(ni):
        row = raw_in[t, pl.ds(i, 1), :]
        row = jnp.where(lane_row < nq, row, 0)
        low = pltpu.roll(row, t * nq, 1) if t else row
        packed = packed + jnp.where(lax.rem(q, 2) == 1, low, pltpu.roll(row, q_rows + t * nq, 1))
    meta_in[q] = packed + own_targets
    meta_copies = [send(meta_in.at[q], meta_in.at[q], ring(k)) for k in (4, 3, 5, 2, 6, 1, 7)]
    emb_x.wait_recv()
    emb_far = emb_all.at[rows((core * gx + 1 - x) * block, block)]
    emb_f = send(emb_far, emb_far, on_core)
    tok_own = tokens_all.at[rows(i_pos * block, block)]
    tok_x = send(tok_own, tok_own, on_x)
    tok_c = send(tok_own, tok_own, on_core)

    arrived(meta_copies)
    lane = lax.broadcasted_iota(jnp.int32, (meta_rows, 128), 1)
    sub = lax.broadcasted_iota(jnp.int32, (meta_rows, 128), 0)
    want_tiles, flag_tiles = [], []
    for t in range(nq // per):
        even, odd = meta_in[t * per], meta_in[t * per + 1]
        want_tiles.append(jnp.where(lane_row < q_rows, even, odd))
        flag = jnp.zeros((meta_rows, 128), F32)
        for h, sent in ((0, even), (1, odd)):
            at = sub * nq + q + (q_rows if h == 0 else 0)
            ours = (lane == at) & (sub < ni)
            column = jnp.sum(jnp.where(ours, sent, 0).astype(F32), axis=1, keepdims=True)
            inside = (lane >= h * q_rows) & (lane < (h + 1) * q_rows)
            flag = flag + jnp.where(inside, column, 0.0)
        flag_tiles.append(flag)
    wanted = jnp.concatenate(want_tiles, axis=1)
    flags_all[...] = jnp.concatenate(flag_tiles, axis=1)

    def located(p):
        item = lax.rem(p, gx) * 2 + lax.div(p, gx)
        first = (item * nq + q) * block
        ids = lax.broadcasted_iota(jnp.int32, (block, n_q), 0)
        hit = ids == (wanted - first)
        live = flags_all[pl.ds(item, 1), :] > 0.5
        return hit, live

    def score_block(p, carried):
        top, total, positive = carried
        hit, live = located(p)
        s = 0.25 * dot(emb_all[rows(p * block, block), :], q_all[...], (1, 1))
        here = jnp.max(s, axis=0, keepdims=True)
        e = jnp.exp(s - here)
        scores[rows(p * block, block), :] = e
        added = jnp.sum(e, axis=0, keepdims=True)
        positive = positive + jnp.sum(jnp.where(hit, s, 0.0), axis=0, keepdims=True)
        here = jnp.where(live, here, -1e30)
        tops[pl.ds(p, 1), :] = here
        new_top = jnp.maximum(top, here)
        total = total * jnp.exp(top - new_top) + jnp.where(live, added * jnp.exp(here - new_top), 0.0)
        return new_top, total, positive

    arrived(query_copies)
    carried = (jnp.full((1, n_q), -1e30, F32), jnp.zeros((1, n_q), F32), jnp.zeros((1, n_q), F32))
    carried = score_block(i_pos, carried)
    carried = score_block(core * gx + 1 - x, carried)
    emb_c.wait_recv()
    carried = score_block((1 - core) * gx + x, carried)
    emb_f.wait_recv()
    carried = score_block((1 - core) * gx + 1 - x, carried)
    top, total, positive = carried
    part_norm = jnp.where(total > 0.0, top + jnp.log(jnp.maximum(total, 1e-30)), -1e30)
    tiles = n_q // 128

    def stacked(row):
        return [row[:, t * 128 : (t + 1) * 128] for t in range(tiles)]

    stats_all[0] = jnp.concatenate(stacked(part_norm) + stacked(positive), axis=0)
    stats_copies = [send(stats_all.at[0], stats_all.at[k], ring(k)) for k in (4, 3, 5, 2, 6, 1, 7)]
    my_cols = pl.ds(pl.multiple_of(i * cols, 128), cols)

    def forward_cols(p):
        part = rows(p * block, block)
        pre = dot(tokens_all[part, :], w1_ref[:, my_cols], (1, 0))
        sig = jax.nn.sigmoid(pre)
        hid_cols[part, :] = (pre * sig).astype(BF16)
        slope[part, :] = sig * (1.0 + pre * (1.0 - sig))

    w2_cols = w2_ref[rows(i * cols, cols), :]
    forward_cols(i_pos)
    tok_c.wait_recv()
    forward_cols((1 - core) * gx + x)
    arrived(stats_copies)
    top = stats_all[0, 0:tiles, :]
    positive = stats_all[0, tiles:, :]
    for k in range(1, nq):
        top = jnp.maximum(top, stats_all[k, 0:tiles, :])
        positive = positive + stats_all[k, tiles:, :]
    total = jnp.zeros((tiles, 128), F32)
    for k in range(nq):
        total = total + jnp.exp(stats_all[k, 0:tiles, :] - top)
    norm_tiles = top + jnp.log(total)
    log_norm = jnp.concatenate([norm_tiles[t : t + 1, :] for t in range(tiles)], axis=1)
    def grad_block(p):
        hit, _ = located(p)
        factor = jnp.exp(tops[pl.ds(p, 1), :] - log_norm)
        c = (scores[rows(p * block, block), :] * factor - hit.astype(F32)).astype(BF16)
        coeffs[rows(p * block, block), :] = c
        e_acc[rows(p * block, block), :] = 0.25 * dot(c, q_all[...], (1, 0))

    crossing = []
    for t in range(gx):
        p = (1 - core) * gx + t
        slot = rows(t * block, block)
        grad_block(p)
        pair = send(e_acc.at[rows(p * block, block)], e_recv_c.at[slot], on_core)
        grad_block(core * gx + t)
        here = rows((core * gx + t) * block, block)
        pair.wait_recv()
        part = e_acc[here, :] + e_recv_c[slot, :]
        e_acc[here, :] = part
        e_send[slot, :] = part.astype(BF16)
        crossing.append(send(e_send.at[slot], e_recv_x.at[slot], on_x))
    q_acc[...] = 0.25 * dot(coeffs[...], emb_all[...], (0, 0))
    q_send[...] = q_acc[...].astype(BF16)
    q_copies = [
        send(
            q_send.at[rows(lax.rem(q + k, nq) * q_rows, q_rows)],
            q_recv.at[rows((k - 1) * q_rows, q_rows)], ring(k),
        )
        for k in (4, 3, 5, 2, 6, 1, 7)
    ]
    tok_x.wait_recv()
    tok_far = tokens_all.at[rows((core * gx + 1 - x) * block, block)]
    tok_f = send(tok_far, tok_far, on_core)
    forward_cols(core * gx + 1 - x)
    losses = norm_tiles - positive
    found = jnp.zeros((1, 128), F32)
    for t in range(tiles):
        found = found + jnp.where(lax.div(q, per) == t, losses[t : t + 1, :], 0.0)
    moved = found
    for h in range(1, per):
        moved = jnp.where(lax.rem(q, per) == h, pltpu.roll(found, (per - h) * q_rows, 1), moved)
    loss_ref[...] = moved[:, :q_rows]

    tok_f.wait_recv()
    forward_cols((1 - core) * gx + 1 - x)

    def tower_b(p, first):
        part = rows(p * block, block)
        b = dot(hid_cols[part, :], grad_all[part, :], (0, 0))
        b = b.reshape(b_acc.shape)
        b_acc[...] = b if first else b_acc[...] + b

    def tower_a(p, first):
        part = rows(p * block, block)
        pre_grad = (dot(grad_all[part, :], w2_cols, (1, 1)) * slope[part, :]).astype(BF16)
        a = dot(tokens_all[part, :], pre_grad, (0, 0))
        a_acc[...] = a if first else a_acc[...] + a

    for t in range(gx):
        mine, theirs = core * gx + t, (1 - core) * gx + t
        here = rows(mine * block, block)
        crossing[t].wait_recv()
        grad_all[here, :] = (e_acc[here, :] + e_recv_x[rows(t * block, block), :].astype(F32)).astype(BF16)
        over = send(grad_all.at[here], grad_all.at[here], on_core)
        tower_b(mine, t == 0)
        tower_a(mine, t == 0)
        over.wait_recv()
        tower_b(theirs, False)
        if t == gx - 1:
            b_send[...] = b_acc[...].astype(BF16)
            b_y = send(b_send.at[:, 1 - y], b_recv_y, on_y)
        tower_a(theirs, False)
    a_rows = a_acc.shape[0] // nq
    a_send[...] = a_acc[...].astype(BF16)
    a_copies = [
        send(
            a_send.at[rows(lax.rem(q + k, nq) * a_rows, a_rows)],
            a_recv.at[rows((k - 1) * a_rows, a_rows)], ring(k),
        )
        for k in (4, 3, 5, 2, 6, 1, 7)
    ]

    b_y.wait_recv()
    b_half[...] = b_acc[:, y] + b_recv_y[...].astype(F32)
    b_part[...] = b_half[...].astype(BF16)
    b_copies = [
        send(b_part.at[lax.rem(z + k, gz)], b_recv.at[k - 1], device(core, x, y, lax.rem(z + k, gz)))
        for k in (2, 1, 3)
    ]
    arrived(q_copies)
    total = q_acc[rows(q * q_rows, q_rows), :]
    for k in range(1, nq):
        total = total + q_recv[rows((k - 1) * q_rows, q_rows), :].astype(F32)
    qgrad_ref[...] = total
    outs = [pltpu.make_async_copy(loss_ref, loss_out, load_sems.at[14]), pltpu.make_async_copy(qgrad_ref, qgrad_out, load_sems.at[15])]
    for copy in outs:
        copy.start()
    kept = []

    def leave(out, x_, y_):
        whole = {id(a_all): a_out, id(b_all): b_out}[id(out)].at[x_, core, :, y_]
        copy = pltpu.make_async_copy(out.at[x_, :, y_], whole, load_sems.at[6 + len(kept)])
        copy.start()
        kept.append(copy)
        return send(out.at[x_, :, y_], whole, on_core)

    def gather_own(copies, parts, out, split):
        arrived(copies)
        total = parts()
        out[x, z, y] = (total * grad_scale).astype(BF16)
        own = out.at[x, z, y]
        first = out.at[x, z, y, pl.ds(0, split)]
        over = [[send(own, own, peer) for peer in (on_xy, on_x, on_y)]]
        up = [send(first, first, device(core, x, y, lax.rem(z + k, gz))) for k in (2, 1, 3)]
        return up, over

    def gather_rest(over, out, split):
        size = out.shape[3] - split
        if size == 0:
            return []
        arrived(over.pop(0))
        rest = out.at[:, z, :, pl.ds(split, size)]
        return [send(rest, rest, device(core, x, y, lax.rem(z + k, gz))) for k in (2, 1, 3)]

    def gather_far(up, over, out, split):
        for n, k in enumerate((2, 1, 3)):
            up[n].wait_recv()
            far = out.at[x, lax.rem(z - k + gz, gz), y, pl.ds(0, split)]
            over.append([send(far, far, peer) for peer in (on_xy, on_x, on_y)])

    def gather_core(over, rest, out):
        arrived(rest)
        crossed = [leave(out, x, y)]
        for n, (x_, y_) in ((1, (1 - x, y)), (2, (x, 1 - y)), (0, (1 - x, 1 - y))):
            arrived([four[n] for four in over])
            crossed.append(leave(out, x_, y_))
        return crossed

    def a_total():
        total = a_acc[rows(q * a_rows, a_rows), :]
        for k in range(1, nq):
            total = total + a_recv[rows((k - 1) * a_rows, a_rows), :].astype(F32)
        return total

    def b_total():
        total = b_half[z]
        for k in range(1, gz):
            total = total + b_recv[k - 1].astype(F32)
        return total

    a_split, b_split = a_rows * 3 // 4, b_all.shape[3]
    a_up, a_over = gather_own(a_copies, a_total, a_all, a_split)
    b_up, b_over = gather_own(b_copies, b_total, b_all, b_split)
    b_rest = gather_rest(b_over, b_all, b_split)
    a_rest = gather_rest(a_over, a_all, a_split)
    gather_far(a_up, a_over, a_all, a_split)
    gather_far(b_up, b_over, b_all, b_split)
    crossed = gather_core(a_over, a_rest, a_all)
    crossed += gather_core(b_over, b_rest, b_all)
    arrived(crossed)
    for copy in kept + outs:
        copy.wait()
    for copy in started:
        copy.wait_send()


def finish_kernel(loss_in, qgrad_in, a_in, b_in, loss_ref, qgrad_ref, a_ref, b_ref):
    loss_ref[...] = loss_in[...]
    qgrad_ref[...] = qgrad_in[...]
    for t in range(a_in.shape[0]):
        for r in range(a_in.shape[1]):
            size, cols = a_in.shape[2], a_in.shape[3]
            a_ref[r * size : (r + 1) * size, t * cols : (t + 1) * cols] = a_in[t, r].astype(F32)
    b_ref[...] = b_in[...].astype(F32)


def on_device_small(query_emb, targets, eligible_tiles, item_feats, w_first, w_second):
    q_rows, width = query_emb.shape
    ni, nq = lax.axis_size("item"), lax.axis_size("query")
    tokens = item_feats.reshape(item_feats.shape[1], item_feats.shape[2])
    block, din = tokens.shape
    hid = w_first.shape[1]
    n_q, items, cols = nq * q_rows, ni * block, hid // ni
    a_rows, b_rows = din // nq, cols // nq
    vmem = pltpu.VMEM
    out = (2, 2, nq // 2, 2)
    loss, query_grad, g1, g2 = pl.pallas_call(
        functools.partial(small_kernel, 1.0 / math.sqrt(items * nq)),
        out_shape=(
            jax.ShapeDtypeStruct((1, q_rows), F32),
            jax.ShapeDtypeStruct((q_rows, width), F32),
            jax.ShapeDtypeStruct(out + (a_rows, cols), BF16),
            jax.ShapeDtypeStruct(out + (b_rows, width), BF16),
        ),
        in_specs=[pl.BlockSpec(memory_space=pl.ANY)] * 6,
        out_specs=(pl.BlockSpec(memory_space=pl.ANY),) * 4,
        scratch_shapes=[
            vmem((1, targets.shape[0]), jnp.int32),
            vmem(eligible_tiles.shape, jnp.int32),
            vmem((1, q_rows), F32),
            vmem((q_rows, width), F32),
            vmem((items, din), BF16),
            vmem((din, hid), BF16),
            vmem((hid, width), BF16),
            vmem((n_q, width), BF16),
            vmem((ni, 8, 128), jnp.int32),
            vmem((nq, 1, 128), jnp.int32),
            vmem((items, width), BF16),
            vmem((8, n_q), F32),
            vmem((items, n_q), F32),
            vmem((items, n_q), BF16),
            vmem((nq, 2 * n_q // 128, 128), F32),
            vmem((8, n_q), F32),
            vmem((items, width), F32),
            vmem((2 * block, width), F32),
            vmem((2 * block, width), BF16),
            vmem((2 * block, width), BF16),
            vmem((items, width), BF16),
            vmem((n_q, width), F32),
            vmem((n_q, width), BF16),
            vmem(((nq - 1) * q_rows, width), BF16),
            vmem((block, hid), BF16),
            vmem((items, cols), F32),
            vmem((items, cols), BF16),
            vmem((din, cols), F32),
            vmem((nq // 2, 2, b_rows, width), F32),
            vmem((din, cols), BF16),
            vmem((nq // 2, 2, b_rows, width), BF16),
            vmem(((nq - 1) * a_rows, cols), BF16),
            vmem((nq // 2, b_rows, width), BF16),
            vmem((nq // 2, b_rows, width), F32),
            vmem((nq // 2, b_rows, width), BF16),
            vmem((nq // 2 - 1, b_rows, width), BF16),
            vmem((2, nq // 2, 2, a_rows, cols), BF16),
            vmem((2, nq // 2, 2, b_rows, width), BF16),
            pltpu.SemaphoreType.DMA((112,)),
            pltpu.SemaphoreType.DMA((112,)),
            pltpu.SemaphoreType.DMA((16,)),
        ],
        compiler_params=pltpu.CompilerParams(
            collective_id=0, has_side_effects=True, vmem_limit_bytes=58 * 2**20
        ),
        name="loss_window",
    )(query_emb, targets.reshape(1, -1), eligible_tiles, tokens, w_first, w_second)
    steps = 2
    loss, query_grad, g1, g2 = pl.pallas_call(
        finish_kernel,
        grid=(steps,),
        out_shape=(
            jax.ShapeDtypeStruct((1, q_rows), F32),
            jax.ShapeDtypeStruct((q_rows, width), F32),
            jax.ShapeDtypeStruct((din, hid), F32),
            jax.ShapeDtypeStruct((ni, nq, b_rows, width), F32),
        ),
        in_specs=[
            pl.BlockSpec((1, q_rows), lambda n: (0, 0)),
            pl.BlockSpec((q_rows // steps, width), lambda n: (n, 0)),
            pl.BlockSpec((ni, nq // steps, a_rows, cols), lambda n: (0, n, 0, 0)),
            pl.BlockSpec((ni, nq // steps, b_rows, width), lambda n: (0, n, 0, 0)),
        ],
        out_specs=(
            pl.BlockSpec((1, q_rows), lambda n: (0, 0)),
            pl.BlockSpec((q_rows // steps, width), lambda n: (n, 0)),
            pl.BlockSpec((din // steps, hid), lambda n: (n, 0)),
            pl.BlockSpec((ni, nq // steps, b_rows, width), lambda n: (0, n, 0, 0)),
        ),
        name="widen",
    )(loss, query_grad, g1.reshape(ni, nq, a_rows, cols), g2.reshape(ni, nq, b_rows, width))
    return loss.reshape(q_rows), query_grad, g1, g2.reshape(hid, width)


def solution(mesh):
    small = mesh.shape["query"] == 8 and mesh.shape["item"] == 4
    return jax.shard_map(
        on_device_small if small else on_device,
        mesh=mesh,
        in_specs=(
            P(("query", "item"), None),
            P("query"),
            P("query", "item"),
            P("item", "query", None),
            P(),
            P(),
        ),
        out_specs=(P(("query", "item")), P(("query", "item"), None), P(), P()),
        check_vma=False,
    )
```
